256 devices in a mesh: seq: 32 (over x, y, core), exp: 8 (over z).
Axes of the slice: x: 4, y: 4, z: 8, core: 2. Of those that a mesh axis runs over, the one named last changes fastest.
Arguments:
- tokens: bfloat16 [96, 4, 1024], P('exp'), may hold values from -48 to 48
- attn_gain: float32 [1024], replicated, may hold values from 0.1 to 1.9
- w_qkv: bfloat16 [3072, 1024], P('seq'), may hold values from -0.1875 to 0.1875
- window_cache: bfloat16 [2, 96, 4096, 1024], P(None, 'exp', 'seq'), may hold values from -180 to 180
- sink_cache: bfloat16 [2, 96, 4, 1024], P(None, 'exp'), may hold values from -6 to 6
- lengths: int32 [96], P('exp'), may hold values from 8 to 16384, as said below
- w_out: bfloat16 [1024, 1024], P('seq'), may hold values from -0.1875 to 0.1875
- moe_gain: float32 [1024], replicated, may hold values from 0.1 to 1.9
- router: bfloat16 [1024, 16], replicated, may hold values from -0.1875 to 0.1875
- expert_ids: int32 [96, 4, 2], P('exp'), may hold values from 0 to 15, all different within a row
- slot_order: int32 [8, 48], P('exp'), may hold values from 0 to 47, each once within a row
- expert_in: bfloat16 [2, 8, 5632, 1024], P(None, 'exp', 'seq'), may hold values from -0.1875 to 0.1875
- expert_down: bfloat16 [8, 5632, 1024], P('exp', 'seq'), may hold values from -0.109375 to 0.109375
Outputs:
- output: bfloat16 [96, 4, 1024], P('exp')
The draws below stay inside these ranges and needn't reach their ends.
Inputs may be any that keep to these rules, and one draw needn't show every extreme that they name: `lengths`: at least one request holds 16384 tokens. `expert_ids`: the 2 experts of a token differ, and every expert is named by some token. `slot_order`: each group's row holds every number of 0 to 47 once.
All inputs are finite; a program needn't handle non-finite values.
Results may differ from the reference program's by a relative error of at most 0.0083.
The reference program's roundings to bfloat16 on the way count: a program that leaves them out, or rounds other values in their place, can miss the bound.
Values may be sent and summed in bfloat16 or wider, within the bound.
A program may use at most 64 MiB of HBM per device.

```python
import math
import jax
import jax.numpy as jnp
from jax import lax

D = 1024
FF = 2816
HEADS = 16
HD = 64
EXPERTS = 16
TOPK = 2
SINKS = 4
WIN = 4096
STEPS = 4
MAXLEN = 16384
GROUPS = 8
REQS = 96
ROWS_GRP = 48
CAP = 8
EXP_GRP = 2
N_EXP = 8


def draw_tokens(key, part):
    key_noise, key_rows, key_cols = jax.random.split(key, 3)
    row_scale = jnp.exp(jax.random.uniform(key_rows, (REQS, STEPS, 1), jnp.float32, math.log(0.5), math.log(5.0)))
    column_scale = jnp.exp(jax.random.uniform(key_cols, (D,), jnp.float32, math.log(0.3), math.log(3.0)))
    base_part = jnp.clip(jax.random.normal(key_noise, (REQS, STEPS, D), jnp.float32), -3.0, 3.0)
    return (base_part * row_scale * column_scale).astype(jnp.bfloat16)


def draw_window_cache(key, part):
    key_keys, key_values = jax.random.split(key)
    key_table = 2.0 * jnp.clip(jax.random.normal(key_keys, (REQS, WIN, D), jnp.float32), -4.0, 4.0)
    value_table = jnp.clip(jax.random.normal(key_values, (REQS, WIN, D), jnp.float32), -4.0, 4.0)
    return jnp.stack([key_table, value_table]).astype(jnp.bfloat16)


def draw_lengths(key, part):
    key_power, key_extra, key_long, key_short = jax.random.split(key, 4)
    top_power = MAXLEN.bit_length() - 1
    doubling = jax.random.randint(key_power, (REQS,), 3, top_power + 1)
    floor_len = jnp.left_shift(jnp.ones((REQS,), jnp.int32), doubling)
    added_len = jax.random.randint(key_extra, (REQS,), 0, floor_len)
    length = jnp.minimum(floor_len + added_len, MAXLEN)
    longest = jax.random.randint(key_long, (), 0, REQS)
    offset = jax.random.randint(key_short, (), 1, REQS)
    length = length.at[longest].set(MAXLEN)
    length = length.at[(longest + offset) % REQS].set(8)
    return length.astype(jnp.int32)


def block_levels(key, extent, shards, smallest, high):
    gain = 1.0
    for axis_at, parts in shards:
        draws = jax.random.uniform(jax.random.fold_in(jax.random.fold_in(key, 6), axis_at), (parts,), jnp.float32, smallest / len(shards), high / len(shards))
        gain = gain * jnp.repeat(jnp.exp(draws), extent[axis_at] // parts).reshape((-1,) + (1,) * (len(extent) - 1 - axis_at))
    return gain


def distinct(own_key, rows, amount, top, lift):
    sequence = jax.random.permutation(jax.random.fold_in(own_key, 1), amount)
    favour = sequence
    for power in range(3):
        favour = favour * favour // amount
    favour = favour * lift // amount
    tickets = jax.random.randint(jax.random.fold_in(own_key, 2), (rows, amount), 0, 4096) + favour
    fixed_rows = jax.random.permutation(jax.random.fold_in(own_key, 3), rows)[jnp.arange(amount) % rows]
    tickets = jnp.where(jnp.arange(rows)[:, None] == fixed_rows[None, :], 1 << 14, tickets)
    merit = tickets * amount + jnp.arange(amount)
    return lax.top_k(merit.astype(jnp.int32), top)[1].astype(jnp.int32)


def normal_values(rng, extent, width, limit, shards=(), held_as=jnp.bfloat16):
    gain = block_levels(rng, extent, shards, -0.22, 0.18) if shards else 1.0
    array = jax.random.normal(rng, extent, jnp.float32) * width * gain
    return jnp.minimum(jnp.maximum(array, -limit), limit).astype(held_as)


def setup_inputs(seed: int = 0) -> dict:
    key_list = jax.random.split(jax.random.key(seed), 14)
    tokens = draw_tokens(jax.random.fold_in(key_list[13], 71), 0)
    attn_gain = jnp.clip(1.0 + 0.18 * jax.random.normal(key_list[1], (D,), jnp.float32), 0.1, 1.9)
    w_qkv = normal_values(key_list[2], (3 * D, D), D ** -0.5, 0.1875, ((0, 32),))
    window_cache = draw_window_cache(jax.random.fold_in(key_list[13], 71), 0)
    sink_cache = normal_values(key_list[4], (2, REQS, SINKS, D), 1.5, 6.0, ((1, 8),))
    lengths = draw_lengths(jax.random.fold_in(key_list[13], 71), 0)
    w_out = normal_values(key_list[6], (D, D), D ** -0.5, 0.1875, ((0, 32),))
    moe_gain = jnp.clip(1.0 + 0.18 * jax.random.normal(key_list[7], (D,), jnp.float32), 0.1, 1.9)
    router = normal_values(key_list[8], (D, EXPERTS), D ** -0.5, 0.1875)
    expert_ids = distinct(key_list[9], REQS * STEPS, EXPERTS, TOPK, 2048).reshape((REQS, STEPS, TOPK))
    slot_order = jax.vmap(lambda own: jax.random.permutation(own, ROWS_GRP))(jax.random.split(key_list[10], GROUPS)).reshape((GROUPS, ROWS_GRP)).astype(jnp.int32)
    expert_in = normal_values(key_list[11], (2, N_EXP, EXP_GRP * FF, D), D ** -0.5, 0.1875, ((1, 8), (2, 32)))
    expert_down = normal_values(key_list[12], (N_EXP, EXP_GRP * FF, D), FF ** -0.5, 0.109375, ((0, 8), (1, 32)))
    return dict(tokens=tokens, attn_gain=attn_gain, w_qkv=w_qkv, window_cache=window_cache, sink_cache=sink_cache, lengths=lengths, w_out=w_out, moe_gain=moe_gain, router=router, expert_ids=expert_ids, slot_order=slot_order, expert_in=expert_in, expert_down=expert_down)


EPSILON = 1e-06
MASKED = -1e+30

def rms_scale(values, gain_row):
    widened = values.astype(jnp.float32)
    inverse = lax.rsqrt(lax.optimization_barrier(jnp.mean(widened * widened, axis=-1, keepdims=True)) + EPSILON)
    return (widened * inverse * gain_row).astype(jnp.bfloat16)

def attend_request(inputs):
    queries, new_keys, new_values, window_keys, window_values, sink_keys, sink_values, length = inputs
    step_ids = jnp.arange(STEPS, dtype=jnp.int32)
    slot_ids = jnp.arange(WIN, dtype=jnp.int32)
    written = (length + step_ids - SINKS) % WIN
    overwritten = jnp.cumsum((slot_ids[None, :] == written[:, None]).astype(jnp.int32), axis=0) > 0
    window_live = (slot_ids[None, :] < jnp.minimum(WIN, length - SINKS)) & jnp.logical_not(overwritten)
    causal = step_ids[None, :] <= step_ids[:, None]
    live_keys = jnp.concatenate([window_live, jnp.ones((STEPS, SINKS), jnp.bool_), causal], axis=1)[:, None, :]
    all_keys = jnp.concatenate([window_keys.reshape(WIN, HEADS, HD), sink_keys.reshape(SINKS, HEADS, HD), new_keys], axis=0).astype(jnp.float32)
    all_values = jnp.concatenate([window_values.reshape(WIN, HEADS, HD), sink_values.reshape(SINKS, HEADS, HD), new_values], axis=0).astype(jnp.float32)
    scores = jnp.einsum('she,khe->shk', queries.astype(jnp.float32), all_keys) * HD ** (-0.5)
    peak_score = lax.optimization_barrier(jnp.max(jnp.where(live_keys, scores, MASKED), axis=-1, keepdims=True))
    exponent = jnp.where(live_keys, jnp.exp(scores - peak_score), 0.0)
    weight_sum = lax.optimization_barrier(jnp.sum(exponent, axis=-1, keepdims=True))
    rounded = lax.optimization_barrier(exponent.astype(jnp.bfloat16)).astype(jnp.float32)
    weighted = jnp.einsum('shk,khe->she', rounded, all_values) / weight_sum
    return weighted.reshape(STEPS, D).astype(jnp.bfloat16)

def route_group(chosen, priority, features, logits):
    onehot = (chosen[:, :, None] == jnp.arange(EXPERTS, dtype=jnp.int32)).astype(jnp.float32)
    gate_values = jax.nn.sigmoid(lax.optimization_barrier(jnp.sum(onehot * logits[:, None, :], axis=-1)))
    earlier = (priority[None, :] < priority[:, None]).astype(jnp.float32)
    counts = jnp.dot(earlier, lax.optimization_barrier(jnp.sum(onehot, axis=1)), precision=lax.Precision.HIGHEST)
    position = lax.optimization_barrier(jnp.sum(onehot * counts[:, None, :], axis=-1)).astype(jnp.int32)
    column = chosen * CAP + position
    select = ((column[:, :, None] == jnp.arange(EXPERTS * CAP, dtype=jnp.int32)) & (position < CAP)[:, :, None]).astype(jnp.float32)
    dispatch = lax.optimization_barrier(jnp.sum(select, axis=1)).astype(jnp.bfloat16)
    buffer = jnp.dot(dispatch.T, features, preferred_element_type=jnp.float32).astype(jnp.bfloat16)
    return (buffer, select, gate_values)

def run_expert(inputs):
    rows_in, weights_in, weights_down = inputs
    gate_up = jnp.einsum('nd,pfd->pnf', rows_in.astype(jnp.float32), weights_in.astype(jnp.float32))
    hidden = (jax.nn.gelu(gate_up[0], approximate=True) * gate_up[1]).astype(jnp.bfloat16)
    return jnp.dot(hidden, weights_down, preferred_element_type=jnp.float32).astype(jnp.bfloat16)

def reference(tokens, attn_gain, w_qkv, window_cache, sink_cache, lengths, w_out, moe_gain, router, expert_ids, slot_order, expert_in, expert_down):
    flat_rows = tokens.reshape(REQS * STEPS, D)
    normed_attn = rms_scale(flat_rows, attn_gain)
    mixed_rows = jnp.dot(normed_attn, w_qkv.T, preferred_element_type=jnp.float32).astype(jnp.bfloat16)
    mixed_rows = lax.optimization_barrier(mixed_rows).reshape(REQS, STEPS, 3, HEADS, HD)
    attended = lax.map(attend_request, (mixed_rows[:, :, 0], mixed_rows[:, :, 1], mixed_rows[:, :, 2], window_cache[0], window_cache[1], sink_cache[0], sink_cache[1], lengths))
    projected = jnp.dot(attended.reshape(REQS * STEPS, D), w_out.T, preferred_element_type=jnp.float32).astype(jnp.bfloat16)
    residual = flat_rows.astype(jnp.float32) + lax.optimization_barrier(projected).astype(jnp.float32)
    normed_moe = rms_scale(residual, moe_gain)
    logits = jnp.dot(normed_moe, router, preferred_element_type=jnp.float32)
    buffers, selects, gate_values = jax.vmap(route_group)(expert_ids.reshape(GROUPS, ROWS_GRP, TOPK), slot_order, normed_moe.reshape(GROUPS, ROWS_GRP, D), logits.reshape(GROUPS, ROWS_GRP, EXPERTS))
    by_expert = buffers.reshape(GROUPS, EXPERTS, CAP, D).transpose(1, 0, 2, 3).reshape(EXPERTS, GROUPS * CAP, D)
    weights_in = expert_in.reshape(2, EXPERTS, FF, D).transpose(1, 0, 2, 3)
    weights_down = expert_down.reshape(EXPERTS, FF, D)
    outputs = lax.map(run_expert, (by_expert, weights_in, weights_down))
    outputs = lax.optimization_barrier(outputs)
    by_group = outputs.reshape(EXPERTS, GROUPS, CAP, D).transpose(1, 0, 2, 3).reshape(GROUPS, EXPERTS * CAP, D)
    picked = jnp.einsum('grkc,gcd->grkd', selects, by_group.astype(jnp.float32))
    moe_rows = lax.optimization_barrier(jnp.sum(gate_values[..., None] * picked, axis=2))
    final_rows = (residual.reshape(GROUPS, ROWS_GRP, D) + moe_rows).astype(jnp.bfloat16)
    return final_rows.reshape(REQS, STEPS, D)
```

```python
import functools

import jax
import jax.numpy as jnp
from jax import lax
from jax.experimental import pallas as pl
from jax.experimental.pallas import tpu as pltpu
from jax.sharding import PartitionSpec as P

HEADS = 16
HD = 64
EXPERTS = 16
SINKS = 4
WIN = 4096
CAP = 8
STEPS = 4
EPSILON = 1e-06
MASKED = -1e30
MESH = pl.DeviceIdType.MESH
F32 = jnp.float32
BF16 = jnp.bfloat16
LAST = (((1,), (1,)), ((), ()))


def iota(shape, axis):
    return lax.broadcasted_iota(jnp.int32, shape, axis)


def wait_bytes(ref, sem):
    pltpu.make_async_copy(ref, ref, sem).wait()


def layer_kernel(
    seq_count,
    group_count,
    tokens_ref,
    attn_gain_ref,
    w_qkv_ref,
    cache_hbm,
    sink_ref,
    lengths_ref,
    w_out_ref,
    moe_gain_ref,
    router_ref,
    ids_ref,
    order_ref,
    in_hbm,
    down_hbm,
    out_ref,
    kv,
    win,
    down,
    x_tok,
    idcol,
    mix,
    qkv_in,
    qkv,
    q4,
    part_out,
    part_in,
    sinks,
    att_in,
    w_rows,
    proj_in,
    disp_out,
    disp_in,
    exp_out,
    exp_in,
    back_out,
    back_in,
    fin_in,
    kv_sem,
    wt_sem,
    loc_sem,
    send_sem,
    recv_sem,
):
    s = lax.axis_index("seq")
    z = lax.axis_index("exp")
    t = s // 4
    rg = lax.rem(s, 4)
    half = s // 16
    owner16 = lax.rem(s, 16)
    gh = owner16 // 8
    owner8 = 8 * half + lax.rem(s, 8)

    barrier = pltpu.get_barrier_semaphore()

    def greet_plane(k, _):
        pl.semaphore_signal(
            barrier, inc=1, device_id=(lax.rem(s + k, seq_count), z), device_id_type=MESH
        )
        return 0

    def greet_line(k, _):
        pl.semaphore_signal(
            barrier, inc=1, device_id=(s, lax.rem(z + k, group_count)), device_id_type=MESH
        )
        return 0

    lax.fori_loop(1, seq_count, greet_plane, 0)
    lax.fori_loop(1, group_count, greet_line, 0)

    for part in range(3):
        for which in range(2):
            pltpu.make_async_copy(
                cache_hbm.at[which, pl.ds(4 * part, 4)],
                kv.at[which, pl.ds(4 * part, 4)],
                kv_sem.at[which, part],
            ).start()
    pltpu.make_async_copy(in_hbm.at[:, 0], win, wt_sem.at[0]).start()
    pltpu.make_async_copy(down_hbm.at[0], down, wt_sem.at[1]).start()

    def rcopy(src, dst, stage, dest_s, dest_z):
        pltpu.make_async_remote_copy(
            src_ref=src,
            dst_ref=dst,
            send_sem=send_sem.at[stage],
            recv_sem=recv_sem.at[stage],
            device_id=(dest_s, dest_z),
            device_id_type=MESH,
        ).start()

    def to_plane(src, dst, stage):
        def send(k, _):
            rcopy(src, dst, stage, lax.rem(s + k, seq_count), z)
            return 0

        lax.fori_loop(1, seq_count, send, 0)

    for r in range(12):
        x_tok[4 * r : 4 * r + 4, :] = tokens_ref[r].astype(F32)
    x = x_tok[...]
    inverse = lax.rsqrt(jnp.mean(x * x, axis=-1, keepdims=True) + EPSILON)
    normed = (x * inverse * attn_gain_ref[...]).astype(BF16)
    own_mix = lax.dot_general(normed, w_qkv_ref[...], LAST, preferred_element_type=F32)
    mix[...] = jnp.concatenate([own_mix, jnp.zeros((48, 32), F32)], axis=1).astype(BF16)

    pl.semaphore_wait(barrier, seq_count - 1 + group_count - 1)
    to_plane(mix, qkv_in.at[s], 0)
    qkv_in[s] = mix[...]
    w_rows[rg] = w_out_ref[...]
    for k in range(1, 4):
        rcopy(w_out_ref, w_rows.at[rg], 1, 4 * t + lax.rem(rg + k, 4), z)

    for r in range(12):
        idcol[4 * r : 4 * r + 4, :] = ids_ref[r]
    eye = iota((48, 48), 0) == iota((48, 48), 1)
    prio_row = order_ref[...]
    prio_col = jnp.sum(jnp.where(eye, prio_row, 0), axis=1, keepdims=True)
    earlier = (prio_row < prio_col).astype(F32).astype(BF16)
    expert_lane = iota((48, EXPERTS), 1)
    ids = idcol[...]
    onehots = []
    for c in range(2):
        onehots.append((expert_lane == ids[:, c : c + 1]).astype(F32))
    counts = jnp.dot(earlier, (onehots[0] + onehots[1]).astype(BF16), preferred_element_type=F32)
    sel_rows = iota((64, 48), 0)
    sel_expert = 2 * (sel_rows // CAP) + half
    sel_slot = sel_rows % CAP
    col_ids = iota((48, 64), 1)
    col_expert = 2 * (col_ids // CAP) + half
    col_slot = col_ids % CAP
    dispatch = jnp.zeros((64, 48), F32)
    picks = []
    for c in range(2):
        pos_col = jnp.sum(onehots[c] * counts, axis=1, keepdims=True).astype(jnp.int32)
        id_col = ids[:, c : c + 1]
        pos_row = jnp.sum(jnp.where(eye, pos_col, 0), axis=0, keepdims=True)
        id_row = jnp.sum(jnp.where(eye, id_col, 0), axis=0, keepdims=True)
        dispatch = dispatch + ((id_row == sel_expert) & (pos_row == sel_slot)).astype(F32)
        picks.append(((id_col == col_expert) & (pos_col == col_slot)).astype(F32))
    dispatch = dispatch.astype(BF16)

    for r in range(12):
        for which in range(2):
            sinks[which, 4 * r : 4 * r + 4, :] = sink_ref[which, r].astype(F32)

    lane48 = iota((48, 128), 1)

    def tiles_of(group):
        b0, b1, b2, b3 = (qkv_in[4 * group + k].astype(F32) for k in range(4))
        r1 = pltpu.roll(b1, 96, 1)
        r2 = pltpu.roll(b2, 64, 1)
        r3 = pltpu.roll(b3, 32, 1)
        return (
            jnp.where(lane48 < 96, b0, r1),
            jnp.where(lane48 < 64, r1, r2),
            jnp.where(lane48 < 32, r2, r3),
        )

    wait_bytes(qkv_in.at[pl.ds(0, seq_count - 1)], recv_sem.at[0])
    tiles = []
    for group in range(3):
        for at, tile in enumerate(tiles_of(group)):
            tiles.append(tile)
            qkv[3 * group + at] = tile
    sub6 = iota((6, 8, 128), 1)
    lane6 = iota((6, 8, 128), 2)
    diag6 = (sub6 < 4) == (lane6 < 64)
    zero6 = jnp.zeros((6, 8, 128), F32)
    for u in range(4):
        tops = []
        for tile in (tiles[2 * u], tiles[2 * u + 1]):
            v = tile.reshape(6, 8, 128)
            w = pltpu.roll(v, 4, 1)
            even = jnp.where(diag6, jnp.where(sub6 < 4, v, w), 0.0)
            odd = jnp.where(diag6, jnp.where(sub6 < 4, w, v), 0.0)
            tops.append((even, odd))
        for parity in range(2):
            upper = jnp.concatenate([tops[0][parity], zero6], axis=2)
            lower = jnp.concatenate([zero6, tops[1][parity]], axis=2)
            q4[:, parity, u] = jnp.concatenate([upper, lower], axis=1).astype(BF16)

    for part in range(3):
        for which in range(2):
            pltpu.make_async_copy(
                cache_hbm.at[which, pl.ds(4 * part, 4)],
                kv.at[which, pl.ds(4 * part, 4)],
                kv_sem.at[which, part],
            ).wait()

    sub8 = iota((8, 8, 128), 1)
    lane8 = iota((8, 8, 128), 2)
    lane_in = lane8 % 64
    step_id = iota((8, 128), 0) % STEPS
    slot_id = s * 128 + iota((8, 128), 1)

    def merge(a, b):
        ar = pltpu.roll(a, 4, 1)
        br = pltpu.roll(b, 4, 1)
        return jnp.where(
            sub8 < 4, jnp.where(lane8 < 64, a, ar), jnp.where(lane8 < 64, br, b)
        )

    def attend(pair, parity):
        r = 2 * pair + parity
        scores = []
        for u in range(4):
            scores.append(
                lax.dot_general(
                    q4[pair, parity, u],
                    kv[0, r, :, 256 * u : 256 * u + 256],
                    LAST,
                    preferred_element_type=F32,
                )
            )
        score = jnp.concatenate(scores, axis=0).reshape(8, 8, 128) * (HD ** (-0.5))
        held = lengths_ref[r] - SINKS
        age = (slot_id - held) & (WIN - 1)
        live = ((slot_id < jnp.minimum(WIN, held)) & (age > step_id))[None]
        peak = jnp.max(jnp.where(live, score, MASKED), axis=-1, keepdims=True)
        weight = jnp.where(live, jnp.exp(score - peak), 0.0)
        total = jnp.sum(weight, axis=-1, keepdims=True)
        rounded = weight.reshape(64, 128).astype(BF16)
        values = []
        for u in range(4):
            mixed = jnp.dot(
                rounded[16 * u : 16 * u + 16],
                kv[1, r, :, 256 * u : 256 * u + 256],
                preferred_element_type=F32,
            )
            values.append(mixed[0:8, 0:128])
            values.append(mixed[8:16, 128:256])
        value = jnp.concatenate(values, axis=0).reshape(8, 8, 128)
        peak = jnp.broadcast_to(peak, (8, 8, 128))
        total = jnp.broadcast_to(total, (8, 8, 128))
        p_hi = peak.astype(BF16).astype(F32)
        p_mid = (peak - p_hi).astype(BF16).astype(F32)
        p_low = peak - p_hi - p_mid
        t_hi = total.astype(BF16).astype(F32)
        t_low = total - t_hi
        stat = jnp.where(
            lane_in == 0,
            p_hi,
            jnp.where(
                lane_in == 1,
                p_mid,
                jnp.where(
                    lane_in == 2,
                    p_low,
                    jnp.where(lane_in == 3, t_hi, jnp.where(lane_in == 4, t_low, 0.0)),
                ),
            ),
        )
        return value, stat

    def attend_rows(group, _):
        halves = []
        for at in range(2):
            va, sa = attend(2 * group + at, 0)
            vb, sb = attend(2 * group + at, 1)
            halves.append((merge(va, vb), merge(sa, sb)))
        value = jnp.concatenate([halves[0][0], halves[1][0]], axis=1).astype(BF16)
        stat = jnp.concatenate([halves[0][1], halves[1][1]], axis=1).astype(BF16)
        part_out[group, :, 0:16, :] = value
        part_out[group, :, 16:32, :] = stat

        def send(tile, _):
            dest = 4 * tile + group

            @pl.when(dest != s)
            def _():
                rcopy(part_out.at[group, tile], part_in.at[s], 2, dest, z)

            return 0

        lax.fori_loop(0, 8, send, 0)
        return 0

    lax.fori_loop(0, 3, attend_rows, 0)

    for group in range(3, 8):
        for at, tile in enumerate(tiles_of(group)):
            qkv[3 * group + at] = tile

    wait_bytes(w_rows.at[pl.ds(0, 3)], recv_sem.at[1])

    @pl.when(rg < 3)
    def _():
        part_in[s] = part_out[rg, t]
        rows = pl.ds(pl.multiple_of(16 * rg, 16), 16)
        lanes = pl.ds(pl.multiple_of(128 * t, 128), 128)
        q_own = qkv[t, rows, :]
        k_own = qkv[8 + t, rows, :].astype(BF16)
        v_own = qkv[16 + t, rows, :].astype(BF16)
        k_sink = sinks[0, rows, lanes].astype(BF16)
        v_sink = sinks[1, rows, lanes].astype(BF16)
        rep_row = iota((64, 16), 0)
        rep_col = iota((64, 16), 1)
        repeat = (
            ((rep_row % 16) // 4 == rep_col // 4) & (rep_row // 16 == rep_col % 4)
        ).astype(F32).astype(BF16)
        keys = jnp.concatenate(
            [
                jnp.dot(repeat, k_sink, preferred_element_type=F32),
                jnp.dot(repeat, k_own, preferred_element_type=F32),
            ],
            axis=0,
        ).reshape(8, 16, 128)
        vals = jnp.concatenate(
            [
                jnp.dot(repeat, v_sink, preferred_element_type=F32),
                jnp.dot(repeat, v_own, preferred_element_type=F32),
            ],
            axis=0,
        ).reshape(8, 16, 128)
        prod = (q_own[None] * keys).reshape(128, 128)
        prod_hi = prod.astype(BF16)
        prod_low = (prod - prod_hi.astype(F32)).astype(BF16)
        same_half = (
            (iota((128, 128), 0) < 64) == (iota((128, 128), 1) < 64)
        ).astype(F32).astype(BF16)
        score = (
            jnp.dot(prod_hi, same_half, preferred_element_type=F32)
            + jnp.dot(prod_low, same_half, preferred_element_type=F32)
        ).reshape(8, 16, 128) * (HD ** (-0.5))
        key_id = iota((8, 16, 128), 0)
        row_step = iota((8, 16, 128), 1) % STEPS
        live = (key_id < SINKS) | (key_id - SINKS <= row_step)
        near_peak = jnp.max(jnp.where(live, score, MASKED), axis=0)
        weight = jnp.where(live, jnp.exp(score - near_peak[None]), 0.0)
        near_total = jnp.sum(weight, axis=0)
        near_value = jnp.sum(weight.astype(BF16).astype(F32) * vals, axis=0)

        wait_bytes(part_in.at[pl.ds(0, seq_count - 1)], recv_sem.at[2])
        spread_row = iota((128, 256), 0)
        spread_col = iota((128, 256), 1)
        kk = spread_row % 64
        wanted = jnp.where(spread_col < 128, (kk < 3).astype(F32), ((kk == 3) | (kk == 4)).astype(F32))
        spread = jnp.where(
            (spread_row < 64) == (spread_col % 128 < 64), wanted, 0.0
        ).astype(BF16)
        stats = jnp.dot(
            part_in[:, 16:32, :].reshape(seq_count * 16, 128), spread, preferred_element_type=F32
        ).reshape(seq_count, 16, 256)
        peaks = stats[:, :, 0:128]
        totals = stats[:, :, 128:256]
        overall = jnp.maximum(jnp.max(peaks, axis=0), near_peak)
        factor = jnp.exp(peaks - overall[None])
        near_factor = jnp.exp(near_peak - overall)
        total = jnp.sum(factor * totals, axis=0) + near_factor * near_total
        value = (
            jnp.sum(factor * part_in[:, 0:16, :].astype(F32), axis=0) + near_factor * near_value
        )
        att_in[t] = (value / total).astype(BF16)

        def send_att(k, _):
            rcopy(att_in.at[t], att_in.at[t], 3, 4 * lax.rem(t + k, 8) + rg, z)
            return 0

        lax.fori_loop(1, 8, send_att, 0)
        wait_bytes(att_in.at[pl.ds(0, 7)], recv_sem.at[3])
        attended = jnp.concatenate([att_in[k] for k in range(8)], axis=1)
        weights = w_rows[...].reshape(128, 1024)
        proj_in[8 * rg + t] = lax.dot_general(
            attended, weights, LAST, preferred_element_type=F32
        ).astype(BF16)
        to_plane(proj_in.at[8 * rg + t], proj_in.at[8 * rg + t], 4)
        wait_bytes(proj_in.at[pl.ds(0, 23)], recv_sem.at[4])

    @pl.when(rg == 3)
    def _():
        wait_bytes(proj_in, recv_sem.at[4])

    projected = jnp.concatenate(
        [
            jnp.concatenate([proj_in[8 * g + k] for k in range(8)], axis=1)
            for g in range(3)
        ],
        axis=0,
    )
    residual = x_tok[...] + projected.astype(F32)
    x_tok[...] = residual
    inverse = lax.rsqrt(jnp.mean(residual * residual, axis=-1, keepdims=True) + EPSILON)
    normed = (residual * inverse * moe_gain_ref[...]).astype(BF16)
    buffer = jnp.dot(dispatch, normed, preferred_element_type=F32)
    disp_out[...] = buffer.reshape(8, 8, 1024).astype(BF16)

    def send_rows(k, _):
        dest = lax.rem(z + k, group_count)
        rcopy(disp_out.at[dest], disp_in.at[z], 5, s, dest)
        return 0

    lax.fori_loop(1, group_count, send_rows, 0)
    disp_in[z] = disp_out[z]

    logits = jnp.dot(normed, router_ref[...], preferred_element_type=F32)
    gates = jnp.zeros((48, 64), F32)
    for c in range(2):
        logit = jnp.sum(onehots[c] * logits, axis=1, keepdims=True)
        gates = gates + picks[c] * jax.nn.sigmoid(logit)
    gates_hi = gates.astype(BF16)
    gates_low = (gates - gates_hi.astype(F32)).astype(BF16)

    pltpu.make_async_copy(in_hbm.at[:, 0], win, wt_sem.at[0]).wait()
    pltpu.make_async_copy(down_hbm.at[0], down, wt_sem.at[1]).wait()
    wait_bytes(disp_in.at[pl.ds(0, group_count - 1)], recv_sem.at[5])
    rows_in = disp_in[...].astype(F32).reshape(64, 1024).astype(BF16)
    gate_part = lax.dot_general(rows_in, win[0], LAST, preferred_element_type=F32)
    up_part = lax.dot_general(rows_in, win[1], LAST, preferred_element_type=F32)
    hidden = (jax.nn.gelu(gate_part, approximate=True) * up_part).astype(BF16)
    partial = jnp.dot(hidden, down[...], preferred_element_type=F32).astype(BF16)
    for g in range(2):
        for k in range(8):
            exp_out[8 * g + k] = partial[32 * g : 32 * g + 32, 128 * k : 128 * k + 128]

    def send_exp(k, _):
        dest = lax.rem(owner16 + k, 16)
        rcopy(exp_out.at[dest], exp_in.at[owner16], 6, 16 * half + dest, z)
        return 0

    lax.fori_loop(1, 16, send_exp, 0)
    exp_in[owner16] = exp_out[owner16]
    wait_bytes(exp_in.at[pl.ds(0, 15)], recv_sem.at[6])
    summed = jnp.sum(exp_in[...].astype(F32), axis=0)
    back_out[...] = summed.reshape(4, 8, 128).astype(BF16)

    def send_back(k, _):
        dest = 4 * gh + k

        @pl.when(dest != z)
        def _():
            rcopy(back_out.at[k], back_in.at[z], 7, s, dest)

        return 0

    lax.fori_loop(0, 4, send_back, 0)
    here = gh == z // 4

    @pl.when(here)
    def _():
        back_in[z] = back_out[lax.rem(z, 4)]
        wait_bytes(back_in.at[pl.ds(0, group_count - 1)], recv_sem.at[7])
        returned = back_in[...].astype(F32).reshape(64, 128).astype(BF16)
        fin_in[owner8] = (
            jnp.dot(gates_hi, returned, preferred_element_type=F32)
            + jnp.dot(gates_low, returned, preferred_element_type=F32)
        ).astype(BF16)
        to_plane(fin_in.at[owner8], fin_in.at[owner8], 8)
        wait_bytes(fin_in.at[pl.ds(0, 15)], recv_sem.at[8])

    @pl.when(jnp.logical_not(here))
    def _():
        wait_bytes(fin_in, recv_sem.at[8])

    for k in range(8):
        lanes = slice(128 * k, 128 * k + 128)
        out_ref[:, lanes] = (
            x_tok[:, lanes] + (fin_in[k].astype(F32) + fin_in[8 + k].astype(F32))
        ).astype(BF16)

    wait_bytes(qkv_in.at[pl.ds(0, seq_count - 1)], send_sem.at[0])
    wait_bytes(w_rows.at[pl.ds(0, 3)], send_sem.at[1])

    @pl.when(rg < 3)
    def _():
        wait_bytes(part_in.at[pl.ds(0, 23)], send_sem.at[2])
        wait_bytes(att_in.at[pl.ds(0, 7)], send_sem.at[3])
        wait_bytes(part_in.at[pl.ds(0, 31), pl.ds(0, 16)], send_sem.at[4])

    @pl.when(rg == 3)
    def _():
        wait_bytes(part_in.at[pl.ds(0, 24)], send_sem.at[2])

    wait_bytes(disp_in.at[pl.ds(0, group_count - 1)], send_sem.at[5])
    wait_bytes(exp_in.at[pl.ds(0, 15)], send_sem.at[6])

    @pl.when(here)
    def _():
        wait_bytes(back_out.at[pl.ds(0, 3)], send_sem.at[7])
        wait_bytes(qkv_in.at[pl.ds(0, seq_count - 1)], send_sem.at[8])

    @pl.when(jnp.logical_not(here))
    def _():
        wait_bytes(back_out, send_sem.at[7])


def solution(mesh):
    seq_count = mesh.shape["seq"]
    group_count = mesh.shape["exp"]
    vmem = pl.BlockSpec(memory_space=pltpu.VMEM)
    hbm = pl.BlockSpec(memory_space=pl.ANY)
    smem = pl.BlockSpec(memory_space=pltpu.SMEM)

    def body(
        tokens,
        attn_gain,
        w_qkv,
        window_cache,
        sink_cache,
        lengths,
        w_out,
        moe_gain,
        router,
        expert_ids,
        slot_order,
        expert_in,
        expert_down,
    ):
        out = pl.pallas_call(
            functools.partial(layer_kernel, seq_count, group_count),
            out_shape=jax.ShapeDtypeStruct((48, 1024), BF16),
            in_specs=[vmem, vmem, vmem, hbm, vmem, smem, vmem, vmem, vmem, vmem, vmem, hbm, hbm],
            out_specs=vmem,
            scratch_shapes=[
                pltpu.VMEM((2, 12, 128, 1024), BF16),
                pltpu.VMEM((2, 176, 1024), BF16),
                pltpu.VMEM((176, 1024), BF16),
                pltpu.VMEM((48, 1024), F32),
                pltpu.VMEM((48, 2), jnp.int32),
                pltpu.VMEM((48, 128), BF16),
                pltpu.VMEM((32, 48, 128), BF16),
                pltpu.VMEM((24, 48, 128), F32),
                pltpu.VMEM((6, 2, 4, 16, 256), BF16),
                pltpu.VMEM((3, 8, 32, 128), BF16),
                pltpu.VMEM((32, 32, 128), BF16),
                pltpu.VMEM((2, 48, 1024), F32),
                pltpu.VMEM((8, 16, 128), BF16),
                pltpu.VMEM((4, 32, 1024), BF16),
                pltpu.VMEM((24, 16, 128), BF16),
                pltpu.VMEM((8, 8, 1024), BF16),
                pltpu.VMEM((8, 8, 1024), BF16),
                pltpu.VMEM((16, 32, 128), BF16),
                pltpu.VMEM((16, 32, 128), BF16),
                pltpu.VMEM((4, 8, 128), BF16),
                pltpu.VMEM((8, 8, 128), BF16),
                pltpu.VMEM((16, 48, 128), BF16),
                pltpu.SemaphoreType.DMA((2, 3)),
                pltpu.SemaphoreType.DMA((2,)),
                pltpu.SemaphoreType.DMA((1,)),
                pltpu.SemaphoreType.DMA((9,)),
                pltpu.SemaphoreType.DMA((9,)),
            ],
            compiler_params=pltpu.CompilerParams(
                collective_id=0, has_side_effects=True, vmem_limit_bytes=48 * 1024 * 1024
            ),
            name="layer",
        )(
            tokens,
            attn_gain.reshape(1, -1),
            w_qkv,
            window_cache,
            sink_cache,
            lengths,
            w_out,
            moe_gain.reshape(1, -1),
            router,
            expert_ids,
            slot_order,
            expert_in,
            expert_down,
        )
        return out.reshape(tokens.shape)

    in_specs = (
        P("exp", None, None),
        P(),
        P("seq", None),
        P(None, "exp", "seq", None),
        P(None, "exp", None, None),
        P("exp"),
        P("seq", None),
        P(),
        P(),
        P("exp", None, None),
        P("exp", None),
        P(None, "exp", "seq", None),
        P("exp", "seq", None),
    )
    out_specs = P("exp", None, None)
    return jax.shard_map(body, mesh=mesh, in_specs=in_specs, out_specs=out_specs, check_vma=False)
```

```python
import functools

import jax
import jax.numpy as jnp
from jax import lax
from jax.experimental import pallas as pl
from jax.experimental.pallas import tpu as pltpu
from jax.sharding import PartitionSpec as P

HEADS = 16
HD = 64
EXPERTS = 16
SINKS = 4
WIN = 4096
CAP = 8
STEPS = 4
EPSILON = 1e-06
MASKED = -1e30
QUERY_BLOCKS = 11
MESH = pl.DeviceIdType.MESH
F32 = jnp.float32
BF16 = jnp.bfloat16
LAST = (((1,), (1,)), ((), ()))


def iota(shape, axis):
    return lax.broadcasted_iota(jnp.int32, shape, axis)


def wait_bytes(ref, sem):
    pltpu.make_async_copy(ref, ref, sem).wait()


def layer_kernel(
    seq_count,
    group_count,
    tokens_hbm,
    attn_gain_hbm,
    w_qkv_hbm,
    cache_hbm,
    sink_hbm,
    lengths_hbm,
    w_out_hbm,
    moe_gain_hbm,
    router_hbm,
    ids_hbm,
    order_hbm,
    in_hbm,
    down_hbm,
    out_ref,
    tokens_ref,
    attn_gain_ref,
    w_qkv_ref,
    sink_ref,
    lengths_ref,
    w_out_ref,
    moe_gain_ref,
    router_ref,
    ids_ref,
    order_ref,
    kv,
    win,
    down,
    x_tok,
    mix,
    qkv_in,
    qkv,
    near,
    q4,
    part_out,
    part_in,
    sinks,
    att_in,
    w_rows,
    proj_in,
    disp_out,
    disp_in,
    exp_out,
    exp_in,
    back_out,
    back_in,
    fin_in,
    mix_send,
    mix_recv,
    kv_sem,
    wt_sem,
    arg_sem,
    send_sem,
    recv_sem,
):
    s = lax.axis_index("seq")
    z = lax.axis_index("exp")
    col = s // 8
    rg = lax.rem(s // 2, 4)
    core = lax.rem(s, 2)
    t = 2 * col + core
    half = s // 16
    owner16 = lax.rem(s, 16)
    owner = rg < 3
    own_rows = core == rg // 2

    def holder(tile, group):
        return 8 * (tile // 2) + 2 * group + lax.rem(tile, 2)

    small = (
        (tokens_hbm, tokens_ref),
        (w_qkv_hbm, w_qkv_ref),
        (attn_gain_hbm, attn_gain_ref),
        (w_out_hbm, w_out_ref),
        (ids_hbm, ids_ref),
        (order_hbm, order_ref),
        (sink_hbm, sink_ref),
        (lengths_hbm, lengths_ref),
        (moe_gain_hbm, moe_gain_ref),
        (router_hbm, router_ref),
    )

    def fetch(at):
        return pltpu.make_async_copy(small[at][0], small[at][1], arg_sem.at[at])

    for at in range(len(small)):
        fetch(at).start()

    barrier = pltpu.get_barrier_semaphore()

    def greet_plane(k, _):
        pl.semaphore_signal(
            barrier, inc=1, device_id=(lax.rem(s + k, seq_count), z), device_id_type=MESH
        )
        return 0

    def greet_line(k, _):
        pl.semaphore_signal(
            barrier, inc=1, device_id=(s, lax.rem(z + k, group_count)), device_id_type=MESH
        )
        return 0

    lax.fori_loop(1, seq_count, greet_plane, 0)
    lax.fori_loop(1, group_count, greet_line, 0)

    for part in range(3):
        for which in range(2):
            pltpu.make_async_copy(
                cache_hbm.at[which, pl.ds(4 * part, 4)],
                kv.at[which, pl.ds(4 * part, 4)],
                kv_sem.at[which, part],
            ).start()
    pltpu.make_async_copy(in_hbm.at[:, 0], win, wt_sem.at[0]).start()
    pltpu.make_async_copy(down_hbm.at[0], down, wt_sem.at[1]).start()

    def rcopy(src, dst, stage, dest_s, dest_z):
        pltpu.make_async_remote_copy(
            src_ref=src,
            dst_ref=dst,
            send_sem=send_sem.at[stage],
            recv_sem=recv_sem.at[stage],
            device_id=(dest_s, dest_z),
            device_id_type=MESH,
        ).start()

    def to_plane(src, dst, stage):
        def send(k, _):
            rcopy(src, dst, stage, lax.rem(s + k, seq_count), z)
            return 0

        lax.fori_loop(1, seq_count, send, 0)

    for at in range(3):
        fetch(at).wait()
    for r in range(12):
        x_tok[4 * r : 4 * r + 4, :] = tokens_ref[r].astype(F32)
    x = x_tok[...]
    inverse = lax.rsqrt(jnp.mean(x * x, axis=-1, keepdims=True) + EPSILON)
    normed = (x * inverse * attn_gain_ref[...]).astype(BF16)
    own_mix = lax.dot_general(normed, w_qkv_ref[...], LAST, preferred_element_type=F32)
    mix[...] = jnp.concatenate([own_mix, jnp.zeros((48, 32), F32)], axis=1).astype(BF16)

    pl.semaphore_wait(barrier, seq_count - 1 + group_count - 1)

    def send_mix(at, dest):
        return pltpu.make_async_remote_copy(
            src_ref=mix,
            dst_ref=qkv_in.at[s],
            send_sem=mix_send.at[at],
            recv_sem=mix_recv.at[s],
            device_id=(dest, z),
            device_id_type=MESH,
        )

    has_query = s < QUERY_BLOCKS
    first_tile = (96 * s) // 128
    last_tile = (96 * s + 95) // 128

    @pl.when(has_query)
    def _():
        def send(k, _):
            send_mix(0, lax.rem(s + k, seq_count)).start()
            return 0

        lax.fori_loop(1, seq_count, send, 0)

    def each_owner(act):
        for group in range(3):
            for at, tile in enumerate((first_tile, last_tile)):
                dest = holder(lax.rem(tile, 8), group)
                go = jnp.logical_not(has_query) & (dest != s)
                if at == 1:
                    go = go & (first_tile != last_tile)

                @pl.when(go)
                def _():
                    act(send_mix(1 + 2 * group + at, dest))

    each_owner(lambda copy: copy.start())
    qkv_in[s] = mix[...]
    fetch(3).wait()

    w_at = 2 * lax.rem(rg, 2) + core

    @pl.when(owner & own_rows)
    def _():
        w_rows[w_at] = w_out_ref[...]

    for group in range(3):
        w_dest = 8 * col + 2 * group + rg // 2

        @pl.when(w_dest != s)
        def _():
            rcopy(w_out_ref, w_rows.at[w_at], 1, w_dest, z)

    for at in range(4, 10):
        fetch(at).wait()
    eye = iota((48, 48), 0) == iota((48, 48), 1)
    prio_row = order_ref[...]
    prio_col = jnp.sum(jnp.where(eye, prio_row, 0), axis=1, keepdims=True)
    earlier = (prio_row < prio_col).astype(F32).astype(BF16)
    expert_lane = iota((48, EXPERTS), 1)
    id_row_of = iota((48, 12), 0)
    id_lane = iota((48, 12), 1)
    id_cols = []
    onehots = []
    for c in range(2):
        spread_ids = jnp.zeros((48, 12), jnp.int32)
        for step in range(STEPS):
            wanted = (id_row_of // STEPS == id_lane) & (id_row_of % STEPS == step)
            spread_ids = spread_ids + jnp.where(wanted, ids_ref[step, c : c + 1, :], 0)
        id_cols.append(jnp.sum(spread_ids, axis=1, keepdims=True))
        onehots.append((expert_lane == id_cols[c]).astype(F32))
    counts = jnp.dot(earlier, (onehots[0] + onehots[1]).astype(BF16), preferred_element_type=F32)
    sel_rows = iota((64, 48), 0)
    sel_expert = 2 * (sel_rows // CAP) + half
    sel_slot = sel_rows % CAP
    col_ids = iota((48, 64), 1)
    col_expert = 2 * (col_ids // CAP) + half
    col_slot = col_ids % CAP
    dispatch = jnp.zeros((64, 48), F32)
    picks = []
    for c in range(2):
        pos_col = jnp.sum(onehots[c] * counts, axis=1, keepdims=True).astype(jnp.int32)
        id_col = id_cols[c]
        pos_row = jnp.sum(jnp.where(eye, pos_col, 0), axis=0, keepdims=True)
        id_row = jnp.sum(jnp.where(eye, id_col, 0), axis=0, keepdims=True)
        dispatch = dispatch + ((id_row == sel_expert) & (pos_row == sel_slot)).astype(F32)
        picks.append(((id_col == col_expert) & (pos_col == col_slot)).astype(F32))
    dispatch = dispatch.astype(BF16)

    for r in range(12):
        for which in range(2):
            sinks[which, 4 * r : 4 * r + 4, :] = sink_ref[which, r].astype(F32)

    lane48 = iota((48, 128), 1)

    def tiles_of(group):
        last = min(4 * group + 3, QUERY_BLOCKS - 1)
        b0, b1, b2 = (qkv_in[4 * group + k].astype(F32) for k in range(3))
        b3 = qkv_in[last].astype(F32)
        r1 = pltpu.roll(b1, 96, 1)
        r2 = pltpu.roll(b2, 64, 1)
        r3 = pltpu.roll(b3, 32, 1)
        return (
            jnp.where(lane48 < 96, b0, r1),
            jnp.where(lane48 < 64, r1, r2),
            jnp.where(lane48 < 32, r2, r3),
        )

    def wait_block(block):
        @pl.when(block != s)
        def _():
            wait_bytes(qkv_in.at[block], mix_recv.at[block])

    def wait_query(block, _):
        wait_block(block)
        return 0

    lax.fori_loop(0, QUERY_BLOCKS, wait_query, 0)
    tiles = []
    for group in range(3):
        for at, tile in enumerate(tiles_of(group)):
            tiles.append(tile)
            if 3 * group + at < 8:
                qkv[3 * group + at] = tile
    sub6 = iota((6, 8, 128), 1)
    lane6 = iota((6, 8, 128), 2)
    diag6 = (sub6 < 4) == (lane6 < 64)
    zero6 = jnp.zeros((6, 8, 128), F32)
    for u in range(4):
        tops = []
        for tile in (tiles[2 * u], tiles[2 * u + 1]):
            v = tile.reshape(6, 8, 128)
            w = pltpu.roll(v, 4, 1)
            even = jnp.where(diag6, jnp.where(sub6 < 4, v, w), 0.0)
            odd = jnp.where(diag6, jnp.where(sub6 < 4, w, v), 0.0)
            tops.append((even, odd))
        for parity in range(2):
            upper = jnp.concatenate([tops[0][parity], zero6], axis=2)
            lower = jnp.concatenate([zero6, tops[1][parity]], axis=2)
            q4[:, parity, u] = jnp.concatenate([upper, lower], axis=1).astype(BF16)

    for part in range(3):
        for which in range(2):
            pltpu.make_async_copy(
                cache_hbm.at[which, pl.ds(4 * part, 4)],
                kv.at[which, pl.ds(4 * part, 4)],
                kv_sem.at[which, part],
            ).wait()

    sub8 = iota((8, 8, 128), 1)
    lane8 = iota((8, 8, 128), 2)
    lane_in = lane8 % 64
    step_id = iota((8, 128), 0) % STEPS
    slot_id = s * 128 + iota((8, 128), 1)

    def merge(a, b):
        ar = pltpu.roll(a, 4, 1)
        br = pltpu.roll(b, 4, 1)
        return jnp.where(
            sub8 < 4, jnp.where(lane8 < 64, a, ar), jnp.where(lane8 < 64, br, b)
        )

    def attend(pair, parity):
        r = 2 * pair + parity
        scores = []
        for u in range(4):
            scores.append(
                lax.dot_general(
                    q4[pair, parity, u],
                    kv[0, r, :, 256 * u : 256 * u + 256],
                    LAST,
                    preferred_element_type=F32,
                )
            )
        score = jnp.concatenate(scores, axis=0).reshape(8, 8, 128) * (HD ** (-0.5))
        held = lengths_ref[r] - SINKS
        age = (slot_id - held) & (WIN - 1)
        live = ((slot_id < jnp.minimum(WIN, held)) & (age > step_id))[None]
        peak = jnp.max(jnp.where(live, score, MASKED), axis=-1, keepdims=True)
        weight = jnp.where(live, jnp.exp(score - peak), 0.0)
        total = jnp.sum(weight, axis=-1, keepdims=True)
        rounded = weight.reshape(64, 128).astype(BF16)
        values = []
        for u in range(4):
            mixed = jnp.dot(
                rounded[16 * u : 16 * u + 16],
                kv[1, r, :, 256 * u : 256 * u + 256],
                preferred_element_type=F32,
            )
            values.append(mixed[0:8, 0:128])
            values.append(mixed[8:16, 128:256])
        value = jnp.concatenate(values, axis=0).reshape(8, 8, 128)
        peak = jnp.broadcast_to(peak, (8, 8, 128))
        total = jnp.broadcast_to(total, (8, 8, 128))
        p_hi = peak.astype(BF16).astype(F32)
        p_mid = (peak - p_hi).astype(BF16).astype(F32)
        p_low = peak - p_hi - p_mid
        t_hi = total.astype(BF16).astype(F32)
        t_low = total - t_hi
        stat = jnp.where(
            lane_in == 0,
            p_hi,
            jnp.where(
                lane_in == 1,
                p_mid,
                jnp.where(
                    lane_in == 2,
                    p_low,
                    jnp.where(lane_in == 3, t_hi, jnp.where(lane_in == 4, t_low, 0.0)),
                ),
            ),
        )
        return value, stat

    def attend_rows(group, _):
        halves = []
        for at in range(2):
            va, sa = attend(2 * group + at, 0)
            vb, sb = attend(2 * group + at, 1)
            halves.append((merge(va, vb), merge(sa, sb)))
        value = jnp.concatenate([halves[0][0], halves[1][0]], axis=1).astype(BF16)
        stat = jnp.concatenate([halves[0][1], halves[1][1]], axis=1).astype(BF16)
        part_out[group, :, 0:16, :] = value
        part_out[group, :, 16:32, :] = stat

        def send(tile, _):
            dest = holder(tile, group)

            @pl.when(dest != s)
            def _():
                rcopy(part_out.at[group, tile], part_in.at[s], 2, dest, z)

            return 0

        lax.fori_loop(0, 8, send, 0)
        return 0

    lax.fori_loop(0, 3, attend_rows, 0)

    @pl.when(owner & own_rows)
    def _():
        wait_bytes(w_rows.at[pl.ds(0, 3)], recv_sem.at[1])

    @pl.when(owner & jnp.logical_not(own_rows))
    def _():
        wait_bytes(w_rows, recv_sem.at[1])

    @pl.when(owner)
    def _():
        part_in[s] = part_out[rg, t]
        rows = pl.ds(pl.multiple_of(16 * rg, 16), 16)
        lanes = pl.ds(pl.multiple_of(128 * t, 128), 128)
        q_own = qkv[t, rows, :]

        def own_tile(tile):
            block = (128 * tile) // 96
            offset = 128 * tile - 96 * block
            for b in (block, block + 1):

                @pl.when(b >= QUERY_BLOCKS)
                def _():
                    wait_block(b)

            low = pltpu.roll(qkv_in[block, rows, :].astype(F32), 128 - offset, 1)
            high = pltpu.roll(qkv_in[block + 1, rows, :].astype(F32), 96 - offset, 1)
            return jnp.where(iota((16, 128), 1) < 96 - offset, low, high).astype(BF16)

        k_own = own_tile(8 + t)
        v_own = own_tile(16 + t)
        k_sink = sinks[0, rows, lanes].astype(BF16)
        v_sink = sinks[1, rows, lanes].astype(BF16)
        rep_row = iota((64, 16), 0)
        rep_col = iota((64, 16), 1)
        repeat = (
            ((rep_row % 16) // 4 == rep_col // 4) & (rep_row // 16 == rep_col % 4)
        ).astype(F32).astype(BF16)
        keys = jnp.concatenate(
            [
                jnp.dot(repeat, k_sink, preferred_element_type=F32),
                jnp.dot(repeat, k_own, preferred_element_type=F32),
            ],
            axis=0,
        ).reshape(8, 16, 128)
        vals = jnp.concatenate(
            [
                jnp.dot(repeat, v_sink, preferred_element_type=F32),
                jnp.dot(repeat, v_own, preferred_element_type=F32),
            ],
            axis=0,
        ).reshape(8, 16, 128)
        prod = (q_own[None] * keys).reshape(128, 128)
        prod_hi = prod.astype(BF16)
        prod_low = (prod - prod_hi.astype(F32)).astype(BF16)
        same_half = (
            (iota((128, 128), 0) < 64) == (iota((128, 128), 1) < 64)
        ).astype(F32).astype(BF16)
        score = (
            jnp.dot(prod_hi, same_half, preferred_element_type=F32)
            + jnp.dot(prod_low, same_half, preferred_element_type=F32)
        ).reshape(8, 16, 128) * (HD ** (-0.5))
        key_id = iota((8, 16, 128), 0)
        row_step = iota((8, 16, 128), 1) % STEPS
        live = (key_id < SINKS) | (key_id - SINKS <= row_step)
        near_peak = jnp.max(jnp.where(live, score, MASKED), axis=0)
        weight = jnp.where(live, jnp.exp(score - near_peak[None]), 0.0)
        near_total = jnp.sum(weight, axis=0)
        near_value = jnp.sum(weight.astype(BF16).astype(F32) * vals, axis=0)

        near[0] = near_peak
        near[1] = near_total
        near[2] = near_value
        wait_bytes(part_in.at[pl.ds(0, seq_count - 1)], recv_sem.at[2])


    @pl.when(owner)
    def _():
        near_peak, near_total, near_value = near[0], near[1], near[2]
        spread_row = iota((128, 256), 0)
        spread_col = iota((128, 256), 1)
        kk = spread_row % 64
        wanted = jnp.where(spread_col < 128, (kk < 3).astype(F32), ((kk == 3) | (kk == 4)).astype(F32))
        spread = jnp.where(
            (spread_row < 64) == (spread_col % 128 < 64), wanted, 0.0
        ).astype(BF16)
        stats = jnp.dot(
            part_in[:, 16:32, :].reshape(seq_count * 16, 128), spread, preferred_element_type=F32
        ).reshape(seq_count, 16, 256)
        peaks = stats[:, :, 0:128]
        totals = stats[:, :, 128:256]
        overall = jnp.maximum(jnp.max(peaks, axis=0), near_peak)
        factor = jnp.exp(peaks - overall[None])
        near_factor = jnp.exp(near_peak - overall)
        total = jnp.sum(factor * totals, axis=0) + near_factor * near_total
        value = (
            jnp.sum(factor * part_in[:, 0:16, :].astype(F32), axis=0) + near_factor * near_value
        )
        att_in[t] = (value / total).astype(BF16)

        def send_att(k, _):
            rcopy(att_in.at[t], att_in.at[t], 3, holder(lax.rem(t + k, 8), rg), z)
            return 0

        lax.fori_loop(1, 8, send_att, 0)
        wait_bytes(att_in.at[pl.ds(0, 7)], recv_sem.at[3])


    @pl.when(owner)
    def _():
        attended = jnp.concatenate([att_in[k] for k in range(8)], axis=1)
        weights = w_rows[...].reshape(128, 1024)
        proj_in[8 * rg + t] = lax.dot_general(
            attended, weights, LAST, preferred_element_type=F32
        ).astype(BF16)
        to_plane(proj_in.at[8 * rg + t], proj_in.at[8 * rg + t], 4)
        wait_bytes(proj_in.at[pl.ds(0, 23)], recv_sem.at[4])

    @pl.when(rg == 3)
    def _():
        wait_bytes(proj_in, recv_sem.at[4])


    projected = jnp.concatenate(
        [
            jnp.concatenate([proj_in[8 * g + k] for k in range(8)], axis=1)
            for g in range(3)
        ],
        axis=0,
    )
    residual = x_tok[...] + projected.astype(F32)
    x_tok[...] = residual
    inverse = lax.rsqrt(jnp.mean(residual * residual, axis=-1, keepdims=True) + EPSILON)
    normed = (residual * inverse * moe_gain_ref[...]).astype(BF16)
    own_half = jnp.where(core == 0, normed[:, 0:512], normed[:, 512:1024])
    buffer = jnp.dot(dispatch, own_half, preferred_element_type=F32)
    disp_out[...] = buffer.reshape(8, 8, 512).astype(BF16)

    def send_rows(k, _):
        dest = lax.rem(z + k, group_count)
        rcopy(disp_out.at[dest], disp_in.at[core, z], 5, s, dest)
        return 0

    lax.fori_loop(1, group_count, send_rows, 0)
    disp_in[core, z] = disp_out[z]

    logits = lax.dot_general(normed, router_ref[...], LAST, preferred_element_type=F32)
    gates = jnp.zeros((48, 64), F32)
    for c in range(2):
        logit = jnp.sum(onehots[c] * logits, axis=1, keepdims=True)
        gates = gates + picks[c] * jax.nn.sigmoid(logit)
    gates_hi = gates.astype(BF16)
    gates_low = (gates - gates_hi.astype(F32)).astype(BF16)

    pltpu.make_async_copy(in_hbm.at[:, 0], win, wt_sem.at[0]).wait()
    pltpu.make_async_copy(down_hbm.at[0], down, wt_sem.at[1]).wait()
    wait_bytes(disp_in.at[0, pl.ds(0, group_count - 1)], recv_sem.at[5])
    rcopy(disp_in.at[core], disp_in.at[core], 9, s + 1 - 2 * core, z)
    wait_bytes(disp_in.at[0], recv_sem.at[9])
    rows_in = jnp.concatenate(
        [disp_in[c].astype(F32).reshape(64, 512).astype(BF16) for c in range(2)], axis=1
    )
    gate_part = lax.dot_general(rows_in, win[0], LAST, preferred_element_type=F32)
    up_part = lax.dot_general(rows_in, win[1], LAST, preferred_element_type=F32)
    hidden = (jax.nn.gelu(gate_part, approximate=True) * up_part).astype(BF16)
    partial = jnp.dot(hidden, down[...], preferred_element_type=F32)
    left32 = iota((32, 128), 1) < 64
    for k in range(8):
        upper = partial[0:32, 128 * k : 128 * k + 128]
        lower = partial[32:64, 128 * k : 128 * k + 128]
        exp_out[2 * k] = jnp.where(left32, upper, pltpu.roll(lower, 64, 1)).astype(BF16)
        exp_out[2 * k + 1] = jnp.where(left32, pltpu.roll(upper, 64, 1), lower).astype(BF16)

    def send_exp(k, _):
        dest = lax.rem(owner16 + k, 16)
        rcopy(exp_out.at[dest], exp_in.at[owner16], 6, 16 * half + dest, z)
        return 0

    lax.fori_loop(1, 16, send_exp, 0)
    exp_in[owner16] = exp_out[owner16]
    wait_bytes(exp_in.at[pl.ds(0, 15)], recv_sem.at[6])
    summed = jnp.sum(exp_in[...].astype(F32), axis=0)
    back_out[...] = summed.reshape(4, 8, 128).astype(BF16)

    def send_back(k, _):
        dest = lax.rem(z + k, group_count)
        rcopy(back_out.at[lax.rem(dest, 4)], back_in.at[z], 7, s, dest)
        return 0

    lax.fori_loop(1, group_count, send_back, 0)
    back_in[z] = back_out[lax.rem(z, 4)]
    wait_bytes(back_in.at[pl.ds(0, group_count - 1)], recv_sem.at[7])
    returned = back_in[...].astype(F32).reshape(64, 128).astype(BF16)
    shared = jnp.dot(gates_hi, returned, preferred_element_type=F32) + jnp.dot(
        gates_low, returned, preferred_element_type=F32
    )
    swapped = pltpu.roll(shared, 64, 1)
    left24 = iota((24, 128), 1) < 64
    fin_in[s] = jnp.where(
        z < 4,
        jnp.where(left24, shared[0:24], swapped[24:48]),
        jnp.where(left24, swapped[0:24], shared[24:48]),
    ).astype(BF16)
    to_plane(fin_in.at[s], fin_in.at[s], 8)
    wait_bytes(fin_in.at[pl.ds(0, seq_count - 1)], recv_sem.at[8])

    for k in range(8):
        lanes = slice(128 * k, 128 * k + 128)
        even = fin_in[2 * k].astype(F32) + fin_in[16 + 2 * k].astype(F32)
        odd = fin_in[2 * k + 1].astype(F32) + fin_in[17 + 2 * k].astype(F32)
        upper = jnp.where(left24, even, pltpu.roll(odd, 64, 1))
        lower = jnp.where(left24, pltpu.roll(even, 64, 1), odd)
        out_ref[0:24, lanes] = (x_tok[0:24, lanes] + upper).astype(BF16)
        out_ref[24:48, lanes] = (x_tok[24:48, lanes] + lower).astype(BF16)

    @pl.when(has_query)
    def _():
        wait_bytes(qkv_in.at[pl.ds(0, seq_count - 1)], mix_send.at[0])

    each_owner(lambda copy: copy.wait_send())

    @pl.when(owner & own_rows)
    def _():
        wait_bytes(w_rows.at[pl.ds(0, 2)], send_sem.at[1])

    @pl.when(jnp.logical_not(owner & own_rows))
    def _():
        wait_bytes(w_rows.at[pl.ds(0, 3)], send_sem.at[1])

    @pl.when(owner)
    def _():
        wait_bytes(part_in.at[pl.ds(0, 23)], send_sem.at[2])
        wait_bytes(att_in.at[pl.ds(0, 7)], send_sem.at[3])
        wait_bytes(part_in.at[pl.ds(0, 31), pl.ds(0, 16)], send_sem.at[4])

    @pl.when(jnp.logical_not(owner))
    def _():
        wait_bytes(part_in.at[pl.ds(0, 24)], send_sem.at[2])

    wait_bytes(disp_in.at[0, pl.ds(0, group_count - 1)], send_sem.at[5])
    wait_bytes(disp_in.at[0], send_sem.at[9])
    wait_bytes(exp_in.at[pl.ds(0, 15)], send_sem.at[6])
    wait_bytes(back_in.at[pl.ds(0, group_count - 1)], send_sem.at[7])
    wait_bytes(fin_in.at[pl.ds(0, seq_count - 1)], send_sem.at[8])


def solution(mesh):
    seq_count = mesh.shape["seq"]
    group_count = mesh.shape["exp"]
    vmem = pl.BlockSpec(memory_space=pltpu.VMEM)
    hbm = pl.BlockSpec(memory_space=pltpu.HBM)

    def body(
        tokens,
        attn_gain,
        w_qkv,
        window_cache,
        sink_cache,
        lengths,
        w_out,
        moe_gain,
        router,
        expert_ids,
        slot_order,
        expert_in,
        expert_down,
    ):
        out = pl.pallas_call(
            functools.partial(layer_kernel, seq_count, group_count),
            out_shape=jax.ShapeDtypeStruct((48, 1024), BF16),
            in_specs=[hbm] * 13,
            out_specs=vmem,
            scratch_shapes=[
                pltpu.VMEM((12, 4, 1024), BF16),
                pltpu.VMEM((1, 1024), F32),
                pltpu.VMEM((96, 1024), BF16),
                pltpu.VMEM((2, 12, 4, 1024), BF16),
                pltpu.SMEM((12,), jnp.int32),
                pltpu.VMEM((32, 1024), BF16),
                pltpu.VMEM((1, 1024), F32),
                pltpu.VMEM((16, 1024), BF16),
                pltpu.VMEM((4, 2, 12), jnp.int32),
                pltpu.VMEM((1, 48), jnp.int32),
                pltpu.VMEM((2, 12, 128, 1024), BF16),
                pltpu.VMEM((2, 176, 1024), BF16),
                pltpu.VMEM((176, 1024), BF16),
                pltpu.VMEM((48, 1024), F32),
                pltpu.VMEM((48, 128), BF16),
                pltpu.VMEM((32, 48, 128), BF16),
                pltpu.VMEM((8, 48, 128), F32),
                pltpu.VMEM((3, 16, 128), F32),
                pltpu.VMEM((6, 2, 4, 16, 256), BF16),
                pltpu.VMEM((3, 8, 32, 128), BF16),
                pltpu.VMEM((32, 32, 128), BF16),
                pltpu.VMEM((2, 48, 1024), F32),
                pltpu.VMEM((8, 16, 128), BF16),
                pltpu.VMEM((4, 32, 1024), BF16),
                pltpu.VMEM((24, 16, 128), BF16),
                pltpu.VMEM((8, 8, 512), BF16),
                pltpu.VMEM((2, 8, 8, 512), BF16),
                pltpu.VMEM((16, 32, 128), BF16),
                pltpu.VMEM((16, 32, 128), BF16),
                pltpu.VMEM((4, 8, 128), BF16),
                pltpu.VMEM((8, 8, 128), BF16),
                pltpu.VMEM((32, 24, 128), BF16),
                pltpu.SemaphoreType.DMA((7,)),
                pltpu.SemaphoreType.DMA((32,)),
                pltpu.SemaphoreType.DMA((2, 3)),
                pltpu.SemaphoreType.DMA((2,)),
                pltpu.SemaphoreType.DMA((10,)),
                pltpu.SemaphoreType.DMA((10,)),
                pltpu.SemaphoreType.DMA((10,)),
            ],
            compiler_params=pltpu.CompilerParams(
                collective_id=0, has_side_effects=True, vmem_limit_bytes=67043328
            ),
            name="layer",
        )(
            tokens,
            attn_gain.reshape(1, -1),
            w_qkv,
            window_cache,
            sink_cache,
            lengths,
            w_out,
            moe_gain.reshape(1, -1),
            router.T,
            expert_ids.transpose(1, 2, 0),
            slot_order,
            expert_in,
            expert_down,
        )
        return out.reshape(tokens.shape)

    in_specs = (
        P("exp", None, None),
        P(),
        P("seq", None),
        P(None, "exp", "seq", None),
        P(None, "exp", None, None),
        P("exp"),
        P("seq", None),
        P(),
        P(),
        P("exp", None, None),
        P("exp", None),
        P(None, "exp", "seq", None),
        P("exp", "seq", None),
    )
    out_specs = P("exp", None, None)
    return jax.shard_map(body, mesh=mesh, in_specs=in_specs, out_specs=out_specs, check_vma=False)
```

```python
import functools

import jax
import jax.numpy as jnp
from jax import lax
from jax.experimental import pallas as pl
from jax.experimental.pallas import tpu as pltpu
from jax.sharding import PartitionSpec as P

HEADS = 16
HD = 64
EXPERTS = 16
SINKS = 4
WIN = 4096
CAP = 8
STEPS = 4
EPSILON = 1e-06
MASKED = -1e30
QUERY_BLOCKS = 11
MESH = pl.DeviceIdType.MESH
F32 = jnp.float32
BF16 = jnp.bfloat16
LAST = (((1,), (1,)), ((), ()))


def iota(shape, axis):
    return lax.broadcasted_iota(jnp.int32, shape, axis)


def wait_bytes(ref, sem):
    pltpu.make_async_copy(ref, ref, sem).wait()


def layer_kernel(
    seq_count,
    group_count,
    tokens_hbm,
    attn_gain_hbm,
    w_qkv_hbm,
    cache_hbm,
    sink_hbm,
    lengths_hbm,
    w_out_hbm,
    moe_gain_hbm,
    router_hbm,
    ids_hbm,
    order_hbm,
    in_hbm,
    down_hbm,
    out_ref,
    tokens_ref,
    attn_gain_ref,
    w_qkv_ref,
    sink_ref,
    lengths_ref,
    w_out_ref,
    moe_gain_ref,
    router_ref,
    ids_ref,
    order_ref,
    kv,
    win,
    down,
    x_tok,
    mix,
    qkv_in,
    qkv,
    near,
    q4,
    part_out,
    part_in,
    sinks,
    att_in,
    w_rows,
    proj_in,
    disp_out,
    disp_in,
    exp_out,
    exp_in,
    back_out,
    back_in,
    fin_in,
    mix_send,
    mix_recv,
    kv_sem,
    wt_sem,
    arg_sem,
    send_sem,
    recv_sem,
):
    s = lax.axis_index("seq")
    z = lax.axis_index("exp")
    col = s // 8
    rg = lax.rem(s // 2, 4)
    core = lax.rem(s, 2)
    t = 2 * col + core
    half = s // 16
    owner16 = lax.rem(s, 16)
    owner = rg < 3
    own_rows = core == rg // 2

    def holder(tile, group):
        return 8 * (tile // 2) + 2 * group + lax.rem(tile, 2)

    small = (
        (tokens_hbm, tokens_ref),
        (w_qkv_hbm, w_qkv_ref),
        (attn_gain_hbm, attn_gain_ref),
        (w_out_hbm, w_out_ref),
        (ids_hbm, ids_ref),
        (order_hbm, order_ref),
        (sink_hbm, sink_ref),
        (lengths_hbm, lengths_ref),
        (moe_gain_hbm, moe_gain_ref),
        (router_hbm, router_ref),
    )

    def fetch(at):
        return pltpu.make_async_copy(small[at][0], small[at][1], arg_sem.at[at])

    for at in range(len(small)):
        fetch(at).start()

    barrier = pltpu.get_barrier_semaphore()

    def greet_plane(k, _):
        pl.semaphore_signal(
            barrier, inc=1, device_id=(lax.rem(s + k, seq_count), z), device_id_type=MESH
        )
        return 0

    def greet_line(k, _):
        pl.semaphore_signal(
            barrier, inc=1, device_id=(s, lax.rem(z + k, group_count)), device_id_type=MESH
        )
        return 0

    lax.fori_loop(1, seq_count, greet_plane, 0)
    lax.fori_loop(1, group_count, greet_line, 0)

    for part in range(3):
        for which in range(2):
            pltpu.make_async_copy(
                cache_hbm.at[which, pl.ds(4 * part, 4)],
                kv.at[which, pl.ds(4 * part, 4)],
                kv_sem.at[which, part],
            ).start()
    pltpu.make_async_copy(in_hbm.at[:, 0], win, wt_sem.at[0]).start()
    pltpu.make_async_copy(down_hbm.at[0], down, wt_sem.at[1]).start()

    def rcopy(src, dst, stage, dest_s, dest_z):
        pltpu.make_async_remote_copy(
            src_ref=src,
            dst_ref=dst,
            send_sem=send_sem.at[stage],
            recv_sem=recv_sem.at[stage],
            device_id=(dest_s, dest_z),
            device_id_type=MESH,
        ).start()

    def ring4(at, position):
        return lax.rem(position + ((54 >> (2 * at)) & 3), 4)

    def ring8(at, position):
        return lax.rem(position + ((0o7162534 >> (3 * at)) & 7), group_count)

    def plane_peer(k):
        return 8 * ring4(k // 8, col) + 2 * ring4((k // 2) & 3, rg) + lax.rem(core + 1 + k, 2)

    def to_plane(src, dst, stage):
        def send(k, _):
            rcopy(src, dst, stage, plane_peer(k), z)
            return 0

        lax.fori_loop(0, seq_count - 1, send, 0)

    for at in range(3):
        fetch(at).wait()
    for r in range(12):
        x_tok[4 * r : 4 * r + 4, :] = tokens_ref[r].astype(F32)
    x = x_tok[...]
    inverse = lax.rsqrt(jnp.mean(x * x, axis=-1, keepdims=True) + EPSILON)
    normed = (x * inverse * attn_gain_ref[...]).astype(BF16)
    own_mix = lax.dot_general(normed, w_qkv_ref[...], LAST, preferred_element_type=F32)
    mix[...] = jnp.concatenate([own_mix, jnp.zeros((48, 32), F32)], axis=1).astype(BF16)

    pl.semaphore_wait(barrier, seq_count - 1 + group_count - 1)

    def send_mix(at, dest):
        return pltpu.make_async_remote_copy(
            src_ref=mix,
            dst_ref=qkv_in.at[s],
            send_sem=mix_send.at[at],
            recv_sem=mix_recv.at[s],
            device_id=(dest, z),
            device_id_type=MESH,
        )

    has_query = s < QUERY_BLOCKS
    first_tile = (96 * s) // 128
    last_tile = (96 * s + 95) // 128

    @pl.when(has_query)
    def _():
        def send(k, _):
            send_mix(0, plane_peer(k)).start()
            return 0

        lax.fori_loop(0, seq_count - 1, send, 0)

    def each_owner(act):
        for group in range(3):
            for at, tile in enumerate((first_tile, last_tile)):
                dest = holder(lax.rem(tile, 8), group)
                go = jnp.logical_not(has_query) & (dest != s)
                if at == 1:
                    go = go & (first_tile != last_tile)

                @pl.when(go)
                def _():
                    act(send_mix(1 + 2 * group + at, dest))

    each_owner(lambda copy: copy.start())
    qkv_in[s] = mix[...]
    fetch(3).wait()

    w_at = 2 * lax.rem(rg, 2) + core

    @pl.when(owner & own_rows)
    def _():
        w_rows[w_at] = w_out_ref[...]

    for group in range(3):
        w_dest = 8 * col + 2 * group + rg // 2

        @pl.when(w_dest != s)
        def _():
            rcopy(w_out_ref, w_rows.at[w_at], 1, w_dest, z)

    for at in range(4, 10):
        fetch(at).wait()
    eye = iota((48, 48), 0) == iota((48, 48), 1)
    prio_row = order_ref[...]
    prio_col = jnp.sum(jnp.where(eye, prio_row, 0), axis=1, keepdims=True)
    earlier = (prio_row < prio_col).astype(F32).astype(BF16)
    expert_lane = iota((48, EXPERTS), 1)
    id_row_of = iota((48, 12), 0)
    id_lane = iota((48, 12), 1)
    id_cols = []
    onehots = []
    for c in range(2):
        spread_ids = jnp.zeros((48, 12), jnp.int32)
        for step in range(STEPS):
            wanted = (id_row_of // STEPS == id_lane) & (id_row_of % STEPS == step)
            spread_ids = spread_ids + jnp.where(wanted, ids_ref[step, c : c + 1, :], 0)
        id_cols.append(jnp.sum(spread_ids, axis=1, keepdims=True))
        onehots.append((expert_lane == id_cols[c]).astype(F32))
    counts = jnp.dot(earlier, (onehots[0] + onehots[1]).astype(BF16), preferred_element_type=F32)
    sel_rows = iota((64, 48), 0)
    sel_expert = 2 * (sel_rows // CAP) + half
    sel_slot = sel_rows % CAP
    col_ids = iota((48, 64), 1)
    col_expert = 2 * (col_ids // CAP) + half
    col_slot = col_ids % CAP
    dispatch = jnp.zeros((64, 48), F32)
    picks = []
    for c in range(2):
        pos_col = jnp.sum(onehots[c] * counts, axis=1, keepdims=True).astype(jnp.int32)
        id_col = id_cols[c]
        pos_row = jnp.sum(jnp.where(eye, pos_col, 0), axis=0, keepdims=True)
        id_row = jnp.sum(jnp.where(eye, id_col, 0), axis=0, keepdims=True)
        dispatch = dispatch + ((id_row == sel_expert) & (pos_row == sel_slot)).astype(F32)
        picks.append(((id_col == col_expert) & (pos_col == col_slot)).astype(F32))
    dispatch = dispatch.astype(BF16)

    for r in range(12):
        for which in range(2):
            sinks[which, 4 * r : 4 * r + 4, :] = sink_ref[which, r].astype(F32)

    lane48 = iota((48, 128), 1)

    def tiles_of(group):
        last = min(4 * group + 3, QUERY_BLOCKS - 1)
        b0, b1, b2 = (qkv_in[4 * group + k].astype(F32) for k in range(3))
        b3 = qkv_in[last].astype(F32)
        r1 = pltpu.roll(b1, 96, 1)
        r2 = pltpu.roll(b2, 64, 1)
        r3 = pltpu.roll(b3, 32, 1)
        return (
            jnp.where(lane48 < 96, b0, r1),
            jnp.where(lane48 < 64, r1, r2),
            jnp.where(lane48 < 32, r2, r3),
        )

    def wait_block(block):
        @pl.when(block != s)
        def _():
            wait_bytes(qkv_in.at[block], mix_recv.at[block])

    def wait_query(block, _):
        wait_block(block)
        return 0

    lax.fori_loop(0, QUERY_BLOCKS, wait_query, 0)
    tiles = []
    for group in range(3):
        for at, tile in enumerate(tiles_of(group)):
            tiles.append(tile)
            if 3 * group + at < 8:
                qkv[3 * group + at] = tile
    sub6 = iota((6, 8, 128), 1)
    lane6 = iota((6, 8, 128), 2)
    diag6 = (sub6 < 4) == (lane6 < 64)
    zero6 = jnp.zeros((6, 8, 128), F32)
    for u in range(4):
        tops = []
        for tile in (tiles[2 * u], tiles[2 * u + 1]):
            v = tile.reshape(6, 8, 128)
            w = pltpu.roll(v, 4, 1)
            even = jnp.where(diag6, jnp.where(sub6 < 4, v, w), 0.0)
            odd = jnp.where(diag6, jnp.where(sub6 < 4, w, v), 0.0)
            tops.append((even, odd))
        for parity in range(2):
            upper = jnp.concatenate([tops[0][parity], zero6], axis=2)
            lower = jnp.concatenate([zero6, tops[1][parity]], axis=2)
            q4[:, parity, u] = jnp.concatenate([upper, lower], axis=1).astype(BF16)

    for part in range(3):
        for which in range(2):
            pltpu.make_async_copy(
                cache_hbm.at[which, pl.ds(4 * part, 4)],
                kv.at[which, pl.ds(4 * part, 4)],
                kv_sem.at[which, part],
            ).wait()

    sub8 = iota((8, 8, 128), 1)
    lane8 = iota((8, 8, 128), 2)
    lane_in = lane8 % 64
    step_id = iota((8, 128), 0) % STEPS
    slot_id = s * 128 + iota((8, 128), 1)

    def merge(a, b):
        ar = pltpu.roll(a, 4, 1)
        br = pltpu.roll(b, 4, 1)
        return jnp.where(
            sub8 < 4, jnp.where(lane8 < 64, a, ar), jnp.where(lane8 < 64, br, b)
        )

    def attend(pair, parity):
        r = 2 * pair + parity
        scores = []
        for u in range(4):
            scores.append(
                lax.dot_general(
                    q4[pair, parity, u],
                    kv[0, r, :, 256 * u : 256 * u + 256],
                    LAST,
                    preferred_element_type=F32,
                )
            )
        score = jnp.concatenate(scores, axis=0).reshape(8, 8, 128) * (HD ** (-0.5))
        held = lengths_ref[r] - SINKS
        age = (slot_id - held) & (WIN - 1)
        live = ((slot_id < jnp.minimum(WIN, held)) & (age > step_id))[None]
        peak = jnp.max(jnp.where(live, score, MASKED), axis=-1, keepdims=True)
        weight = jnp.where(live, jnp.exp(score - peak), 0.0)
        total = jnp.sum(weight, axis=-1, keepdims=True)
        rounded = weight.reshape(64, 128).astype(BF16)
        values = []
        for u in range(4):
            mixed = jnp.dot(
                rounded[16 * u : 16 * u + 16],
                kv[1, r, :, 256 * u : 256 * u + 256],
                preferred_element_type=F32,
            )
            values.append(mixed[0:8, 0:128])
            values.append(mixed[8:16, 128:256])
        value = jnp.concatenate(values, axis=0).reshape(8, 8, 128)
        peak = jnp.broadcast_to(peak, (8, 8, 128))
        total = jnp.broadcast_to(total, (8, 8, 128))
        p_hi = peak.astype(BF16).astype(F32)
        p_mid = (peak - p_hi).astype(BF16).astype(F32)
        p_low = peak - p_hi - p_mid
        t_hi = total.astype(BF16).astype(F32)
        t_low = total - t_hi
        stat = jnp.where(
            lane_in == 0,
            p_hi,
            jnp.where(
                lane_in == 1,
                p_mid,
                jnp.where(
                    lane_in == 2,
                    p_low,
                    jnp.where(lane_in == 3, t_hi, jnp.where(lane_in == 4, t_low, 0.0)),
                ),
            ),
        )
        return value, stat

    def attend_rows(group, _):
        halves = []
        for at in range(2):
            va, sa = attend(2 * group + at, 0)
            vb, sb = attend(2 * group + at, 1)
            halves.append((merge(va, vb), merge(sa, sb)))
        value = jnp.concatenate([halves[0][0], halves[1][0]], axis=1).astype(BF16)
        stat = jnp.concatenate([halves[0][1], halves[1][1]], axis=1).astype(BF16)
        part_out[group, :, 0:16, :] = value
        part_out[group, :, 16:32, :] = stat

        def send(k, _):
            tile = 2 * ring4(k // 2, col) + lax.rem(core + k, 2)
            dest = holder(tile, group)

            @pl.when(dest != s)
            def _():
                rcopy(part_out.at[group, tile], part_in.at[s], 2, dest, z)

            return 0

        lax.fori_loop(0, 8, send, 0)
        return 0

    lax.fori_loop(0, 3, attend_rows, 0)

    @pl.when(owner & own_rows)
    def _():
        wait_bytes(w_rows.at[pl.ds(0, 3)], recv_sem.at[1])

    @pl.when(owner & jnp.logical_not(own_rows))
    def _():
        wait_bytes(w_rows, recv_sem.at[1])

    @pl.when(owner)
    def _():
        part_in[s] = part_out[rg, t]
        rows = pl.ds(pl.multiple_of(16 * rg, 16), 16)
        lanes = pl.ds(pl.multiple_of(128 * t, 128), 128)
        q_own = qkv[t, rows, :]

        def own_tile(tile):
            block = (128 * tile) // 96
            offset = 128 * tile - 96 * block
            for b in (block, block + 1):

                @pl.when(b >= QUERY_BLOCKS)
                def _():
                    wait_block(b)

            low = pltpu.roll(qkv_in[block, rows, :].astype(F32), 128 - offset, 1)
            high = pltpu.roll(qkv_in[block + 1, rows, :].astype(F32), 96 - offset, 1)
            return jnp.where(iota((16, 128), 1) < 96 - offset, low, high).astype(BF16)

        k_own = own_tile(8 + t)
        v_own = own_tile(16 + t)
        k_sink = sinks[0, rows, lanes].astype(BF16)
        v_sink = sinks[1, rows, lanes].astype(BF16)
        rep_row = iota((64, 16), 0)
        rep_col = iota((64, 16), 1)
        repeat = (
            ((rep_row % 16) // 4 == rep_col // 4) & (rep_row // 16 == rep_col % 4)
        ).astype(F32).astype(BF16)
        keys = jnp.concatenate(
            [
                jnp.dot(repeat, k_sink, preferred_element_type=F32),
                jnp.dot(repeat, k_own, preferred_element_type=F32),
            ],
            axis=0,
        ).reshape(8, 16, 128)
        vals = jnp.concatenate(
            [
                jnp.dot(repeat, v_sink, preferred_element_type=F32),
                jnp.dot(repeat, v_own, preferred_element_type=F32),
            ],
            axis=0,
        ).reshape(8, 16, 128)
        prod = (q_own[None] * keys).reshape(128, 128)
        prod_hi = prod.astype(BF16)
        prod_low = (prod - prod_hi.astype(F32)).astype(BF16)
        same_half = (
            (iota((128, 128), 0) < 64) == (iota((128, 128), 1) < 64)
        ).astype(F32).astype(BF16)
        score = (
            jnp.dot(prod_hi, same_half, preferred_element_type=F32)
            + jnp.dot(prod_low, same_half, preferred_element_type=F32)
        ).reshape(8, 16, 128) * (HD ** (-0.5))
        key_id = iota((8, 16, 128), 0)
        row_step = iota((8, 16, 128), 1) % STEPS
        live = (key_id < SINKS) | (key_id - SINKS <= row_step)
        near_peak = jnp.max(jnp.where(live, score, MASKED), axis=0)
        weight = jnp.where(live, jnp.exp(score - near_peak[None]), 0.0)
        near_total = jnp.sum(weight, axis=0)
        near_value = jnp.sum(weight.astype(BF16).astype(F32) * vals, axis=0)

        near[0] = near_peak
        near[1] = near_total
        near[2] = near_value
        wait_bytes(part_in.at[pl.ds(0, seq_count - 1)], recv_sem.at[2])


    @pl.when(owner)
    def _():
        near_peak, near_total, near_value = near[0], near[1], near[2]
        spread_row = iota((128, 256), 0)
        spread_col = iota((128, 256), 1)
        kk = spread_row % 64
        wanted = jnp.where(spread_col < 128, (kk < 3).astype(F32), ((kk == 3) | (kk == 4)).astype(F32))
        spread = jnp.where(
            (spread_row < 64) == (spread_col % 128 < 64), wanted, 0.0
        ).astype(BF16)
        stats = jnp.dot(
            part_in[:, 16:32, :].reshape(seq_count * 16, 128), spread, preferred_element_type=F32
        ).reshape(seq_count, 16, 256)
        peaks = stats[:, :, 0:128]
        totals = stats[:, :, 128:256]
        overall = jnp.maximum(jnp.max(peaks, axis=0), near_peak)
        factor = jnp.exp(peaks - overall[None])
        near_factor = jnp.exp(near_peak - overall)
        total = jnp.sum(factor * totals, axis=0) + near_factor * near_total
        value = (
            jnp.sum(factor * part_in[:, 0:16, :].astype(F32), axis=0) + near_factor * near_value
        )
        att_in[t] = (value / total).astype(BF16)

        def send_att(k, _):
            tile = 2 * ring4(k // 2, col) + lax.rem(core + 1 + k, 2)
            rcopy(att_in.at[t], att_in.at[t], 3, holder(tile, rg), z)
            return 0

        lax.fori_loop(0, 7, send_att, 0)
        wait_bytes(att_in.at[pl.ds(0, 7)], recv_sem.at[3])


    @pl.when(owner)
    def _():
        attended = jnp.concatenate([att_in[k] for k in range(8)], axis=1)
        weights = w_rows[...].reshape(128, 1024)
        proj_in[8 * rg + t] = lax.dot_general(
            attended, weights, LAST, preferred_element_type=F32
        ).astype(BF16)
        to_plane(proj_in.at[8 * rg + t], proj_in.at[8 * rg + t], 4)
        wait_bytes(proj_in.at[pl.ds(0, 23)], recv_sem.at[4])

    @pl.when(rg == 3)
    def _():
        wait_bytes(proj_in, recv_sem.at[4])


    projected = jnp.concatenate(
        [
            jnp.concatenate([proj_in[8 * g + k] for k in range(8)], axis=1)
            for g in range(3)
        ],
        axis=0,
    )
    residual = x_tok[...] + projected.astype(F32)
    x_tok[...] = residual
    inverse = lax.rsqrt(jnp.mean(residual * residual, axis=-1, keepdims=True) + EPSILON)
    normed = (residual * inverse * moe_gain_ref[...]).astype(BF16)
    own_half = jnp.where(core == 0, normed[:, 0:512], normed[:, 512:1024])
    buffer = jnp.dot(dispatch, own_half, preferred_element_type=F32)
    disp_out[...] = buffer.reshape(8, 8, 512).astype(BF16)

    def send_rows(k, _):
        dest = ring8(k, z)
        rcopy(disp_out.at[dest], disp_in.at[core, z], 5, s, dest)
        return 0

    lax.fori_loop(0, group_count - 1, send_rows, 0)
    disp_in[core, z] = disp_out[z]

    logits = lax.dot_general(normed, router_ref[...], LAST, preferred_element_type=F32)
    gates = jnp.zeros((48, 64), F32)
    for c in range(2):
        logit = jnp.sum(onehots[c] * logits, axis=1, keepdims=True)
        gates = gates + picks[c] * jax.nn.sigmoid(logit)
    gates_hi = gates.astype(BF16)
    gates_low = (gates - gates_hi.astype(F32)).astype(BF16)

    pltpu.make_async_copy(in_hbm.at[:, 0], win, wt_sem.at[0]).wait()
    pltpu.make_async_copy(down_hbm.at[0], down, wt_sem.at[1]).wait()
    wait_bytes(disp_in.at[0, pl.ds(0, group_count - 1)], recv_sem.at[5])
    rcopy(disp_in.at[core], disp_in.at[core], 9, s + 1 - 2 * core, z)
    wait_bytes(disp_in.at[0], recv_sem.at[9])
    rows_in = jnp.concatenate(
        [disp_in[c].astype(F32).reshape(64, 512).astype(BF16) for c in range(2)], axis=1
    )
    gate_part = lax.dot_general(rows_in, win[0], LAST, preferred_element_type=F32)
    up_part = lax.dot_general(rows_in, win[1], LAST, preferred_element_type=F32)
    hidden = (jax.nn.gelu(gate_part, approximate=True) * up_part).astype(BF16)
    partial = jnp.dot(hidden, down[...], preferred_element_type=F32)
    left32 = iota((32, 128), 1) < 64
    for k in range(8):
        upper = partial[0:32, 128 * k : 128 * k + 128]
        lower = partial[32:64, 128 * k : 128 * k + 128]
        exp_out[2 * k] = jnp.where(left32, upper, pltpu.roll(lower, 64, 1)).astype(BF16)
        exp_out[2 * k + 1] = jnp.where(left32, pltpu.roll(upper, 64, 1), lower).astype(BF16)

    def send_exp(k, _):
        dest = 8 * lax.rem(col + 1 + k // 8, 2) + 2 * ring4((k // 2) & 3, rg) + lax.rem(core + 1 + k, 2)
        rcopy(exp_out.at[dest], exp_in.at[owner16], 6, 16 * half + dest, z)
        return 0

    lax.fori_loop(0, 15, send_exp, 0)
    exp_in[owner16] = exp_out[owner16]
    wait_bytes(exp_in.at[pl.ds(0, 15)], recv_sem.at[6])
    summed = jnp.sum(exp_in[...].astype(F32), axis=0)
    back_out[...] = summed.reshape(4, 8, 128).astype(BF16)

    def send_back(k, _):
        dest = ring8(k, z)
        rcopy(back_out.at[lax.rem(dest, 4)], back_in.at[z], 7, s, dest)
        return 0

    lax.fori_loop(0, group_count - 1, send_back, 0)
    back_in[z] = back_out[lax.rem(z, 4)]
    wait_bytes(back_in.at[pl.ds(0, group_count - 1)], recv_sem.at[7])
    returned = back_in[...].astype(F32).reshape(64, 128).astype(BF16)
    shared = jnp.dot(gates_hi, returned, preferred_element_type=F32) + jnp.dot(
        gates_low, returned, preferred_element_type=F32
    )
    swapped = pltpu.roll(shared, 64, 1)
    left24 = iota((24, 128), 1) < 64
    fin_in[s] = jnp.where(
        z < 4,
        jnp.where(left24, shared[0:24], swapped[24:48]),
        jnp.where(left24, swapped[0:24], shared[24:48]),
    ).astype(BF16)
    to_plane(fin_in.at[s], fin_in.at[s], 8)
    wait_bytes(fin_in.at[pl.ds(0, seq_count - 1)], recv_sem.at[8])

    for k in range(8):
        lanes = slice(128 * k, 128 * k + 128)
        even = fin_in[2 * k].astype(F32) + fin_in[16 + 2 * k].astype(F32)
        odd = fin_in[2 * k + 1].astype(F32) + fin_in[17 + 2 * k].astype(F32)
        upper = jnp.where(left24, even, pltpu.roll(odd, 64, 1))
        lower = jnp.where(left24, pltpu.roll(even, 64, 1), odd)
        out_ref[0:24, lanes] = (x_tok[0:24, lanes] + upper).astype(BF16)
        out_ref[24:48, lanes] = (x_tok[24:48, lanes] + lower).astype(BF16)

    @pl.when(has_query)
    def _():
        wait_bytes(qkv_in.at[pl.ds(0, seq_count - 1)], mix_send.at[0])

    each_owner(lambda copy: copy.wait_send())

    @pl.when(owner & own_rows)
    def _():
        wait_bytes(w_rows.at[pl.ds(0, 2)], send_sem.at[1])

    @pl.when(jnp.logical_not(owner & own_rows))
    def _():
        wait_bytes(w_rows.at[pl.ds(0, 3)], send_sem.at[1])

    @pl.when(owner)
    def _():
        wait_bytes(part_in.at[pl.ds(0, 23)], send_sem.at[2])
        wait_bytes(att_in.at[pl.ds(0, 7)], send_sem.at[3])
        wait_bytes(part_in.at[pl.ds(0, 31), pl.ds(0, 16)], send_sem.at[4])

    @pl.when(jnp.logical_not(owner))
    def _():
        wait_bytes(part_in.at[pl.ds(0, 24)], send_sem.at[2])

    wait_bytes(disp_in.at[0, pl.ds(0, group_count - 1)], send_sem.at[5])
    wait_bytes(disp_in.at[0], send_sem.at[9])
    wait_bytes(exp_in.at[pl.ds(0, 15)], send_sem.at[6])
    wait_bytes(back_in.at[pl.ds(0, group_count - 1)], send_sem.at[7])
    wait_bytes(fin_in.at[pl.ds(0, seq_count - 1)], send_sem.at[8])


def solution(mesh):
    seq_count = mesh.shape["seq"]
    group_count = mesh.shape["exp"]
    vmem = pl.BlockSpec(memory_space=pltpu.VMEM)
    hbm = pl.BlockSpec(memory_space=pltpu.HBM)

    def body(
        tokens,
        attn_gain,
        w_qkv,
        window_cache,
        sink_cache,
        lengths,
        w_out,
        moe_gain,
        router,
        expert_ids,
        slot_order,
        expert_in,
        expert_down,
    ):
        def pin(value):
            return pltpu.with_memory_space_constraint(value, pltpu.HBM)

        out = pl.pallas_call(
            functools.partial(layer_kernel, seq_count, group_count),
            out_shape=jax.ShapeDtypeStruct((48, 1024), BF16),
            in_specs=[hbm] * 13,
            out_specs=vmem,
            scratch_shapes=[
                pltpu.VMEM((12, 4, 1024), BF16),
                pltpu.VMEM((1, 1024), F32),
                pltpu.VMEM((96, 1024), BF16),
                pltpu.VMEM((2, 12, 4, 1024), BF16),
                pltpu.SMEM((12,), jnp.int32),
                pltpu.VMEM((32, 1024), BF16),
                pltpu.VMEM((1, 1024), F32),
                pltpu.VMEM((16, 1024), BF16),
                pltpu.VMEM((4, 2, 12), jnp.int32),
                pltpu.VMEM((1, 48), jnp.int32),
                pltpu.VMEM((2, 12, 128, 1024), BF16),
                pltpu.VMEM((2, 176, 1024), BF16),
                pltpu.VMEM((176, 1024), BF16),
                pltpu.VMEM((48, 1024), F32),
                pltpu.VMEM((48, 128), BF16),
                pltpu.VMEM((32, 48, 128), BF16),
                pltpu.VMEM((8, 48, 128), F32),
                pltpu.VMEM((3, 16, 128), F32),
                pltpu.VMEM((6, 2, 4, 16, 256), BF16),
                pltpu.VMEM((3, 8, 32, 128), BF16),
                pltpu.VMEM((32, 32, 128), BF16),
                pltpu.VMEM((2, 48, 1024), F32),
                pltpu.VMEM((8, 16, 128), BF16),
                pltpu.VMEM((4, 32, 1024), BF16),
                pltpu.VMEM((24, 16, 128), BF16),
                pltpu.VMEM((8, 8, 512), BF16),
                pltpu.VMEM((2, 8, 8, 512), BF16),
                pltpu.VMEM((16, 32, 128), BF16),
                pltpu.VMEM((16, 32, 128), BF16),
                pltpu.VMEM((4, 8, 128), BF16),
                pltpu.VMEM((8, 8, 128), BF16),
                pltpu.VMEM((32, 24, 128), BF16),
                pltpu.SemaphoreType.DMA((7,)),
                pltpu.SemaphoreType.DMA((32,)),
                pltpu.SemaphoreType.DMA((2, 3)),
                pltpu.SemaphoreType.DMA((2,)),
                pltpu.SemaphoreType.DMA((10,)),
                pltpu.SemaphoreType.DMA((10,)),
                pltpu.SemaphoreType.DMA((10,)),
            ],
            compiler_params=pltpu.CompilerParams(
                collective_id=0, has_side_effects=True, vmem_limit_bytes=48 * 1024 * 1024
            ),
            name="layer",
        )(
            pin(tokens),
            pin(attn_gain.reshape(1, -1)),
            pin(w_qkv),
            pin(window_cache),
            pin(sink_cache),
            pin(lengths),
            pin(w_out),
            pin(moe_gain.reshape(1, -1)),
            pin(router.T),
            pin(expert_ids.transpose(1, 2, 0)),
            pin(slot_order),
            pin(expert_in),
            pin(expert_down),
        )
        return out.reshape(tokens.shape)

    in_specs = (
        P("exp", None, None),
        P(),
        P("seq", None),
        P(None, "exp", "seq", None),
        P(None, "exp", None, None),
        P("exp"),
        P("seq", None),
        P(),
        P(),
        P("exp", None, None),
        P("exp", None),
        P(None, "exp", "seq", None),
        P("exp", "seq", None),
    )
    out_specs = P("exp", None, None)
    return jax.shard_map(body, mesh=mesh, in_specs=in_specs, out_specs=out_specs, check_vma=False)
```

```python
import functools

import jax
import jax.numpy as jnp
from jax import lax
from jax.experimental import pallas as pl
from jax.experimental.pallas import tpu as pltpu
from jax.sharding import PartitionSpec as P

HEADS = 16
HD = 64
EXPERTS = 16
SINKS = 4
WIN = 4096
CAP = 8
STEPS = 4
EPSILON = 1e-06
MASKED = -1e30
QUERY_BLOCKS = 11
MESH = pl.DeviceIdType.MESH
F32 = jnp.float32
BF16 = jnp.bfloat16
LAST = (((1,), (1,)), ((), ()))


def iota(shape, axis):
    return lax.broadcasted_iota(jnp.int32, shape, axis)


def wait_bytes(ref, sem):
    pltpu.make_async_copy(ref, ref, sem).wait()


def layer_kernel(
    seq_count,
    group_count,
    tokens_hbm,
    attn_gain_hbm,
    w_qkv_hbm,
    cache_hbm,
    sink_hbm,
    lengths_hbm,
    w_out_hbm,
    moe_gain_hbm,
    router_hbm,
    ids_hbm,
    order_hbm,
    in_hbm,
    down_hbm,
    out_ref,
    tokens_ref,
    attn_gain_ref,
    w_qkv_ref,
    sink_ref,
    lengths_ref,
    w_out_ref,
    moe_gain_ref,
    router_ref,
    ids_ref,
    order_ref,
    kv,
    win,
    down,
    x_tok,
    mix,
    qkv_in,
    near,
    part_out,
    part_in,
    sinks,
    att_in,
    w_rows,
    proj_in,
    disp_out,
    disp_in,
    exp_out,
    exp_in,
    back_out,
    back_in,
    fin_in,
    query_send,
    query_recv,
    mix_send,
    mix_recv,
    kv_sem,
    wt_sem,
    arg_sem,
    send_sem,
    recv_sem,
):
    s = lax.axis_index("seq")
    z = lax.axis_index("exp")
    col = s // 8
    rg = lax.rem(s // 2, 4)
    core = lax.rem(s, 2)
    t = 2 * col + core
    half = s // 16
    owner16 = lax.rem(s, 16)
    owner = rg < 3
    own_rows = core == rg // 2

    def holder(tile, group):
        return 8 * (tile // 2) + 2 * group + lax.rem(tile, 2)

    small = (
        (tokens_hbm, tokens_ref),
        (w_qkv_hbm, w_qkv_ref),
        (attn_gain_hbm, attn_gain_ref),
        (w_out_hbm, w_out_ref),
        (ids_hbm, ids_ref),
        (order_hbm, order_ref),
        (sink_hbm, sink_ref),
        (lengths_hbm, lengths_ref),
        (moe_gain_hbm, moe_gain_ref),
        (router_hbm, router_ref),
    )

    def fetch(at):
        return pltpu.make_async_copy(small[at][0], small[at][1], arg_sem.at[at])

    barrier = pltpu.get_barrier_semaphore()

    def ring4(at, position):
        return lax.rem(position + ((54 >> (2 * at)) & 3), 4)

    def ring8(at, position):
        return lax.rem(position + ((0o7162534 >> (3 * at)) & 7), group_count)

    def plane_peer(k):
        return 8 * ring4(k // 8, col) + 2 * ring4((k // 2) & 3, rg) + lax.rem(core + 1 + k, 2)

    def greet_plane(k, _):
        pl.semaphore_signal(barrier, inc=1, device_id=(plane_peer(k), z), device_id_type=MESH)
        return 0

    def greet_line(k, _):
        pl.semaphore_signal(barrier, inc=1, device_id=(s, ring8(k, z)), device_id_type=MESH)
        return 0

    lax.fori_loop(0, group_count - 1, greet_line, 0)
    lax.fori_loop(0, seq_count - 1, greet_plane, 0)

    for at in range(len(small)):
        fetch(at).start()

    for part in range(3):
        for which in range(2):
            pltpu.make_async_copy(
                cache_hbm.at[which, pl.ds(4 * part, 4)],
                kv.at[which, pl.ds(4 * part, 4)],
                kv_sem.at[which, part],
            ).start()
    pltpu.make_async_copy(in_hbm.at[:, 0], win, wt_sem.at[0]).start()
    pltpu.make_async_copy(down_hbm.at[0], down, wt_sem.at[1]).start()

    def rcopy(src, dst, stage, dest_s, dest_z):
        pltpu.make_async_remote_copy(
            src_ref=src,
            dst_ref=dst,
            send_sem=send_sem.at[stage],
            recv_sem=recv_sem.at[stage],
            device_id=(dest_s, dest_z),
            device_id_type=MESH,
        ).start()

    def to_plane(src, dst, stage):
        def send(k, _):
            rcopy(src, dst, stage, plane_peer(k), z)
            return 0

        lax.fori_loop(0, seq_count - 1, send, 0)

    for at in range(3):
        fetch(at).wait()
    for r in range(12):
        x_tok[4 * r : 4 * r + 4, :] = tokens_ref[r].astype(F32)
    x = x_tok[...]
    inverse = lax.rsqrt(jnp.mean(x * x, axis=-1, keepdims=True) + EPSILON)
    normed = (x * inverse * attn_gain_ref[...]).astype(BF16)
    own_mix = lax.dot_general(normed, w_qkv_ref[...], LAST, preferred_element_type=F32)
    mix[...] = jnp.concatenate([own_mix, jnp.zeros((48, 32), F32)], axis=1).astype(BF16)

    pl.semaphore_wait(barrier, seq_count - 1 + group_count - 1)

    qkv_in[s] = mix[...]

    def send_mix(group, send_to, recv_to, dest):
        rows = pl.ds(pl.multiple_of(16 * group, 16), 16)
        return pltpu.make_async_remote_copy(
            src_ref=mix.at[rows],
            dst_ref=qkv_in.at[s, rows],
            send_sem=send_to,
            recv_sem=recv_to,
            device_id=(dest, z),
            device_id_type=MESH,
        )

    has_query = s < QUERY_BLOCKS
    first_tile = (96 * s) // 128
    last_tile = (96 * s + 95) // 128

    @pl.when(has_query)
    def _():
        def send(k, _):
            group = k // (seq_count - 1)
            peer = plane_peer(k - group * (seq_count - 1))
            send_mix(group, query_send.at[0], query_recv.at[group], peer).start()
            return 0

        lax.fori_loop(0, 3 * (seq_count - 1), send, 0)

    def each_owner(act):
        for group in range(3):
            for at, tile in enumerate((first_tile, last_tile)):
                dest = holder(lax.rem(tile, 8), group)
                go = jnp.logical_not(has_query) & (dest != s)
                if at == 1:
                    go = go & (first_tile != last_tile)
                place = 2 * (tile // 16) + s - (128 * tile) // 96

                @pl.when(go)
                def _():
                    act(
                        send_mix(
                            group, mix_send.at[2 * group + at], mix_recv.at[place], dest
                        )
                    )

    each_owner(lambda copy: copy.start())
    fetch(3).wait()

    w_at = 2 * lax.rem(rg, 2) + core

    @pl.when(owner & own_rows)
    def _():
        w_rows[w_at] = w_out_ref[...]

    for group in range(3):
        w_dest = 8 * col + 2 * group + rg // 2

        @pl.when(w_dest != s)
        def _():
            rcopy(w_out_ref, w_rows.at[w_at], 1, w_dest, z)

    for at in range(4, 10):
        fetch(at).wait()
    eye = iota((48, 48), 0) == iota((48, 48), 1)
    prio_row = order_ref[...]
    prio_col = jnp.sum(jnp.where(eye, prio_row, 0), axis=1, keepdims=True)
    earlier = (prio_row < prio_col).astype(F32).astype(BF16)
    expert_lane = iota((48, EXPERTS), 1)
    id_row_of = iota((48, 12), 0)
    id_lane = iota((48, 12), 1)
    id_cols = []
    onehots = []
    for c in range(2):
        spread_ids = jnp.zeros((48, 12), jnp.int32)
        for step in range(STEPS):
            wanted = (id_row_of // STEPS == id_lane) & (id_row_of % STEPS == step)
            spread_ids = spread_ids + jnp.where(wanted, ids_ref[step, c : c + 1, :], 0)
        id_cols.append(jnp.sum(spread_ids, axis=1, keepdims=True))
        onehots.append((expert_lane == id_cols[c]).astype(F32))
    counts = jnp.dot(earlier, (onehots[0] + onehots[1]).astype(BF16), preferred_element_type=F32)
    sel_rows = iota((64, 48), 0)
    sel_expert = 2 * (sel_rows // CAP) + half
    sel_slot = sel_rows % CAP
    col_ids = iota((48, 64), 1)
    col_expert = 2 * (col_ids // CAP) + half
    col_slot = col_ids % CAP
    dispatch = jnp.zeros((64, 48), F32)
    picks = []
    for c in range(2):
        pos_col = jnp.sum(onehots[c] * counts, axis=1, keepdims=True).astype(jnp.int32)
        id_col = id_cols[c]
        pos_row = jnp.sum(jnp.where(eye, pos_col, 0), axis=0, keepdims=True)
        id_row = jnp.sum(jnp.where(eye, id_col, 0), axis=0, keepdims=True)
        dispatch = dispatch + ((id_row == sel_expert) & (pos_row == sel_slot)).astype(F32)
        picks.append(((id_col == col_expert) & (pos_col == col_slot)).astype(F32))
    dispatch = dispatch.astype(BF16)

    for r in range(12):
        for which in range(2):
            sinks[which, 4 * r : 4 * r + 4, :] = sink_ref[which, r].astype(F32)

    def wait_query(group):
        @pl.when(has_query)
        def _():
            wait_bytes(qkv_in.at[pl.ds(0, QUERY_BLOCKS - 1), pl.ds(0, 16)], query_recv.at[group])

        @pl.when(jnp.logical_not(has_query))
        def _():
            wait_bytes(qkv_in.at[pl.ds(0, QUERY_BLOCKS), pl.ds(0, 16)], query_recv.at[group])

    lane16 = iota((16, 128), 1)

    def query_tiles(rows):
        tiles = []
        for first in range(0, QUERY_BLOCKS, 4):
            last = min(first + 3, QUERY_BLOCKS - 1)
            b0, b1, b2, b3 = (
                qkv_in[b, rows, :].astype(F32) for b in (first, first + 1, first + 2, last)
            )
            r1 = pltpu.roll(b1, 96, 1)
            r2 = pltpu.roll(b2, 64, 1)
            r3 = pltpu.roll(b3, 32, 1)
            tiles.append(jnp.where(lane16 < 96, b0, r1))
            tiles.append(jnp.where(lane16 < 64, r1, r2))
            tiles.append(jnp.where(lane16 < 32, r2, r3))
        return tiles[0:8]

    sub2 = iota((2, 8, 128), 1)
    lane2 = iota((2, 8, 128), 2)
    diag2 = (sub2 < 4) == (lane2 < 64)
    zero = jnp.zeros((8, 128), F32)

    def spread_queries(tiles):
        parts = []
        for tile in tiles:
            v = tile.reshape(2, 8, 128)
            w = pltpu.roll(v, 4, 1)
            even = jnp.where(diag2, jnp.where(sub2 < 4, v, w), 0.0)
            odd = jnp.where(diag2, jnp.where(sub2 < 4, w, v), 0.0)
            parts.append((even, odd))
        spread = []
        for pair in range(2):
            for parity in range(2):
                row = []
                for u in range(4):
                    upper = jnp.concatenate([parts[2 * u][parity][pair], zero], axis=1)
                    lower = jnp.concatenate([zero, parts[2 * u + 1][parity][pair]], axis=1)
                    row.append(jnp.concatenate([upper, lower], axis=0).astype(BF16))
                spread.append(row)
        return spread

    sub8 = iota((8, 8, 128), 1)
    lane8 = iota((8, 8, 128), 2)
    lane_in = lane8 % 64
    step_id = iota((8, 128), 0) % STEPS
    slot_id = s * 128 + iota((8, 128), 1)

    def merge(a, b):
        ar = pltpu.roll(a, 4, 1)
        br = pltpu.roll(b, 4, 1)
        return jnp.where(
            sub8 < 4, jnp.where(lane8 < 64, a, ar), jnp.where(lane8 < 64, br, b)
        )

    def cache_part(which, group):
        at = pl.ds(4 * group, 4)
        return pltpu.make_async_copy(
            cache_hbm.at[which, at], kv.at[which, at], kv_sem.at[which, group]
        )

    def attend_rows(group, _):
        cache_part(0, group).wait()
        cache_part(1, group).wait()
        wait_query(group)
        queries = spread_queries(query_tiles(pl.ds(pl.multiple_of(16 * group, 16), 16)))
        scores = []
        for k in range(4):
            for u in range(4):
                scores.append(
                    lax.dot_general(
                        queries[k][u],
                        kv[0, 4 * group + k, :, 256 * u : 256 * u + 256],
                        LAST,
                        preferred_element_type=F32,
                    )
                )
        score = jnp.concatenate(scores, axis=0).reshape(4, 8, 8, 128) * (HD ** (-0.5))
        lives = []
        for k in range(4):
            held = lengths_ref[4 * group + k] - SINKS
            age = (slot_id - held) & (WIN - 1)
            lives.append(((slot_id < jnp.minimum(WIN, held)) & (age > step_id)).astype(F32))
        live = jnp.concatenate(lives, axis=0).reshape(4, 1, 8, 128) > 0.0
        peak = jnp.max(jnp.where(live, score, MASKED), axis=-1, keepdims=True)
        weight = jnp.where(live, jnp.exp(score - peak), 0.0)
        total = jnp.sum(weight, axis=-1, keepdims=True)
        rounded = weight.reshape(256, 128).astype(BF16)
        values = []
        for k in range(4):
            found = []
            for u in range(4):
                at = 64 * k + 16 * u
                mixed = jnp.dot(
                    rounded[at : at + 16],
                    kv[1, 4 * group + k, :, 256 * u : 256 * u + 256],
                    preferred_element_type=F32,
                )
                found.append(mixed[0:8, 0:128])
                found.append(mixed[8:16, 128:256])
            values.append(jnp.concatenate(found, axis=0).reshape(8, 8, 128))
        peak = jnp.broadcast_to(peak, (4, 8, 8, 128))
        total = jnp.broadcast_to(total, (4, 8, 8, 128))
        p_hi = peak.astype(BF16).astype(F32)
        p_mid = (peak - p_hi).astype(BF16).astype(F32)
        p_low = peak - p_hi - p_mid
        t_hi = total.astype(BF16).astype(F32)
        t_low = total - t_hi
        lane_at = lane_in[None]
        stat = jnp.where(
            lane_at == 0,
            p_hi,
            jnp.where(
                lane_at == 1,
                p_mid,
                jnp.where(
                    lane_at == 2,
                    p_low,
                    jnp.where(lane_at == 3, t_hi, jnp.where(lane_at == 4, t_low, 0.0)),
                ),
            ),
        )
        part_out[group, :, 0:16, :] = jnp.concatenate(
            [merge(values[0], values[1]), merge(values[2], values[3])], axis=1
        ).astype(BF16)
        part_out[group, :, 16:32, :] = jnp.concatenate(
            [merge(stat[0], stat[1]), merge(stat[2], stat[3])], axis=1
        ).astype(BF16)

        def send(k, _):
            tile = 2 * ring4(k // 2, col) + lax.rem(core + k, 2)
            dest = holder(tile, group)

            @pl.when(dest != s)
            def _():
                rcopy(part_out.at[group, tile], part_in.at[s], 2, dest, z)

            return 0

        lax.fori_loop(0, 8, send, 0)
        return 0

    lax.fori_loop(0, 3, attend_rows, 0)

    @pl.when(owner & own_rows)
    def _():
        wait_bytes(w_rows.at[pl.ds(0, 3)], recv_sem.at[1])

    @pl.when(owner & jnp.logical_not(own_rows))
    def _():
        wait_bytes(w_rows, recv_sem.at[1])

    @pl.when(owner)
    def _():
        part_in[s] = part_out[rg, t]
        rows = pl.ds(pl.multiple_of(16 * rg, 16), 16)
        lanes = pl.ds(pl.multiple_of(128 * t, 128), 128)

        def own_tile(tile):
            block = (128 * tile) // 96
            offset = 128 * tile - 96 * block
            for k in range(2):

                @pl.when((block + k >= QUERY_BLOCKS) & (block + k != s))
                def _():
                    wait_bytes(mix.at[pl.ds(0, 16)], mix_recv.at[2 * (tile // 16) + k])

            low = pltpu.roll(qkv_in[block, rows, :].astype(F32), 128 - offset, 1)
            high = pltpu.roll(qkv_in[block + 1, rows, :].astype(F32), 96 - offset, 1)
            return jnp.where(lane16 < 96 - offset, low, high)

        q_own = own_tile(t)
        k_own = own_tile(8 + t).astype(BF16)
        v_own = own_tile(16 + t).astype(BF16)
        k_sink = sinks[0, rows, lanes].astype(BF16)
        v_sink = sinks[1, rows, lanes].astype(BF16)
        rep_row = iota((64, 16), 0)
        rep_col = iota((64, 16), 1)
        repeat = (
            ((rep_row % 16) // 4 == rep_col // 4) & (rep_row // 16 == rep_col % 4)
        ).astype(F32).astype(BF16)
        keys = jnp.concatenate(
            [
                jnp.dot(repeat, k_sink, preferred_element_type=F32),
                jnp.dot(repeat, k_own, preferred_element_type=F32),
            ],
            axis=0,
        ).reshape(8, 16, 128)
        vals = jnp.concatenate(
            [
                jnp.dot(repeat, v_sink, preferred_element_type=F32),
                jnp.dot(repeat, v_own, preferred_element_type=F32),
            ],
            axis=0,
        ).reshape(8, 16, 128)
        prod = (q_own[None] * keys).reshape(128, 128)
        prod_hi = prod.astype(BF16)
        prod_low = (prod - prod_hi.astype(F32)).astype(BF16)
        same_half = (
            (iota((128, 128), 0) < 64) == (iota((128, 128), 1) < 64)
        ).astype(F32).astype(BF16)
        score = (
            jnp.dot(prod_hi, same_half, preferred_element_type=F32)
            + jnp.dot(prod_low, same_half, preferred_element_type=F32)
        ).reshape(8, 16, 128) * (HD ** (-0.5))
        key_id = iota((8, 16, 128), 0)
        row_step = iota((8, 16, 128), 1) % STEPS
        live = (key_id < SINKS) | (key_id - SINKS <= row_step)
        near_peak = jnp.max(jnp.where(live, score, MASKED), axis=0)
        weight = jnp.where(live, jnp.exp(score - near_peak[None]), 0.0)
        near_total = jnp.sum(weight, axis=0)
        near_value = jnp.sum(weight.astype(BF16).astype(F32) * vals, axis=0)

        near[0] = near_peak
        near[1] = near_total
        near[2] = near_value
        wait_bytes(part_in.at[pl.ds(0, seq_count - 1)], recv_sem.at[2])


    @pl.when(owner)
    def _():
        near_peak, near_total, near_value = near[0], near[1], near[2]
        spread_row = iota((128, 256), 0)
        spread_col = iota((128, 256), 1)
        kk = spread_row % 64
        wanted = jnp.where(spread_col < 128, (kk < 3).astype(F32), ((kk == 3) | (kk == 4)).astype(F32))
        spread = jnp.where(
            (spread_row < 64) == (spread_col % 128 < 64), wanted, 0.0
        ).astype(BF16)
        stats = jnp.dot(
            part_in[:, 16:32, :].reshape(seq_count * 16, 128), spread, preferred_element_type=F32
        ).reshape(seq_count, 16, 256)
        peaks = stats[:, :, 0:128]
        totals = stats[:, :, 128:256]
        overall = jnp.maximum(jnp.max(peaks, axis=0), near_peak)
        factor = jnp.exp(peaks - overall[None])
        near_factor = jnp.exp(near_peak - overall)
        total = jnp.sum(factor * totals, axis=0) + near_factor * near_total
        value = (
            jnp.sum(factor * part_in[:, 0:16, :].astype(F32), axis=0) + near_factor * near_value
        )
        att_in[t] = (value / total).astype(BF16)

        def send_att(k, _):
            tile = 2 * ring4(k // 2, col) + lax.rem(core + 1 + k, 2)
            rcopy(att_in.at[t], att_in.at[t], 3, holder(tile, rg), z)
            return 0

        lax.fori_loop(0, 7, send_att, 0)
        wait_bytes(att_in.at[pl.ds(0, 7)], recv_sem.at[3])


    @pl.when(owner)
    def _():
        attended = jnp.concatenate([att_in[k] for k in range(8)], axis=1)
        weights = w_rows[...].reshape(128, 1024)
        proj_in[8 * rg + t] = lax.dot_general(
            attended, weights, LAST, preferred_element_type=F32
        ).astype(BF16)
        to_plane(proj_in.at[8 * rg + t], proj_in.at[8 * rg + t], 4)
        wait_bytes(proj_in.at[pl.ds(0, 23)], recv_sem.at[4])

    @pl.when(rg == 3)
    def _():
        wait_bytes(proj_in, recv_sem.at[4])


    projected = jnp.concatenate(
        [
            jnp.concatenate([proj_in[8 * g + k] for k in range(8)], axis=1)
            for g in range(3)
        ],
        axis=0,
    )
    residual = x_tok[...] + projected.astype(F32)
    x_tok[...] = residual
    inverse = lax.rsqrt(jnp.mean(residual * residual, axis=-1, keepdims=True) + EPSILON)
    normed = (residual * inverse * moe_gain_ref[...]).astype(BF16)
    own_half = jnp.where(core == 0, normed[:, 0:512], normed[:, 512:1024])
    buffer = jnp.dot(dispatch, own_half, preferred_element_type=F32)
    disp_out[...] = buffer.reshape(8, 8, 512).astype(BF16)

    def send_rows(k, _):
        dest = ring8(k, z)
        rcopy(disp_out.at[dest], disp_in.at[core, z], 5, s, dest)
        return 0

    lax.fori_loop(0, group_count - 1, send_rows, 0)
    disp_in[core, z] = disp_out[z]

    logits = lax.dot_general(normed, router_ref[...], LAST, preferred_element_type=F32)
    gates = jnp.zeros((48, 64), F32)
    for c in range(2):
        logit = jnp.sum(onehots[c] * logits, axis=1, keepdims=True)
        gates = gates + picks[c] * jax.nn.sigmoid(logit)
    gates_hi = gates.astype(BF16)
    gates_low = (gates - gates_hi.astype(F32)).astype(BF16)

    pltpu.make_async_copy(in_hbm.at[:, 0], win, wt_sem.at[0]).wait()
    pltpu.make_async_copy(down_hbm.at[0], down, wt_sem.at[1]).wait()
    wait_bytes(disp_in.at[0, pl.ds(0, group_count - 1)], recv_sem.at[5])
    rcopy(disp_in.at[core], disp_in.at[core], 9, s + 1 - 2 * core, z)
    wait_bytes(disp_in.at[0], recv_sem.at[9])
    rows_in = jnp.concatenate(
        [disp_in[c].astype(F32).reshape(64, 512).astype(BF16) for c in range(2)], axis=1
    )
    gate_part = lax.dot_general(rows_in, win[0], LAST, preferred_element_type=F32)
    up_part = lax.dot_general(rows_in, win[1], LAST, preferred_element_type=F32)
    hidden = (jax.nn.gelu(gate_part, approximate=True) * up_part).astype(BF16)
    partial = jnp.dot(hidden, down[...], preferred_element_type=F32)
    left32 = iota((32, 128), 1) < 64
    for k in range(8):
        upper = partial[0:32, 128 * k : 128 * k + 128]
        lower = partial[32:64, 128 * k : 128 * k + 128]
        exp_out[2 * k] = jnp.where(left32, upper, pltpu.roll(lower, 64, 1)).astype(BF16)
        exp_out[2 * k + 1] = jnp.where(left32, pltpu.roll(upper, 64, 1), lower).astype(BF16)

    def send_exp(k, _):
        dest = 8 * lax.rem(col + 1 + k // 8, 2) + 2 * ring4((k // 2) & 3, rg) + lax.rem(core + 1 + k, 2)
        rcopy(exp_out.at[dest], exp_in.at[owner16], 6, 16 * half + dest, z)
        return 0

    lax.fori_loop(0, 15, send_exp, 0)
    exp_in[owner16] = exp_out[owner16]
    wait_bytes(exp_in.at[pl.ds(0, 15)], recv_sem.at[6])
    summed = jnp.sum(exp_in[...].astype(F32), axis=0)
    back_out[...] = summed.reshape(4, 8, 128).astype(BF16)

    def send_back(k, _):
        dest = ring8(k, z)
        rcopy(back_out.at[lax.rem(dest, 4)], back_in.at[z], 7, s, dest)
        return 0

    lax.fori_loop(0, group_count - 1, send_back, 0)
    back_in[z] = back_out[lax.rem(z, 4)]
    wait_bytes(back_in.at[pl.ds(0, group_count - 1)], recv_sem.at[7])
    returned = back_in[...].astype(F32).reshape(64, 128).astype(BF16)
    shared = jnp.dot(gates_hi, returned, preferred_element_type=F32) + jnp.dot(
        gates_low, returned, preferred_element_type=F32
    )
    swapped = pltpu.roll(shared, 64, 1)
    left24 = iota((24, 128), 1) < 64
    fin_in[s] = jnp.where(
        z < 4,
        jnp.where(left24, shared[0:24], swapped[24:48]),
        jnp.where(left24, swapped[0:24], shared[24:48]),
    ).astype(BF16)
    to_plane(fin_in.at[s], fin_in.at[s], 8)
    wait_bytes(fin_in.at[pl.ds(0, seq_count - 1)], recv_sem.at[8])

    for k in range(8):
        lanes = slice(128 * k, 128 * k + 128)
        even = fin_in[2 * k].astype(F32) + fin_in[16 + 2 * k].astype(F32)
        odd = fin_in[2 * k + 1].astype(F32) + fin_in[17 + 2 * k].astype(F32)
        upper = jnp.where(left24, even, pltpu.roll(odd, 64, 1))
        lower = jnp.where(left24, pltpu.roll(even, 64, 1), odd)
        out_ref[0:24, lanes] = (x_tok[0:24, lanes] + upper).astype(BF16)
        out_ref[24:48, lanes] = (x_tok[24:48, lanes] + lower).astype(BF16)

    @pl.when(has_query)
    def _():
        wait_bytes(qkv_in.at[pl.ds(0, seq_count - 1)], query_send.at[0])

    each_owner(lambda copy: copy.wait_send())

    @pl.when(owner & own_rows)
    def _():
        wait_bytes(w_rows.at[pl.ds(0, 2)], send_sem.at[1])

    @pl.when(jnp.logical_not(owner & own_rows))
    def _():
        wait_bytes(w_rows.at[pl.ds(0, 3)], send_sem.at[1])

    @pl.when(owner)
    def _():
        wait_bytes(part_in.at[pl.ds(0, 23)], send_sem.at[2])
        wait_bytes(att_in.at[pl.ds(0, 7)], send_sem.at[3])
        wait_bytes(part_in.at[pl.ds(0, 31), pl.ds(0, 16)], send_sem.at[4])

    @pl.when(jnp.logical_not(owner))
    def _():
        wait_bytes(part_in.at[pl.ds(0, 24)], send_sem.at[2])

    wait_bytes(disp_in.at[0, pl.ds(0, group_count - 1)], send_sem.at[5])
    wait_bytes(disp_in.at[0], send_sem.at[9])
    wait_bytes(exp_in.at[pl.ds(0, 15)], send_sem.at[6])
    wait_bytes(back_in.at[pl.ds(0, group_count - 1)], send_sem.at[7])
    wait_bytes(fin_in.at[pl.ds(0, seq_count - 1)], send_sem.at[8])


def solution(mesh):
    seq_count = mesh.shape["seq"]
    group_count = mesh.shape["exp"]
    vmem = pl.BlockSpec(memory_space=pltpu.VMEM)
    hbm = pl.BlockSpec(memory_space=pltpu.HBM)

    def body(
        tokens,
        attn_gain,
        w_qkv,
        window_cache,
        sink_cache,
        lengths,
        w_out,
        moe_gain,
        router,
        expert_ids,
        slot_order,
        expert_in,
        expert_down,
    ):
        def pin(value):
            return pltpu.with_memory_space_constraint(value, pltpu.HBM)

        out = pl.pallas_call(
            functools.partial(layer_kernel, seq_count, group_count),
            out_shape=jax.ShapeDtypeStruct((48, 1024), BF16),
            in_specs=[hbm] * 13,
            out_specs=vmem,
            scratch_shapes=[
                pltpu.VMEM((12, 4, 1024), BF16),
                pltpu.VMEM((1, 1024), F32),
                pltpu.VMEM((96, 1024), BF16),
                pltpu.VMEM((2, 12, 4, 1024), BF16),
                pltpu.SMEM((12,), jnp.int32),
                pltpu.VMEM((32, 1024), BF16),
                pltpu.VMEM((1, 1024), F32),
                pltpu.VMEM((16, 1024), BF16),
                pltpu.VMEM((4, 2, 12), jnp.int32),
                pltpu.VMEM((1, 48), jnp.int32),
                pltpu.VMEM((2, 12, 128, 1024), BF16),
                pltpu.VMEM((2, 176, 1024), BF16),
                pltpu.VMEM((176, 1024), BF16),
                pltpu.VMEM((48, 1024), F32),
                pltpu.VMEM((48, 128), BF16),
                pltpu.VMEM((32, 48, 128), BF16),
                pltpu.VMEM((3, 16, 128), F32),
                pltpu.VMEM((3, 8, 32, 128), BF16),
                pltpu.VMEM((32, 32, 128), BF16),
                pltpu.VMEM((2, 48, 1024), F32),
                pltpu.VMEM((8, 16, 128), BF16),
                pltpu.VMEM((4, 32, 1024), BF16),
                pltpu.VMEM((24, 16, 128), BF16),
                pltpu.VMEM((8, 8, 512), BF16),
                pltpu.VMEM((2, 8, 8, 512), BF16),
                pltpu.VMEM((16, 32, 128), BF16),
                pltpu.VMEM((16, 32, 128), BF16),
                pltpu.VMEM((4, 8, 128), BF16),
                pltpu.VMEM((8, 8, 128), BF16),
                pltpu.VMEM((32, 24, 128), BF16),
                pltpu.SemaphoreType.DMA((1,)),
                pltpu.SemaphoreType.DMA((3,)),
                pltpu.SemaphoreType.DMA((6,)),
                pltpu.SemaphoreType.DMA((4,)),
                pltpu.SemaphoreType.DMA((2, 3)),
                pltpu.SemaphoreType.DMA((2,)),
                pltpu.SemaphoreType.DMA((10,)),
                pltpu.SemaphoreType.DMA((10,)),
                pltpu.SemaphoreType.DMA((10,)),
            ],
            compiler_params=pltpu.CompilerParams(
                collective_id=0, has_side_effects=True, vmem_limit_bytes=48 * 1024 * 1024
            ),
            name="layer",
        )(
            pin(tokens),
            pin(attn_gain.reshape(1, -1)),
            pin(w_qkv),
            pin(window_cache),
            pin(sink_cache),
            pin(lengths),
            pin(w_out),
            pin(moe_gain.reshape(1, -1)),
            pin(router.T),
            pin(expert_ids.transpose(1, 2, 0)),
            pin(slot_order),
            pin(expert_in),
            pin(expert_down),
        )
        return out.reshape(tokens.shape)

    in_specs = (
        P("exp", None, None),
        P(),
        P("seq", None),
        P(None, "exp", "seq", None),
        P(None, "exp", None, None),
        P("exp"),
        P("seq", None),
        P(),
        P(),
        P("exp", None, None),
        P("exp", None),
        P(None, "exp", "seq", None),
        P("exp", "seq", None),
    )
    out_specs = P("exp", None, None)
    return jax.shard_map(body, mesh=mesh, in_specs=in_specs, out_specs=out_specs, check_vma=False)
```

```python
import functools

import jax
import jax.numpy as jnp
from jax import lax
from jax.experimental import pallas as pl
from jax.experimental.pallas import tpu as pltpu
from jax.sharding import PartitionSpec as P

HEADS = 16
HD = 64
EXPERTS = 16
SINKS = 4
WIN = 4096
CAP = 8
STEPS = 4
EPSILON = 1e-06
MASKED = -1e30
QUERY_BLOCKS = 11
MESH = pl.DeviceIdType.MESH
F32 = jnp.float32
BF16 = jnp.bfloat16
LAST = (((1,), (1,)), ((), ()))


def iota(shape, axis):
    return lax.broadcasted_iota(jnp.int32, shape, axis)


def wait_bytes(ref, sem):
    pltpu.make_async_copy(ref, ref, sem).wait()


def layer_kernel(
    seq_count,
    group_count,
    tokens_hbm,
    attn_gain_hbm,
    w_qkv_hbm,
    cache_hbm,
    sink_hbm,
    lengths_hbm,
    w_out_hbm,
    moe_gain_hbm,
    router_hbm,
    ids_hbm,
    order_hbm,
    in_hbm,
    down_hbm,
    out_ref,
    tokens_ref,
    attn_gain_ref,
    w_qkv_ref,
    sink_ref,
    lengths_ref,
    w_out_ref,
    moe_gain_ref,
    router_ref,
    ids_ref,
    order_ref,
    kv,
    win,
    down,
    x_tok,
    mix,
    qkv_in,
    near,
    part_out,
    part_in,
    sinks,
    att_in,
    w_rows,
    proj_in,
    disp_out,
    disp_in,
    exp_out,
    exp_in,
    back_out,
    back_in,
    fin_in,
    query_send,
    query_recv,
    mix_send,
    mix_recv,
    kv_sem,
    wt_sem,
    arg_sem,
    send_sem,
    recv_sem,
):
    s = lax.axis_index("seq")
    z = lax.axis_index("exp")
    col = s // 8
    rg = lax.rem(s // 2, 4)
    core = lax.rem(s, 2)
    t = 2 * col + core
    half = s // 16
    owner16 = lax.rem(s, 16)
    owner = rg < 3
    own_rows = core == rg // 2

    def holder(tile, group):
        return 8 * (tile // 2) + 2 * group + lax.rem(tile, 2)

    small = (
        (tokens_hbm, tokens_ref),
        (w_qkv_hbm, w_qkv_ref),
        (attn_gain_hbm, attn_gain_ref),
        (w_out_hbm, w_out_ref),
        (ids_hbm, ids_ref),
        (order_hbm, order_ref),
        (sink_hbm, sink_ref),
        (lengths_hbm, lengths_ref),
        (moe_gain_hbm, moe_gain_ref),
        (router_hbm, router_ref),
    )

    def fetch(at):
        return pltpu.make_async_copy(small[at][0], small[at][1], arg_sem.at[at])

    barrier = pltpu.get_barrier_semaphore()

    def ring4(at, position):
        return lax.rem(position + ((54 >> (2 * at)) & 3), 4)

    def ring8(at, position):
        return lax.rem(position + ((0o7162534 >> (3 * at)) & 7), group_count)

    def plane_peer(k):
        return 8 * ring4(k // 8, col) + 2 * ring4((k // 2) & 3, rg) + lax.rem(core + 1 + k, 2)

    def greet_plane(k, _):
        pl.semaphore_signal(barrier, inc=1, device_id=(plane_peer(k), z), device_id_type=MESH)
        return 0

    def greet_line(k, _):
        pl.semaphore_signal(barrier, inc=1, device_id=(s, ring8(k, z)), device_id_type=MESH)
        return 0

    lax.fori_loop(0, group_count - 1, greet_line, 0)
    lax.fori_loop(0, seq_count - 1, greet_plane, 0)

    for at in range(len(small)):
        fetch(at).start()

    for part in range(3):
        for which in range(2):
            pltpu.make_async_copy(
                cache_hbm.at[which, pl.ds(4 * part, 4)],
                kv.at[which, pl.ds(4 * part, 4)],
                kv_sem.at[which, part],
            ).start()
    pltpu.make_async_copy(in_hbm.at[:, 0], win, wt_sem.at[0]).start()
    pltpu.make_async_copy(down_hbm.at[0], down, wt_sem.at[1]).start()

    def rcopy(src, dst, stage, dest_s, dest_z):
        pltpu.make_async_remote_copy(
            src_ref=src,
            dst_ref=dst,
            send_sem=send_sem.at[stage],
            recv_sem=recv_sem.at[stage],
            device_id=(dest_s, dest_z),
            device_id_type=MESH,
        ).start()

    def to_plane(src, dst, stage):
        def send(k, _):
            rcopy(src, dst, stage, plane_peer(k), z)
            return 0

        lax.fori_loop(0, seq_count - 1, send, 0)

    for at in range(3):
        fetch(at).wait()
    for r in range(12):
        x_tok[4 * r : 4 * r + 4, :] = tokens_ref[r].astype(F32)
    x = x_tok[...]
    inverse = lax.rsqrt(jnp.mean(x * x, axis=-1, keepdims=True) + EPSILON)
    normed = (x * inverse * attn_gain_ref[...]).astype(BF16)
    own_mix = lax.dot_general(normed, w_qkv_ref[...], LAST, preferred_element_type=F32)
    mix[...] = jnp.concatenate([own_mix, jnp.zeros((48, 32), F32)], axis=1).astype(BF16)

    pl.semaphore_wait(barrier, seq_count - 1 + group_count - 1)

    qkv_in[s] = mix[...]

    def send_mix(group, send_to, recv_to, dest):
        rows = pl.ds(pl.multiple_of(16 * group, 16), 16)
        return pltpu.make_async_remote_copy(
            src_ref=mix.at[rows],
            dst_ref=qkv_in.at[s, rows],
            send_sem=send_to,
            recv_sem=recv_to,
            device_id=(dest, z),
            device_id_type=MESH,
        )

    has_query = s < QUERY_BLOCKS
    first_tile = (96 * s) // 128
    last_tile = (96 * s + 95) // 128

    @pl.when(has_query)
    def _():
        def send(k, _):
            group = k // (seq_count - 1)
            peer = plane_peer(k - group * (seq_count - 1))
            send_mix(group, query_send.at[0], query_recv.at[group], peer).start()
            return 0

        lax.fori_loop(0, 3 * (seq_count - 1), send, 0)

    def each_owner(act):
        for group in range(3):
            for at, tile in enumerate((first_tile, last_tile)):
                dest = holder(lax.rem(tile, 8), group)
                go = jnp.logical_not(has_query) & (dest != s)
                if at == 1:
                    go = go & (first_tile != last_tile)
                place = 2 * (tile // 16) + s - (128 * tile) // 96

                @pl.when(go)
                def _():
                    act(
                        send_mix(
                            group, mix_send.at[2 * group + at], mix_recv.at[place], dest
                        )
                    )

    each_owner(lambda copy: copy.start())
    fetch(3).wait()

    w_at = 2 * lax.rem(rg, 2) + core

    @pl.when(own_rows)
    def _():
        w_rows[w_at] = w_out_ref[...]

    for row in range(4):
        w_dest = 8 * col + 2 * row + rg // 2

        @pl.when(w_dest != s)
        def _():
            rcopy(w_out_ref, w_rows.at[w_at], 1, w_dest, z)

    for at in range(4, 10):
        fetch(at).wait()
    eye = iota((48, 48), 0) == iota((48, 48), 1)
    prio_row = order_ref[...]
    prio_col = jnp.sum(jnp.where(eye, prio_row, 0), axis=1, keepdims=True)
    earlier = (prio_row < prio_col).astype(F32).astype(BF16)
    expert_lane = iota((48, EXPERTS), 1)
    id_row_of = iota((48, 12), 0)
    id_lane = iota((48, 12), 1)
    id_cols = []
    onehots = []
    for c in range(2):
        spread_ids = jnp.zeros((48, 12), jnp.int32)
        for step in range(STEPS):
            wanted = (id_row_of // STEPS == id_lane) & (id_row_of % STEPS == step)
            spread_ids = spread_ids + jnp.where(wanted, ids_ref[step, c : c + 1, :], 0)
        id_cols.append(jnp.sum(spread_ids, axis=1, keepdims=True))
        onehots.append((expert_lane == id_cols[c]).astype(F32))
    counts = jnp.dot(earlier, (onehots[0] + onehots[1]).astype(BF16), preferred_element_type=F32)
    sel_rows = iota((128, 48), 0)
    sel_expert = 2 * ((sel_rows // CAP) % 8) + sel_rows // 64
    sel_slot = sel_rows % CAP
    col_ids = iota((48, 64), 1)
    col_expert = 2 * (col_ids // CAP) + half
    col_slot = col_ids % CAP
    dispatch = jnp.zeros((128, 48), F32)
    picks = []
    for c in range(2):
        pos_col = jnp.sum(onehots[c] * counts, axis=1, keepdims=True).astype(jnp.int32)
        id_col = id_cols[c]
        pos_row = jnp.sum(jnp.where(eye, pos_col, 0), axis=0, keepdims=True)
        id_row = jnp.sum(jnp.where(eye, id_col, 0), axis=0, keepdims=True)
        dispatch = dispatch + ((id_row == sel_expert) & (pos_row == sel_slot)).astype(F32)
        picks.append(((id_col == col_expert) & (pos_col == col_slot)).astype(F32))
    dispatch = dispatch.astype(BF16)

    for r in range(12):
        for which in range(2):
            sinks[which, 4 * r : 4 * r + 4, :] = sink_ref[which, r].astype(F32)

    def wait_query(group):
        @pl.when(has_query)
        def _():
            wait_bytes(qkv_in.at[pl.ds(0, QUERY_BLOCKS - 1), pl.ds(0, 16)], query_recv.at[group])

        @pl.when(jnp.logical_not(has_query))
        def _():
            wait_bytes(qkv_in.at[pl.ds(0, QUERY_BLOCKS), pl.ds(0, 16)], query_recv.at[group])

    lane16 = iota((16, 128), 1)

    def query_tiles(rows):
        tiles = []
        for first in range(0, QUERY_BLOCKS, 4):
            last = min(first + 3, QUERY_BLOCKS - 1)
            b0, b1, b2, b3 = (
                qkv_in[b, rows, :].astype(F32) for b in (first, first + 1, first + 2, last)
            )
            r1 = pltpu.roll(b1, 96, 1)
            r2 = pltpu.roll(b2, 64, 1)
            r3 = pltpu.roll(b3, 32, 1)
            tiles.append(jnp.where(lane16 < 96, b0, r1))
            tiles.append(jnp.where(lane16 < 64, r1, r2))
            tiles.append(jnp.where(lane16 < 32, r2, r3))
        return tiles[0:8]

    sub2 = iota((2, 8, 128), 1)
    lane2 = iota((2, 8, 128), 2)
    diag2 = (sub2 < 4) == (lane2 < 64)
    zero = jnp.zeros((8, 128), F32)

    def spread_queries(tiles):
        parts = []
        for tile in tiles:
            v = tile.reshape(2, 8, 128)
            w = pltpu.roll(v, 4, 1)
            even = jnp.where(diag2, jnp.where(sub2 < 4, v, w), 0.0)
            odd = jnp.where(diag2, jnp.where(sub2 < 4, w, v), 0.0)
            parts.append((even, odd))
        spread = []
        for pair in range(2):
            for parity in range(2):
                row = []
                for u in range(4):
                    upper = jnp.concatenate([parts[2 * u][parity][pair], zero], axis=1)
                    lower = jnp.concatenate([zero, parts[2 * u + 1][parity][pair]], axis=1)
                    row.append(jnp.concatenate([upper, lower], axis=0).astype(BF16))
                spread.append(row)
        return spread

    sub8 = iota((8, 8, 128), 1)
    lane8 = iota((8, 8, 128), 2)
    lane_in = lane8 % 64
    step_id = iota((8, 128), 0) % STEPS
    slot_id = s * 128 + iota((8, 128), 1)

    def merge(a, b):
        ar = pltpu.roll(a, 4, 1)
        br = pltpu.roll(b, 4, 1)
        return jnp.where(
            sub8 < 4, jnp.where(lane8 < 64, a, ar), jnp.where(lane8 < 64, br, b)
        )

    def cache_part(which, group):
        at = pl.ds(4 * group, 4)
        return pltpu.make_async_copy(
            cache_hbm.at[which, at], kv.at[which, at], kv_sem.at[which, group]
        )

    def attend_rows(group, _):
        cache_part(0, group).wait()
        cache_part(1, group).wait()
        wait_query(group)
        queries = spread_queries(query_tiles(pl.ds(pl.multiple_of(16 * group, 16), 16)))
        scores = []
        for k in range(4):
            for u in range(4):
                scores.append(
                    lax.dot_general(
                        queries[k][u],
                        kv[0, 4 * group + k, :, 256 * u : 256 * u + 256],
                        LAST,
                        preferred_element_type=F32,
                    )
                )
        score = jnp.concatenate(scores, axis=0).reshape(4, 8, 8, 128) * (HD ** (-0.5))
        lives = []
        for k in range(4):
            held = lengths_ref[4 * group + k] - SINKS
            age = (slot_id - held) & (WIN - 1)
            lives.append(((slot_id < jnp.minimum(WIN, held)) & (age > step_id)).astype(F32))
        live = jnp.concatenate(lives, axis=0).reshape(4, 1, 8, 128) > 0.0
        peak = jnp.max(jnp.where(live, score, MASKED), axis=-1, keepdims=True)
        weight = jnp.where(live, jnp.exp(score - peak), 0.0)
        total = jnp.sum(weight, axis=-1, keepdims=True)
        rounded = weight.reshape(256, 128).astype(BF16)
        values = []
        for k in range(4):
            found = []
            for u in range(4):
                at = 64 * k + 16 * u
                mixed = jnp.dot(
                    rounded[at : at + 16],
                    kv[1, 4 * group + k, :, 256 * u : 256 * u + 256],
                    preferred_element_type=F32,
                )
                found.append(mixed[0:8, 0:128])
                found.append(mixed[8:16, 128:256])
            values.append(jnp.concatenate(found, axis=0).reshape(8, 8, 128))
        peak = jnp.broadcast_to(peak, (4, 8, 8, 128))
        total = jnp.broadcast_to(total, (4, 8, 8, 128))
        p_hi = peak.astype(BF16).astype(F32)
        p_mid = (peak - p_hi).astype(BF16).astype(F32)
        p_low = peak - p_hi - p_mid
        t_hi = total.astype(BF16).astype(F32)
        t_low = total - t_hi
        lane_at = lane_in[None]
        stat = jnp.where(
            lane_at == 0,
            p_hi,
            jnp.where(
                lane_at == 1,
                p_mid,
                jnp.where(
                    lane_at == 2,
                    p_low,
                    jnp.where(lane_at == 3, t_hi, jnp.where(lane_at == 4, t_low, 0.0)),
                ),
            ),
        )
        part_out[group, :, 0:16, :] = jnp.concatenate(
            [merge(values[0], values[1]), merge(values[2], values[3])], axis=1
        ).astype(BF16)
        part_out[group, :, 16:32, :] = jnp.concatenate(
            [merge(stat[0], stat[1]), merge(stat[2], stat[3])], axis=1
        ).astype(BF16)

        def send(k, _):
            tile = 2 * ring4(k // 2, col) + lax.rem(core + k, 2)
            dest = holder(tile, group)

            @pl.when(dest != s)
            def _():
                rcopy(part_out.at[group, tile], part_in.at[s], 2, dest, z)

            return 0

        lax.fori_loop(0, 8, send, 0)
        return 0

    lax.fori_loop(0, 3, attend_rows, 0)

    @pl.when(owner)
    def _():
        part_in[s] = part_out[rg, t]
        rows = pl.ds(pl.multiple_of(16 * rg, 16), 16)
        lanes = pl.ds(pl.multiple_of(128 * t, 128), 128)

        def own_tile(tile):
            block = (128 * tile) // 96
            offset = 128 * tile - 96 * block
            for k in range(2):

                @pl.when((block + k >= QUERY_BLOCKS) & (block + k != s))
                def _():
                    wait_bytes(mix.at[pl.ds(0, 16)], mix_recv.at[2 * (tile // 16) + k])

            low = pltpu.roll(qkv_in[block, rows, :].astype(F32), 128 - offset, 1)
            high = pltpu.roll(qkv_in[block + 1, rows, :].astype(F32), 96 - offset, 1)
            return jnp.where(lane16 < 96 - offset, low, high)

        q_own = own_tile(t)
        k_own = own_tile(8 + t).astype(BF16)
        v_own = own_tile(16 + t).astype(BF16)
        k_sink = sinks[0, rows, lanes].astype(BF16)
        v_sink = sinks[1, rows, lanes].astype(BF16)
        rep_row = iota((64, 16), 0)
        rep_col = iota((64, 16), 1)
        repeat = (
            ((rep_row % 16) // 4 == rep_col // 4) & (rep_row // 16 == rep_col % 4)
        ).astype(F32).astype(BF16)
        keys = jnp.concatenate(
            [
                jnp.dot(repeat, k_sink, preferred_element_type=F32),
                jnp.dot(repeat, k_own, preferred_element_type=F32),
            ],
            axis=0,
        ).reshape(8, 16, 128)
        vals = jnp.concatenate(
            [
                jnp.dot(repeat, v_sink, preferred_element_type=F32),
                jnp.dot(repeat, v_own, preferred_element_type=F32),
            ],
            axis=0,
        ).reshape(8, 16, 128)
        prod = (q_own[None] * keys).reshape(128, 128)
        prod_hi = prod.astype(BF16)
        prod_low = (prod - prod_hi.astype(F32)).astype(BF16)
        same_half = (
            (iota((128, 128), 0) < 64) == (iota((128, 128), 1) < 64)
        ).astype(F32).astype(BF16)
        score = (
            jnp.dot(prod_hi, same_half, preferred_element_type=F32)
            + jnp.dot(prod_low, same_half, preferred_element_type=F32)
        ).reshape(8, 16, 128) * (HD ** (-0.5))
        key_id = iota((8, 16, 128), 0)
        row_step = iota((8, 16, 128), 1) % STEPS
        live = (key_id < SINKS) | (key_id - SINKS <= row_step)
        near_peak = jnp.max(jnp.where(live, score, MASKED), axis=0)
        weight = jnp.where(live, jnp.exp(score - near_peak[None]), 0.0)
        near_total = jnp.sum(weight, axis=0)
        near_value = jnp.sum(weight.astype(BF16).astype(F32) * vals, axis=0)

        near[0] = near_peak
        near[1] = near_total
        near[2] = near_value
        wait_bytes(part_in.at[pl.ds(0, seq_count - 1)], recv_sem.at[2])


    @pl.when(owner)
    def _():
        near_peak, near_total, near_value = near[0], near[1], near[2]
        spread_row = iota((128, 256), 0)
        spread_col = iota((128, 256), 1)
        kk = spread_row % 64
        wanted = jnp.where(spread_col < 128, (kk < 3).astype(F32), ((kk == 3) | (kk == 4)).astype(F32))
        spread = jnp.where(
            (spread_row < 64) == (spread_col % 128 < 64), wanted, 0.0
        ).astype(BF16)
        stats = jnp.dot(
            part_in[:, 16:32, :].reshape(seq_count * 16, 128), spread, preferred_element_type=F32
        ).reshape(seq_count, 16, 256)
        peaks = stats[:, :, 0:128]
        totals = stats[:, :, 128:256]
        overall = jnp.maximum(jnp.max(peaks, axis=0), near_peak)
        factor = jnp.exp(peaks - overall[None])
        near_factor = jnp.exp(near_peak - overall)
        total = jnp.sum(factor * totals, axis=0) + near_factor * near_total
        value = (
            jnp.sum(factor * part_in[:, 0:16, :].astype(F32), axis=0) + near_factor * near_value
        )
        att_in[8 * rg + t] = (value / total).astype(BF16)
        to_plane(att_in.at[8 * rg + t], att_in.at[8 * rg + t], 3)
        wait_bytes(att_in.at[pl.ds(0, 23)], recv_sem.at[3])

    @pl.when(jnp.logical_not(owner))
    def _():
        wait_bytes(att_in, recv_sem.at[3])

    @pl.when(own_rows)
    def _():
        wait_bytes(w_rows.at[pl.ds(0, 3)], recv_sem.at[1])

    @pl.when(jnp.logical_not(own_rows))
    def _():
        wait_bytes(w_rows, recv_sem.at[1])

    attended = jnp.concatenate(
        [jnp.concatenate([att_in[8 * g + k] for k in range(8)], axis=1) for g in range(3)], axis=0
    )
    proj_in[t] = lax.dot_general(
        attended, w_rows[...].reshape(128, 1024), LAST, preferred_element_type=F32
    ).astype(BF16)
    own_lanes = pl.ds(pl.multiple_of(128 * t, 128), 128)
    own_tile_rows = (x_tok[:, own_lanes] + proj_in[t].astype(F32)).astype(BF16)
    buffer = jnp.dot(dispatch, own_tile_rows, preferred_element_type=F32)
    disp_out[...] = buffer.reshape(16, 8, 128).astype(BF16)

    def send_rows(k, _):
        dest_z = ring8(k // 8, z)
        dest_col = ring4((k // 2) & 3, col)
        dest_s = 8 * dest_col + 2 * rg + lax.rem(core + 1 + k, 2)
        rcopy(
            disp_out.at[8 * (dest_col // 2) + dest_z], disp_in.at[8 * t + z], 5, dest_s, dest_z
        )
        return 0

    lax.fori_loop(0, 8 * group_count - 1, send_rows, 0)
    disp_in[8 * t + z] = disp_out[8 * half + z]

    def send_proj(k, _):
        tile = 2 * ring4(k // 2, col) + lax.rem(core + 1 + k, 2)
        rcopy(proj_in.at[t], proj_in.at[t], 4, holder(tile, rg), z)
        return 0

    lax.fori_loop(0, 7, send_proj, 0)
    wait_bytes(proj_in.at[pl.ds(0, 7)], recv_sem.at[4])
    projected = jnp.concatenate([proj_in[k] for k in range(8)], axis=1)
    residual = x_tok[...] + projected.astype(F32)
    x_tok[...] = residual
    inverse = lax.rsqrt(jnp.mean(residual * residual, axis=-1, keepdims=True) + EPSILON)
    normed = (residual * inverse * moe_gain_ref[...]).astype(BF16)

    logits = lax.dot_general(normed, router_ref[...], LAST, preferred_element_type=F32)
    gates = jnp.zeros((48, 64), F32)
    for c in range(2):
        logit = jnp.sum(onehots[c] * logits, axis=1, keepdims=True)
        gates = gates + picks[c] * jax.nn.sigmoid(logit)
    gates_hi = gates.astype(BF16)
    gates_low = (gates - gates_hi.astype(F32)).astype(BF16)

    pltpu.make_async_copy(in_hbm.at[:, 0], win, wt_sem.at[0]).wait()
    pltpu.make_async_copy(down_hbm.at[0], down, wt_sem.at[1]).wait()
    wait_bytes(disp_in.at[pl.ds(0, 8 * group_count - 1)], recv_sem.at[5])
    raw = jnp.concatenate(
        [disp_in[8 * k : 8 * k + 8].astype(F32).reshape(64, 128) for k in range(8)], axis=1
    )
    inverse = lax.rsqrt(jnp.mean(raw * raw, axis=-1, keepdims=True) + EPSILON)
    rows_in = (raw * inverse * moe_gain_ref[...]).astype(BF16)
    gate_part = lax.dot_general(rows_in, win[0], LAST, preferred_element_type=F32)
    up_part = lax.dot_general(rows_in, win[1], LAST, preferred_element_type=F32)
    hidden = (jax.nn.gelu(gate_part, approximate=True) * up_part).astype(BF16)
    partial = jnp.dot(hidden, down[...], preferred_element_type=F32)
    left32 = iota((32, 128), 1) < 64
    for k in range(8):
        upper = partial[0:32, 128 * k : 128 * k + 128]
        lower = partial[32:64, 128 * k : 128 * k + 128]
        exp_out[2 * k] = jnp.where(left32, upper, pltpu.roll(lower, 64, 1)).astype(BF16)
        exp_out[2 * k + 1] = jnp.where(left32, pltpu.roll(upper, 64, 1), lower).astype(BF16)

    def send_exp(k, _):
        dest = 8 * lax.rem(col + 1 + k // 8, 2) + 2 * ring4((k // 2) & 3, rg) + lax.rem(core + 1 + k, 2)
        rcopy(exp_out.at[dest], exp_in.at[owner16], 6, 16 * half + dest, z)
        return 0

    lax.fori_loop(0, 15, send_exp, 0)
    exp_in[owner16] = exp_out[owner16]
    wait_bytes(exp_in.at[pl.ds(0, 15)], recv_sem.at[6])
    summed = jnp.sum(exp_in[...].astype(F32), axis=0)
    back_out[...] = summed.reshape(4, 8, 128).astype(BF16)

    def send_back(k, _):
        dest = ring8(k, z)
        rcopy(back_out.at[lax.rem(dest, 4)], back_in.at[z], 7, s, dest)
        return 0

    lax.fori_loop(0, group_count - 1, send_back, 0)
    back_in[z] = back_out[lax.rem(z, 4)]
    wait_bytes(back_in.at[pl.ds(0, group_count - 1)], recv_sem.at[7])
    returned = back_in[...].astype(F32).reshape(64, 128).astype(BF16)
    shared = jnp.dot(gates_hi, returned, preferred_element_type=F32) + jnp.dot(
        gates_low, returned, preferred_element_type=F32
    )
    swapped = pltpu.roll(shared, 64, 1)
    left24 = iota((24, 128), 1) < 64
    fin_in[s] = jnp.where(
        z < 4,
        jnp.where(left24, shared[0:24], swapped[24:48]),
        jnp.where(left24, swapped[0:24], shared[24:48]),
    ).astype(BF16)
    to_plane(fin_in.at[s], fin_in.at[s], 8)
    wait_bytes(fin_in.at[pl.ds(0, seq_count - 1)], recv_sem.at[8])

    for k in range(8):
        lanes = slice(128 * k, 128 * k + 128)
        even = fin_in[2 * k].astype(F32) + fin_in[16 + 2 * k].astype(F32)
        odd = fin_in[2 * k + 1].astype(F32) + fin_in[17 + 2 * k].astype(F32)
        upper = jnp.where(left24, even, pltpu.roll(odd, 64, 1))
        lower = jnp.where(left24, pltpu.roll(even, 64, 1), odd)
        out_ref[0:24, lanes] = (x_tok[0:24, lanes] + upper).astype(BF16)
        out_ref[24:48, lanes] = (x_tok[24:48, lanes] + lower).astype(BF16)

    @pl.when(has_query)
    def _():
        wait_bytes(qkv_in.at[pl.ds(0, seq_count - 1)], query_send.at[0])

    each_owner(lambda copy: copy.wait_send())

    @pl.when(own_rows)
    def _():
        wait_bytes(w_rows.at[pl.ds(0, 3)], send_sem.at[1])

    @pl.when(jnp.logical_not(own_rows))
    def _():
        wait_bytes(w_rows, send_sem.at[1])

    @pl.when(owner)
    def _():
        wait_bytes(part_in.at[pl.ds(0, 23)], send_sem.at[2])
        wait_bytes(part_in.at[pl.ds(0, 31), pl.ds(0, 16)], send_sem.at[3])

    @pl.when(jnp.logical_not(owner))
    def _():
        wait_bytes(part_in.at[pl.ds(0, 24)], send_sem.at[2])

    wait_bytes(proj_in.at[pl.ds(0, 7)], send_sem.at[4])
    wait_bytes(disp_in.at[pl.ds(0, 8 * group_count - 1)], send_sem.at[5])
    wait_bytes(exp_in.at[pl.ds(0, 15)], send_sem.at[6])
    wait_bytes(back_in.at[pl.ds(0, group_count - 1)], send_sem.at[7])
    wait_bytes(fin_in.at[pl.ds(0, seq_count - 1)], send_sem.at[8])


def solution(mesh):
    seq_count = mesh.shape["seq"]
    group_count = mesh.shape["exp"]
    vmem = pl.BlockSpec(memory_space=pltpu.VMEM)
    hbm = pl.BlockSpec(memory_space=pltpu.HBM)

    def body(
        tokens,
        attn_gain,
        w_qkv,
        window_cache,
        sink_cache,
        lengths,
        w_out,
        moe_gain,
        router,
        expert_ids,
        slot_order,
        expert_in,
        expert_down,
    ):
        def pin(value):
            return pltpu.with_memory_space_constraint(value, pltpu.HBM)

        out = pl.pallas_call(
            functools.partial(layer_kernel, seq_count, group_count),
            out_shape=jax.ShapeDtypeStruct((48, 1024), BF16),
            in_specs=[hbm] * 13,
            out_specs=vmem,
            scratch_shapes=[
                pltpu.VMEM((12, 4, 1024), BF16),
                pltpu.VMEM((1, 1024), F32),
                pltpu.VMEM((96, 1024), BF16),
                pltpu.VMEM((2, 12, 4, 1024), BF16),
                pltpu.SMEM((12,), jnp.int32),
                pltpu.VMEM((32, 1024), BF16),
                pltpu.VMEM((1, 1024), F32),
                pltpu.VMEM((16, 1024), BF16),
                pltpu.VMEM((4, 2, 12), jnp.int32),
                pltpu.VMEM((1, 48), jnp.int32),
                pltpu.VMEM((2, 12, 128, 1024), BF16),
                pltpu.VMEM((2, 176, 1024), BF16),
                pltpu.VMEM((176, 1024), BF16),
                pltpu.VMEM((48, 1024), F32),
                pltpu.VMEM((48, 128), BF16),
                pltpu.VMEM((32, 48, 128), BF16),
                pltpu.VMEM((3, 16, 128), F32),
                pltpu.VMEM((3, 8, 32, 128), BF16),
                pltpu.VMEM((32, 32, 128), BF16),
                pltpu.VMEM((2, 48, 1024), F32),
                pltpu.VMEM((24, 16, 128), BF16),
                pltpu.VMEM((4, 32, 1024), BF16),
                pltpu.VMEM((8, 48, 128), BF16),
                pltpu.VMEM((16, 8, 128), BF16),
                pltpu.VMEM((64, 8, 128), BF16),
                pltpu.VMEM((16, 32, 128), BF16),
                pltpu.VMEM((16, 32, 128), BF16),
                pltpu.VMEM((4, 8, 128), BF16),
                pltpu.VMEM((8, 8, 128), BF16),
                pltpu.VMEM((32, 24, 128), BF16),
                pltpu.SemaphoreType.DMA((1,)),
                pltpu.SemaphoreType.DMA((3,)),
                pltpu.SemaphoreType.DMA((6,)),
                pltpu.SemaphoreType.DMA((4,)),
                pltpu.SemaphoreType.DMA((2, 3)),
                pltpu.SemaphoreType.DMA((2,)),
                pltpu.SemaphoreType.DMA((10,)),
                pltpu.SemaphoreType.DMA((10,)),
                pltpu.SemaphoreType.DMA((10,)),
            ],
            compiler_params=pltpu.CompilerParams(
                collective_id=0, has_side_effects=True, vmem_limit_bytes=48 * 1024 * 1024
            ),
            name="layer",
        )(
            pin(tokens),
            pin(attn_gain.reshape(1, -1)),
            pin(w_qkv),
            pin(window_cache),
            pin(sink_cache),
            pin(lengths),
            pin(w_out),
            pin(moe_gain.reshape(1, -1)),
            pin(router.T),
            pin(expert_ids.transpose(1, 2, 0)),
            pin(slot_order),
            pin(expert_in),
            pin(expert_down),
        )
        return out.reshape(tokens.shape)

    in_specs = (
        P("exp", None, None),
        P(),
        P("seq", None),
        P(None, "exp", "seq", None),
        P(None, "exp", None, None),
        P("exp"),
        P("seq", None),
        P(),
        P(),
        P("exp", None, None),
        P("exp", None),
        P(None, "exp", "seq", None),
        P("exp", "seq", None),
    )
    out_specs = P("exp", None, None)
    return jax.shard_map(body, mesh=mesh, in_specs=in_specs, out_specs=out_specs, check_vma=False)
```

```python
import functools

import jax
import jax.numpy as jnp
from jax import lax
from jax.experimental import pallas as pl
from jax.experimental.pallas import tpu as pltpu
from jax.sharding import PartitionSpec as P

HEADS = 16
HD = 64
EXPERTS = 16
SINKS = 4
WIN = 4096
CAP = 8
STEPS = 4
EPSILON = 1e-06
MASKED = -1e30
QUERY_BLOCKS = 11
MESH = pl.DeviceIdType.MESH
F32 = jnp.float32
BF16 = jnp.bfloat16
LAST = (((1,), (1,)), ((), ()))


def iota(shape, axis):
    return lax.broadcasted_iota(jnp.int32, shape, axis)


def wait_bytes(ref, sem):
    pltpu.make_async_copy(ref, ref, sem).wait()


def layer_kernel(
    seq_count,
    group_count,
    tokens_hbm,
    attn_gain_hbm,
    w_qkv_hbm,
    cache_hbm,
    sink_hbm,
    lengths_hbm,
    w_out_hbm,
    moe_gain_hbm,
    router_hbm,
    ids_hbm,
    order_hbm,
    in_hbm,
    down_hbm,
    out_ref,
    tokens_ref,
    attn_gain_ref,
    w_qkv_ref,
    sink_ref,
    lengths_ref,
    w_out_ref,
    moe_gain_ref,
    router_ref,
    ids_ref,
    order_ref,
    kv,
    win,
    down,
    x_tok,
    mix,
    qkv_in,
    near,
    part_out,
    part_in,
    sinks,
    att_in,
    w_rows,
    proj_in,
    disp_out,
    disp_in,
    exp_out,
    exp_in,
    back_out,
    back_in,
    fin_in,
    query_send,
    query_recv,
    mix_send,
    mix_recv,
    kv_sem,
    wt_sem,
    arg_sem,
    send_sem,
    recv_sem,
):
    s = lax.axis_index("seq")
    z = lax.axis_index("exp")
    col = s // 8
    rg = lax.rem(s // 2, 4)
    core = lax.rem(s, 2)
    t = 2 * col + core
    half = s // 16
    owner16 = lax.rem(s, 16)
    owner = rg < 3
    own_rows = core == rg // 2

    def holder(tile, group):
        return 8 * (tile // 2) + 2 * group + lax.rem(tile, 2)

    small = (
        (tokens_hbm, tokens_ref),
        (w_qkv_hbm, w_qkv_ref),
        (attn_gain_hbm, attn_gain_ref),
        (w_out_hbm, w_out_ref),
        (ids_hbm, ids_ref),
        (order_hbm, order_ref),
        (sink_hbm, sink_ref),
        (lengths_hbm, lengths_ref),
        (moe_gain_hbm, moe_gain_ref),
        (router_hbm, router_ref),
    )

    def fetch(at):
        return pltpu.make_async_copy(small[at][0], small[at][1], arg_sem.at[at])

    barrier = pltpu.get_barrier_semaphore()

    def ring4(at, position):
        return lax.rem(position + ((54 >> (2 * at)) & 3), 4)

    def ring8(at, position):
        return lax.rem(position + ((0o7162534 >> (3 * at)) & 7), group_count)

    def plane_peer(k):
        return 8 * ring4((k // 2) & 3, col) + 2 * ring4(k // 8, rg) + lax.rem(core + 1 + k, 2)

    def greet_plane(k, _):
        pl.semaphore_signal(barrier, inc=1, device_id=(plane_peer(k), z), device_id_type=MESH)
        return 0

    def greet_line(k, _):
        pl.semaphore_signal(barrier, inc=1, device_id=(s, ring8(k, z)), device_id_type=MESH)
        return 0

    lax.fori_loop(0, group_count - 1, greet_line, 0)
    lax.fori_loop(0, seq_count - 1, greet_plane, 0)

    for at in range(len(small)):
        fetch(at).start()

    for part in range(3):
        for which in range(2):
            pltpu.make_async_copy(
                cache_hbm.at[which, pl.ds(4 * part, 4)],
                kv.at[which, pl.ds(4 * part, 4)],
                kv_sem.at[which, part],
            ).start()
    pltpu.make_async_copy(in_hbm.at[:, 0], win, wt_sem.at[0]).start()
    pltpu.make_async_copy(down_hbm.at[0], down, wt_sem.at[1]).start()

    def rcopy(src, dst, stage, dest_s, dest_z):
        pltpu.make_async_remote_copy(
            src_ref=src,
            dst_ref=dst,
            send_sem=send_sem.at[stage],
            recv_sem=recv_sem.at[stage],
            device_id=(dest_s, dest_z),
            device_id_type=MESH,
        ).start()

    def to_plane(src, dst, stage):
        def send(k, _):
            rcopy(src, dst, stage, plane_peer(k), z)
            return 0

        lax.fori_loop(0, seq_count - 1, send, 0)

    for at in range(3):
        fetch(at).wait()
    for r in range(12):
        x_tok[4 * r : 4 * r + 4, :] = tokens_ref[r].astype(F32)
    x = x_tok[...]
    inverse = lax.rsqrt(jnp.mean(x * x, axis=-1, keepdims=True) + EPSILON)
    normed = (x * inverse * attn_gain_ref[...]).astype(BF16)
    own_mix = lax.dot_general(normed, w_qkv_ref[...], LAST, preferred_element_type=F32)
    mix[...] = jnp.concatenate([own_mix, jnp.zeros((48, 32), F32)], axis=1).astype(BF16)

    pl.semaphore_wait(barrier, seq_count - 1 + group_count - 1)

    qkv_in[s] = mix[...]

    def send_mix(group, send_to, recv_to, dest):
        rows = pl.ds(pl.multiple_of(16 * group, 16), 16)
        return pltpu.make_async_remote_copy(
            src_ref=mix.at[rows],
            dst_ref=qkv_in.at[s, rows],
            send_sem=send_to,
            recv_sem=recv_to,
            device_id=(dest, z),
            device_id_type=MESH,
        )

    has_query = s < QUERY_BLOCKS
    first_tile = (96 * s) // 128
    last_tile = (96 * s + 95) // 128

    @pl.when(has_query)
    def _():
        def send(k, _):
            group = k // (seq_count - 1)
            peer = plane_peer(k - group * (seq_count - 1))
            send_mix(group, query_send.at[0], query_recv.at[group], peer).start()
            return 0

        lax.fori_loop(0, 3 * (seq_count - 1), send, 0)

    def each_owner(act):
        for group in range(3):
            for at, tile in enumerate((first_tile, last_tile)):
                dest = holder(lax.rem(tile, 8), group)
                go = jnp.logical_not(has_query) & (dest != s)
                if at == 1:
                    go = go & (first_tile != last_tile)
                place = 2 * (tile // 16) + s - (128 * tile) // 96

                @pl.when(go)
                def _():
                    act(
                        send_mix(
                            group, mix_send.at[2 * group + at], mix_recv.at[place], dest
                        )
                    )

    each_owner(lambda copy: copy.start())
    fetch(3).wait()

    w_at = 2 * lax.rem(rg, 2) + core

    @pl.when(own_rows)
    def _():
        w_rows[w_at] = w_out_ref[...]

    for row in range(4):
        w_dest = 8 * col + 2 * row + rg // 2

        @pl.when(w_dest != s)
        def _():
            rcopy(w_out_ref, w_rows.at[w_at], 1, w_dest, z)

    for at in range(4, 10):
        fetch(at).wait()
    eye = iota((48, 48), 0) == iota((48, 48), 1)
    prio_row = order_ref[...]
    prio_col = jnp.sum(jnp.where(eye, prio_row, 0), axis=1, keepdims=True)
    earlier = (prio_row < prio_col).astype(F32).astype(BF16)
    expert_lane = iota((48, EXPERTS), 1)
    id_row_of = iota((48, 12), 0)
    id_lane = iota((48, 12), 1)
    id_cols = []
    onehots = []
    for c in range(2):
        spread_ids = jnp.zeros((48, 12), jnp.int32)
        for step in range(STEPS):
            wanted = (id_row_of // STEPS == id_lane) & (id_row_of % STEPS == step)
            spread_ids = spread_ids + jnp.where(wanted, ids_ref[step, c : c + 1, :], 0)
        id_cols.append(jnp.sum(spread_ids, axis=1, keepdims=True))
        onehots.append((expert_lane == id_cols[c]).astype(F32))
    counts = jnp.dot(earlier, (onehots[0] + onehots[1]).astype(BF16), preferred_element_type=F32)
    sel_rows = iota((128, 48), 0)
    sel_expert = 2 * ((sel_rows // CAP) % 8) + sel_rows // 64
    sel_slot = sel_rows % CAP
    col_ids = iota((48, 64), 1)
    col_expert = 2 * (col_ids // CAP) + half
    col_slot = col_ids % CAP
    dispatch = jnp.zeros((128, 48), F32)
    picks = []
    for c in range(2):
        pos_col = jnp.sum(onehots[c] * counts, axis=1, keepdims=True).astype(jnp.int32)
        id_col = id_cols[c]
        pos_row = jnp.sum(jnp.where(eye, pos_col, 0), axis=0, keepdims=True)
        id_row = jnp.sum(jnp.where(eye, id_col, 0), axis=0, keepdims=True)
        dispatch = dispatch + ((id_row == sel_expert) & (pos_row == sel_slot)).astype(F32)
        picks.append(((id_col == col_expert) & (pos_col == col_slot)).astype(F32))
    dispatch = dispatch.astype(BF16)

    for r in range(12):
        for which in range(2):
            sinks[which, 4 * r : 4 * r + 4, :] = sink_ref[which, r].astype(F32)

    def wait_query(group):
        @pl.when(has_query)
        def _():
            wait_bytes(qkv_in.at[pl.ds(0, QUERY_BLOCKS - 1), pl.ds(0, 16)], query_recv.at[group])

        @pl.when(jnp.logical_not(has_query))
        def _():
            wait_bytes(qkv_in.at[pl.ds(0, QUERY_BLOCKS), pl.ds(0, 16)], query_recv.at[group])

    lane16 = iota((16, 128), 1)

    def query_tiles(rows):
        tiles = []
        for first in range(0, QUERY_BLOCKS, 4):
            last = min(first + 3, QUERY_BLOCKS - 1)
            b0, b1, b2, b3 = (
                qkv_in[b, rows, :].astype(F32) for b in (first, first + 1, first + 2, last)
            )
            r1 = pltpu.roll(b1, 96, 1)
            r2 = pltpu.roll(b2, 64, 1)
            r3 = pltpu.roll(b3, 32, 1)
            tiles.append(jnp.where(lane16 < 96, b0, r1))
            tiles.append(jnp.where(lane16 < 64, r1, r2))
            tiles.append(jnp.where(lane16 < 32, r2, r3))
        return tiles[0:8]

    sub2 = iota((2, 8, 128), 1)
    lane2 = iota((2, 8, 128), 2)
    diag2 = (sub2 < 4) == (lane2 < 64)
    zero = jnp.zeros((8, 128), F32)

    def spread_queries(tiles):
        parts = []
        for tile in tiles:
            v = tile.reshape(2, 8, 128)
            w = pltpu.roll(v, 4, 1)
            even = jnp.where(diag2, jnp.where(sub2 < 4, v, w), 0.0)
            odd = jnp.where(diag2, jnp.where(sub2 < 4, w, v), 0.0)
            parts.append((even, odd))
        spread = []
        for pair in range(2):
            for parity in range(2):
                row = []
                for u in range(4):
                    upper = jnp.concatenate([parts[2 * u][parity][pair], zero], axis=1)
                    lower = jnp.concatenate([zero, parts[2 * u + 1][parity][pair]], axis=1)
                    row.append(jnp.concatenate([upper, lower], axis=0).astype(BF16))
                spread.append(row)
        return spread

    sub8 = iota((8, 8, 128), 1)
    lane8 = iota((8, 8, 128), 2)
    lane_in = lane8 % 64
    step_id = iota((8, 128), 0) % STEPS
    slot_id = s * 128 + iota((8, 128), 1)

    def merge(a, b):
        ar = pltpu.roll(a, 4, 1)
        br = pltpu.roll(b, 4, 1)
        return jnp.where(
            sub8 < 4, jnp.where(lane8 < 64, a, ar), jnp.where(lane8 < 64, br, b)
        )

    def cache_part(which, group):
        at = pl.ds(4 * group, 4)
        return pltpu.make_async_copy(
            cache_hbm.at[which, at], kv.at[which, at], kv_sem.at[which, group]
        )

    def attend_rows(group, _):
        cache_part(0, group).wait()
        cache_part(1, group).wait()
        wait_query(group)
        queries = spread_queries(query_tiles(pl.ds(pl.multiple_of(16 * group, 16), 16)))
        scores = []
        for k in range(4):
            for u in range(4):
                scores.append(
                    lax.dot_general(
                        queries[k][u],
                        kv[0, 4 * group + k, :, 256 * u : 256 * u + 256],
                        LAST,
                        preferred_element_type=F32,
                    )
                )
        score = jnp.concatenate(scores, axis=0).reshape(4, 8, 8, 128) * (HD ** (-0.5))
        lives = []
        for k in range(4):
            held = lengths_ref[4 * group + k] - SINKS
            age = (slot_id - held) & (WIN - 1)
            lives.append(((slot_id < jnp.minimum(WIN, held)) & (age > step_id)).astype(F32))
        live = jnp.concatenate(lives, axis=0).reshape(4, 1, 8, 128) > 0.0
        peak = jnp.max(jnp.where(live, score, MASKED), axis=-1, keepdims=True)
        weight = jnp.where(live, jnp.exp(score - peak), 0.0)
        total = jnp.sum(weight, axis=-1, keepdims=True)
        rounded = weight.reshape(256, 128).astype(BF16)
        values = []
        for k in range(4):
            found = []
            for u in range(4):
                at = 64 * k + 16 * u
                mixed = jnp.dot(
                    rounded[at : at + 16],
                    kv[1, 4 * group + k, :, 256 * u : 256 * u + 256],
                    preferred_element_type=F32,
                )
                found.append(mixed[0:8, 0:128])
                found.append(mixed[8:16, 128:256])
            values.append(jnp.concatenate(found, axis=0).reshape(8, 8, 128))
        peak = jnp.broadcast_to(peak, (4, 8, 8, 128))
        total = jnp.broadcast_to(total, (4, 8, 8, 128))
        p_hi = peak.astype(BF16).astype(F32)
        p_mid = (peak - p_hi).astype(BF16).astype(F32)
        p_low = peak - p_hi - p_mid
        t_hi = total.astype(BF16).astype(F32)
        t_low = total - t_hi
        lane_at = lane_in[None]
        stat = jnp.where(
            lane_at == 0,
            p_hi,
            jnp.where(
                lane_at == 1,
                p_mid,
                jnp.where(
                    lane_at == 2,
                    p_low,
                    jnp.where(lane_at == 3, t_hi, jnp.where(lane_at == 4, t_low, 0.0)),
                ),
            ),
        )
        part_out[group, :, 0:16, :] = jnp.concatenate(
            [merge(values[0], values[1]), merge(values[2], values[3])], axis=1
        ).astype(BF16)
        part_out[group, :, 16:32, :] = jnp.concatenate(
            [merge(stat[0], stat[1]), merge(stat[2], stat[3])], axis=1
        ).astype(BF16)

        def send(k, _):
            tile = 2 * ring4(k // 2, col) + lax.rem(core + k, 2)
            dest = holder(tile, group)

            @pl.when(dest != s)
            def _():
                rcopy(part_out.at[group, tile], part_in.at[s], 2, dest, z)

            return 0

        lax.fori_loop(0, 8, send, 0)
        return 0

    lax.fori_loop(0, 3, attend_rows, 0)

    @pl.when(owner)
    def _():
        part_in[s] = part_out[rg, t]
        rows = pl.ds(pl.multiple_of(16 * rg, 16), 16)
        lanes = pl.ds(pl.multiple_of(128 * t, 128), 128)

        def own_tile(tile):
            block = (128 * tile) // 96
            offset = 128 * tile - 96 * block
            for k in range(2):

                @pl.when((block + k >= QUERY_BLOCKS) & (block + k != s))
                def _():
                    wait_bytes(mix.at[pl.ds(0, 16)], mix_recv.at[2 * (tile // 16) + k])

            low = pltpu.roll(qkv_in[block, rows, :].astype(F32), 128 - offset, 1)
            high = pltpu.roll(qkv_in[block + 1, rows, :].astype(F32), 96 - offset, 1)
            return jnp.where(lane16 < 96 - offset, low, high)

        q_own = own_tile(t)
        k_own = own_tile(8 + t).astype(BF16)
        v_own = own_tile(16 + t).astype(BF16)
        k_sink = sinks[0, rows, lanes].astype(BF16)
        v_sink = sinks[1, rows, lanes].astype(BF16)
        rep_row = iota((64, 16), 0)
        rep_col = iota((64, 16), 1)
        repeat = (
            ((rep_row % 16) // 4 == rep_col // 4) & (rep_row // 16 == rep_col % 4)
        ).astype(F32).astype(BF16)
        keys = jnp.concatenate(
            [
                jnp.dot(repeat, k_sink, preferred_element_type=F32),
                jnp.dot(repeat, k_own, preferred_element_type=F32),
            ],
            axis=0,
        ).reshape(8, 16, 128)
        vals = jnp.concatenate(
            [
                jnp.dot(repeat, v_sink, preferred_element_type=F32),
                jnp.dot(repeat, v_own, preferred_element_type=F32),
            ],
            axis=0,
        ).reshape(8, 16, 128)
        prod = (q_own[None] * keys).reshape(128, 128)
        prod_hi = prod.astype(BF16)
        prod_low = (prod - prod_hi.astype(F32)).astype(BF16)
        same_half = (
            (iota((128, 128), 0) < 64) == (iota((128, 128), 1) < 64)
        ).astype(F32).astype(BF16)
        score = (
            jnp.dot(prod_hi, same_half, preferred_element_type=F32)
            + jnp.dot(prod_low, same_half, preferred_element_type=F32)
        ).reshape(8, 16, 128) * (HD ** (-0.5))
        key_id = iota((8, 16, 128), 0)
        row_step = iota((8, 16, 128), 1) % STEPS
        live = (key_id < SINKS) | (key_id - SINKS <= row_step)
        near_peak = jnp.max(jnp.where(live, score, MASKED), axis=0)
        weight = jnp.where(live, jnp.exp(score - near_peak[None]), 0.0)
        near_total = jnp.sum(weight, axis=0)
        near_value = jnp.sum(weight.astype(BF16).astype(F32) * vals, axis=0)

        near[0] = near_peak
        near[1] = near_total
        near[2] = near_value
        wait_bytes(part_in.at[pl.ds(0, seq_count - 1)], recv_sem.at[2])


    @pl.when(owner)
    def _():
        near_peak, near_total, near_value = near[0], near[1], near[2]
        spread_row = iota((128, 256), 0)
        spread_col = iota((128, 256), 1)
        kk = spread_row % 64
        wanted = jnp.where(spread_col < 128, (kk < 3).astype(F32), ((kk == 3) | (kk == 4)).astype(F32))
        spread = jnp.where(
            (spread_row < 64) == (spread_col % 128 < 64), wanted, 0.0
        ).astype(BF16)
        stats = jnp.dot(
            part_in[:, 16:32, :].reshape(seq_count * 16, 128), spread, preferred_element_type=F32
        ).reshape(seq_count, 16, 256)
        peaks = stats[:, :, 0:128]
        totals = stats[:, :, 128:256]
        overall = jnp.maximum(jnp.max(peaks, axis=0), near_peak)
        factor = jnp.exp(peaks - overall[None])
        near_factor = jnp.exp(near_peak - overall)
        total = jnp.sum(factor * totals, axis=0) + near_factor * near_total
        value = (
            jnp.sum(factor * part_in[:, 0:16, :].astype(F32), axis=0) + near_factor * near_value
        )
        att_in[8 * rg + t] = (value / total).astype(BF16)
        to_plane(att_in.at[8 * rg + t], att_in.at[8 * rg + t], 3)
        wait_bytes(att_in.at[pl.ds(0, 23)], recv_sem.at[3])

    @pl.when(jnp.logical_not(owner))
    def _():
        wait_bytes(att_in, recv_sem.at[3])

    @pl.when(own_rows)
    def _():
        wait_bytes(w_rows.at[pl.ds(0, 3)], recv_sem.at[1])

    @pl.when(jnp.logical_not(own_rows))
    def _():
        wait_bytes(w_rows, recv_sem.at[1])

    attended = jnp.concatenate(
        [jnp.concatenate([att_in[8 * g + k] for k in range(8)], axis=1) for g in range(3)], axis=0
    )
    proj_in[t] = lax.dot_general(
        attended, w_rows[...].reshape(128, 1024), LAST, preferred_element_type=F32
    ).astype(BF16)
    own_lanes = pl.ds(pl.multiple_of(128 * t, 128), 128)
    own_tile_rows = (x_tok[:, own_lanes] + proj_in[t].astype(F32)).astype(BF16)
    buffer = jnp.dot(dispatch, own_tile_rows, preferred_element_type=F32)
    disp_out[...] = buffer.reshape(16, 8, 128).astype(BF16)

    def send_rows(k, _):
        dest_z = ring8((k // 2) & 7, z)
        dest_col = ring4(k // 16, col)
        dest_s = 8 * dest_col + 2 * rg + lax.rem(core + 1 + k, 2)
        rcopy(
            disp_out.at[8 * (dest_col // 2) + dest_z], disp_in.at[8 * t + z], 5, dest_s, dest_z
        )
        return 0

    lax.fori_loop(0, 8 * group_count - 1, send_rows, 0)
    disp_in[8 * t + z] = disp_out[8 * half + z]

    def send_proj(k, _):
        tile = 2 * ring4(k // 2, col) + lax.rem(core + 1 + k, 2)
        rcopy(proj_in.at[t], proj_in.at[t], 4, holder(tile, rg), z)
        return 0

    lax.fori_loop(0, 7, send_proj, 0)
    wait_bytes(proj_in.at[pl.ds(0, 7)], recv_sem.at[4])
    projected = jnp.concatenate([proj_in[k] for k in range(8)], axis=1)
    residual = x_tok[...] + projected.astype(F32)
    x_tok[...] = residual
    inverse = lax.rsqrt(jnp.mean(residual * residual, axis=-1, keepdims=True) + EPSILON)
    normed = (residual * inverse * moe_gain_ref[...]).astype(BF16)

    logits = lax.dot_general(normed, router_ref[...], LAST, preferred_element_type=F32)
    gates = jnp.zeros((48, 64), F32)
    for c in range(2):
        logit = jnp.sum(onehots[c] * logits, axis=1, keepdims=True)
        gates = gates + picks[c] * jax.nn.sigmoid(logit)
    gates_hi = gates.astype(BF16)
    gates_low = (gates - gates_hi.astype(F32)).astype(BF16)

    pltpu.make_async_copy(in_hbm.at[:, 0], win, wt_sem.at[0]).wait()
    pltpu.make_async_copy(down_hbm.at[0], down, wt_sem.at[1]).wait()
    wait_bytes(disp_in.at[pl.ds(0, 8 * group_count - 1)], recv_sem.at[5])
    raw = jnp.concatenate(
        [disp_in[8 * k : 8 * k + 8].astype(F32).reshape(64, 128) for k in range(8)], axis=1
    )
    inverse = lax.rsqrt(jnp.mean(raw * raw, axis=-1, keepdims=True) + EPSILON)
    rows_in = (raw * inverse * moe_gain_ref[...]).astype(BF16)
    gate_part = lax.dot_general(rows_in, win[0], LAST, preferred_element_type=F32)
    up_part = lax.dot_general(rows_in, win[1], LAST, preferred_element_type=F32)
    hidden = (jax.nn.gelu(gate_part, approximate=True) * up_part).astype(BF16)
    partial = jnp.dot(hidden, down[...], preferred_element_type=F32)
    left32 = iota((32, 128), 1) < 64
    for k in range(8):
        upper = partial[0:32, 128 * k : 128 * k + 128]
        lower = partial[32:64, 128 * k : 128 * k + 128]
        exp_out[2 * k] = jnp.where(left32, upper, pltpu.roll(lower, 64, 1)).astype(BF16)
        exp_out[2 * k + 1] = jnp.where(left32, pltpu.roll(upper, 64, 1), lower).astype(BF16)

    def send_exp(k, _):
        dest = 8 * lax.rem(col + 1 + k // 8, 2) + 2 * ring4((k // 2) & 3, rg) + lax.rem(core + 1 + k, 2)
        rcopy(exp_out.at[dest], exp_in.at[owner16], 6, 16 * half + dest, z)
        return 0

    lax.fori_loop(0, 15, send_exp, 0)
    exp_in[owner16] = exp_out[owner16]
    wait_bytes(exp_in.at[pl.ds(0, 15)], recv_sem.at[6])
    summed = jnp.sum(exp_in[...].astype(F32), axis=0)
    back_out[...] = summed.reshape(4, 8, 128).astype(BF16)

    def send_back(k, _):
        dest = ring8(k, z)
        rcopy(back_out.at[lax.rem(dest, 4)], back_in.at[z], 7, s, dest)
        return 0

    lax.fori_loop(0, group_count - 1, send_back, 0)
    back_in[z] = back_out[lax.rem(z, 4)]
    wait_bytes(back_in.at[pl.ds(0, group_count - 1)], recv_sem.at[7])
    returned = back_in[...].astype(F32).reshape(64, 128).astype(BF16)
    shared = jnp.dot(gates_hi, returned, preferred_element_type=F32) + jnp.dot(
        gates_low, returned, preferred_element_type=F32
    )
    swapped = pltpu.roll(shared, 64, 1)
    left24 = iota((24, 128), 1) < 64
    fin_in[s] = jnp.where(
        z < 4,
        jnp.where(left24, shared[0:24], swapped[24:48]),
        jnp.where(left24, swapped[0:24], shared[24:48]),
    ).astype(BF16)
    to_plane(fin_in.at[s], fin_in.at[s], 8)
    wait_bytes(fin_in.at[pl.ds(0, seq_count - 1)], recv_sem.at[8])

    for k in range(8):
        lanes = slice(128 * k, 128 * k + 128)
        even = fin_in[2 * k].astype(F32) + fin_in[16 + 2 * k].astype(F32)
        odd = fin_in[2 * k + 1].astype(F32) + fin_in[17 + 2 * k].astype(F32)
        upper = jnp.where(left24, even, pltpu.roll(odd, 64, 1))
        lower = jnp.where(left24, pltpu.roll(even, 64, 1), odd)
        out_ref[0:24, lanes] = (x_tok[0:24, lanes] + upper).astype(BF16)
        out_ref[24:48, lanes] = (x_tok[24:48, lanes] + lower).astype(BF16)

    @pl.when(has_query)
    def _():
        wait_bytes(qkv_in.at[pl.ds(0, seq_count - 1)], query_send.at[0])

    each_owner(lambda copy: copy.wait_send())

    @pl.when(own_rows)
    def _():
        wait_bytes(w_rows.at[pl.ds(0, 3)], send_sem.at[1])

    @pl.when(jnp.logical_not(own_rows))
    def _():
        wait_bytes(w_rows, send_sem.at[1])

    @pl.when(owner)
    def _():
        wait_bytes(part_in.at[pl.ds(0, 23)], send_sem.at[2])
        wait_bytes(part_in.at[pl.ds(0, 31), pl.ds(0, 16)], send_sem.at[3])

    @pl.when(jnp.logical_not(owner))
    def _():
        wait_bytes(part_in.at[pl.ds(0, 24)], send_sem.at[2])

    wait_bytes(proj_in.at[pl.ds(0, 7)], send_sem.at[4])
    wait_bytes(disp_in.at[pl.ds(0, 8 * group_count - 1)], send_sem.at[5])
    wait_bytes(exp_in.at[pl.ds(0, 15)], send_sem.at[6])
    wait_bytes(back_in.at[pl.ds(0, group_count - 1)], send_sem.at[7])
    wait_bytes(fin_in.at[pl.ds(0, seq_count - 1)], send_sem.at[8])


def solution(mesh):
    seq_count = mesh.shape["seq"]
    group_count = mesh.shape["exp"]
    vmem = pl.BlockSpec(memory_space=pltpu.VMEM)
    hbm = pl.BlockSpec(memory_space=pltpu.HBM)

    def body(
        tokens,
        attn_gain,
        w_qkv,
        window_cache,
        sink_cache,
        lengths,
        w_out,
        moe_gain,
        router,
        expert_ids,
        slot_order,
        expert_in,
        expert_down,
    ):
        def pin(value):
            return pltpu.with_memory_space_constraint(value, pltpu.HBM)

        out = pl.pallas_call(
            functools.partial(layer_kernel, seq_count, group_count),
            out_shape=jax.ShapeDtypeStruct((48, 1024), BF16),
            in_specs=[hbm] * 13,
            out_specs=vmem,
            scratch_shapes=[
                pltpu.VMEM((12, 4, 1024), BF16),
                pltpu.VMEM((1, 1024), F32),
                pltpu.VMEM((96, 1024), BF16),
                pltpu.VMEM((2, 12, 4, 1024), BF16),
                pltpu.SMEM((12,), jnp.int32),
                pltpu.VMEM((32, 1024), BF16),
                pltpu.VMEM((1, 1024), F32),
                pltpu.VMEM((16, 1024), BF16),
                pltpu.VMEM((4, 2, 12), jnp.int32),
                pltpu.VMEM((1, 48), jnp.int32),
                pltpu.VMEM((2, 12, 128, 1024), BF16),
                pltpu.VMEM((2, 176, 1024), BF16),
                pltpu.VMEM((176, 1024), BF16),
                pltpu.VMEM((48, 1024), F32),
                pltpu.VMEM((48, 128), BF16),
                pltpu.VMEM((32, 48, 128), BF16),
                pltpu.VMEM((3, 16, 128), F32),
                pltpu.VMEM((3, 8, 32, 128), BF16),
                pltpu.VMEM((32, 32, 128), BF16),
                pltpu.VMEM((2, 48, 1024), F32),
                pltpu.VMEM((24, 16, 128), BF16),
                pltpu.VMEM((4, 32, 1024), BF16),
                pltpu.VMEM((8, 48, 128), BF16),
                pltpu.VMEM((16, 8, 128), BF16),
                pltpu.VMEM((64, 8, 128), BF16),
                pltpu.VMEM((16, 32, 128), BF16),
                pltpu.VMEM((16, 32, 128), BF16),
                pltpu.VMEM((4, 8, 128), BF16),
                pltpu.VMEM((8, 8, 128), BF16),
                pltpu.VMEM((32, 24, 128), BF16),
                pltpu.SemaphoreType.DMA((1,)),
                pltpu.SemaphoreType.DMA((3,)),
                pltpu.SemaphoreType.DMA((6,)),
                pltpu.SemaphoreType.DMA((4,)),
                pltpu.SemaphoreType.DMA((2, 3)),
                pltpu.SemaphoreType.DMA((2,)),
                pltpu.SemaphoreType.DMA((10,)),
                pltpu.SemaphoreType.DMA((10,)),
                pltpu.SemaphoreType.DMA((10,)),
            ],
            compiler_params=pltpu.CompilerParams(
                collective_id=0, has_side_effects=True, vmem_limit_bytes=48 * 1024 * 1024
            ),
            name="layer",
        )(
            pin(tokens),
            pin(attn_gain.reshape(1, -1)),
            pin(w_qkv),
            pin(window_cache),
            pin(sink_cache),
            pin(lengths),
            pin(w_out),
            pin(moe_gain.reshape(1, -1)),
            pin(router.T),
            pin(expert_ids.transpose(1, 2, 0)),
            pin(slot_order),
            pin(expert_in),
            pin(expert_down),
        )
        return out.reshape(tokens.shape)

    in_specs = (
        P("exp", None, None),
        P(),
        P("seq", None),
        P(None, "exp", "seq", None),
        P(None, "exp", None, None),
        P("exp"),
        P("seq", None),
        P(),
        P(),
        P("exp", None, None),
        P("exp", None),
        P(None, "exp", "seq", None),
        P("exp", "seq", None),
    )
    out_specs = P("exp", None, None)
    return jax.shard_map(body, mesh=mesh, in_specs=in_specs, out_specs=out_specs, check_vma=False)
```

```python
import functools

import jax
import jax.numpy as jnp
from jax import lax
from jax.experimental import pallas as pl
from jax.experimental.pallas import tpu as pltpu
from jax.sharding import PartitionSpec as P

HEADS = 16
HD = 64
EXPERTS = 16
SINKS = 4
WIN = 4096
CAP = 8
STEPS = 4
EPSILON = 1e-06
MASKED = -1e30
QUERY_BLOCKS = 11
MESH = pl.DeviceIdType.MESH
F32 = jnp.float32
BF16 = jnp.bfloat16
LAST = (((1,), (1,)), ((), ()))


def iota(shape, axis):
    return lax.broadcasted_iota(jnp.int32, shape, axis)


def wait_bytes(ref, sem):
    pltpu.make_async_copy(ref, ref, sem).wait()


def layer_kernel(
    seq_count,
    group_count,
    tokens_hbm,
    attn_gain_hbm,
    w_qkv_hbm,
    cache_hbm,
    sink_hbm,
    lengths_hbm,
    w_out_hbm,
    moe_gain_hbm,
    router_hbm,
    ids_hbm,
    order_hbm,
    in_hbm,
    down_hbm,
    out_ref,
    tokens_ref,
    attn_gain_ref,
    w_qkv_ref,
    sink_ref,
    lengths_ref,
    w_out_ref,
    moe_gain_ref,
    router_ref,
    ids_ref,
    order_ref,
    kv,
    win,
    down,
    x_tok,
    mix,
    qkv_in,
    near,
    part_out,
    part_in,
    sinks,
    att_in,
    w_rows,
    proj_in,
    disp_out,
    disp_in,
    exp_out,
    exp_in,
    back_out,
    back_in,
    fin_in,
    query_send,
    query_recv,
    mix_send,
    mix_recv,
    kv_sem,
    wt_sem,
    arg_sem,
    send_sem,
    recv_sem,
):
    s = lax.axis_index("seq")
    z = lax.axis_index("exp")
    col = s // 8
    rg = lax.rem(s // 2, 4)
    core = lax.rem(s, 2)
    t = 2 * col + core
    half = s // 16
    owner16 = lax.rem(s, 16)
    owner = rg < 3
    own_rows = core == rg // 2

    def holder(tile, group):
        return 8 * (tile // 2) + 2 * group + lax.rem(tile, 2)

    small = (
        (tokens_hbm, tokens_ref),
        (w_qkv_hbm, w_qkv_ref),
        (attn_gain_hbm, attn_gain_ref),
        (w_out_hbm, w_out_ref),
        (ids_hbm, ids_ref),
        (order_hbm, order_ref),
        (sink_hbm, sink_ref),
        (lengths_hbm, lengths_ref),
        (moe_gain_hbm, moe_gain_ref),
        (router_hbm, router_ref),
    )

    def fetch(at):
        return pltpu.make_async_copy(small[at][0], small[at][1], arg_sem.at[at])

    barrier = pltpu.get_barrier_semaphore()

    def ring4(at, position):
        return lax.rem(position + ((54 >> (2 * at)) & 3), 4)

    def ring8(at, position):
        return lax.rem(position + ((0o7162534 >> (3 * at)) & 7), group_count)

    def plane_peer(k):
        return 8 * ring4((k // 2) & 3, col) + 2 * ring4(k // 8, rg) + lax.rem(core + 1 + k, 2)

    def greet_plane(k, _):
        pl.semaphore_signal(barrier, inc=1, device_id=(plane_peer(k), z), device_id_type=MESH)
        return 0

    def greet_line(k, _):
        pl.semaphore_signal(barrier, inc=1, device_id=(s, ring8(k, z)), device_id_type=MESH)
        return 0

    lax.fori_loop(0, group_count - 1, greet_line, 0)
    lax.fori_loop(0, seq_count - 1, greet_plane, 0)

    for at in range(len(small)):
        fetch(at).start()

    def cache_part(group):
        at = pl.ds(4 * group, 4)
        return pltpu.make_async_copy(cache_hbm.at[:, at], kv.at[:, at], kv_sem.at[group])

    for part in range(3):
        cache_part(part).start()
    pltpu.make_async_copy(in_hbm.at[:, 0], win, wt_sem.at[0]).start()
    pltpu.make_async_copy(down_hbm.at[0], down, wt_sem.at[1]).start()

    def rcopy(src, dst, stage, dest_s, dest_z):
        pltpu.make_async_remote_copy(
            src_ref=src,
            dst_ref=dst,
            send_sem=send_sem.at[stage],
            recv_sem=recv_sem.at[stage],
            device_id=(dest_s, dest_z),
            device_id_type=MESH,
        ).start()

    def to_plane(src, dst, stage):
        def send(k, _):
            rcopy(src, dst, stage, plane_peer(k), z)
            return 0

        lax.fori_loop(0, seq_count - 1, send, 0)

    for at in range(3):
        fetch(at).wait()
    for r in range(12):
        x_tok[4 * r : 4 * r + 4, :] = tokens_ref[r].astype(F32)
    x = x_tok[...]
    inverse = lax.rsqrt(jnp.mean(x * x, axis=-1, keepdims=True) + EPSILON)
    normed = (x * inverse * attn_gain_ref[...]).astype(BF16)
    own_mix = lax.dot_general(normed, w_qkv_ref[...], LAST, preferred_element_type=F32)
    mix[...] = jnp.concatenate([own_mix, jnp.zeros((48, 32), F32)], axis=1).astype(BF16)

    pl.semaphore_wait(barrier, seq_count - 1 + group_count - 1)

    qkv_in[s] = mix[...]

    def send_mix(group, send_to, recv_to, dest):
        rows = pl.ds(pl.multiple_of(16 * group, 16), 16)
        return pltpu.make_async_remote_copy(
            src_ref=mix.at[rows],
            dst_ref=qkv_in.at[s, rows],
            send_sem=send_to,
            recv_sem=recv_to,
            device_id=(dest, z),
            device_id_type=MESH,
        )

    has_query = s < QUERY_BLOCKS
    first_tile = (96 * s) // 128
    last_tile = (96 * s + 95) // 128

    @pl.when(has_query)
    def _():
        def send(k, _):
            group = k // (seq_count - 1)
            peer = plane_peer(k - group * (seq_count - 1))
            send_mix(group, query_send.at[0], query_recv.at[group], peer).start()
            return 0

        lax.fori_loop(0, 3 * (seq_count - 1), send, 0)

    def each_owner(act):
        for group in range(3):
            for at, tile in enumerate((first_tile, last_tile)):
                dest = holder(lax.rem(tile, 8), group)
                go = jnp.logical_not(has_query) & (dest != s)
                if at == 1:
                    go = go & (first_tile != last_tile)
                place = 2 * (tile // 16) + s - (128 * tile) // 96

                @pl.when(go)
                def _():
                    act(
                        send_mix(
                            group, mix_send.at[2 * group + at], mix_recv.at[place], dest
                        )
                    )

    each_owner(lambda copy: copy.start())
    fetch(3).wait()

    w_at = 2 * lax.rem(rg, 2) + core

    @pl.when(own_rows)
    def _():
        w_rows[w_at] = w_out_ref[...]

    for row in range(4):
        w_dest = 8 * col + 2 * row + rg // 2

        @pl.when(w_dest != s)
        def _():
            rcopy(w_out_ref, w_rows.at[w_at], 1, w_dest, z)

    for at in range(4, 10):
        fetch(at).wait()
    eye = iota((48, 48), 0) == iota((48, 48), 1)
    prio_row = order_ref[...]
    prio_col = jnp.sum(jnp.where(eye, prio_row, 0), axis=1, keepdims=True)
    earlier = (prio_row < prio_col).astype(F32).astype(BF16)
    expert_lane = iota((48, EXPERTS), 1)
    id_row_of = iota((48, 12), 0)
    id_lane = iota((48, 12), 1)
    id_cols = []
    onehots = []
    for c in range(2):
        spread_ids = jnp.zeros((48, 12), jnp.int32)
        for step in range(STEPS):
            wanted = (id_row_of // STEPS == id_lane) & (id_row_of % STEPS == step)
            spread_ids = spread_ids + jnp.where(wanted, ids_ref[step, c : c + 1, :], 0)
        id_cols.append(jnp.sum(spread_ids, axis=1, keepdims=True))
        onehots.append((expert_lane == id_cols[c]).astype(F32))
    counts = jnp.dot(earlier, (onehots[0] + onehots[1]).astype(BF16), preferred_element_type=F32)
    sel_rows = iota((128, 48), 0)
    sel_expert = 2 * ((sel_rows // CAP) % 8) + sel_rows // 64
    sel_slot = sel_rows % CAP
    col_ids = iota((48, 64), 1)
    col_expert = 2 * (col_ids // CAP) + half
    col_slot = col_ids % CAP
    dispatch = jnp.zeros((128, 48), F32)
    picks = []
    for c in range(2):
        pos_col = jnp.sum(onehots[c] * counts, axis=1, keepdims=True).astype(jnp.int32)
        id_col = id_cols[c]
        pos_row = jnp.sum(jnp.where(eye, pos_col, 0), axis=0, keepdims=True)
        id_row = jnp.sum(jnp.where(eye, id_col, 0), axis=0, keepdims=True)
        dispatch = dispatch + ((id_row == sel_expert) & (pos_row == sel_slot)).astype(F32)
        picks.append(((id_col == col_expert) & (pos_col == col_slot)).astype(F32))
    dispatch = dispatch.astype(BF16)

    for r in range(12):
        for which in range(2):
            sinks[which, 4 * r : 4 * r + 4, :] = sink_ref[which, r].astype(F32)

    def wait_query(group):
        @pl.when(has_query)
        def _():
            wait_bytes(qkv_in.at[pl.ds(0, QUERY_BLOCKS - 1), pl.ds(0, 16)], query_recv.at[group])

        @pl.when(jnp.logical_not(has_query))
        def _():
            wait_bytes(qkv_in.at[pl.ds(0, QUERY_BLOCKS), pl.ds(0, 16)], query_recv.at[group])

    lane16 = iota((16, 128), 1)

    def query_tiles(rows):
        tiles = []
        for first in range(0, QUERY_BLOCKS, 4):
            last = min(first + 3, QUERY_BLOCKS - 1)
            b0, b1, b2, b3 = (
                qkv_in[b, rows, :].astype(F32) for b in (first, first + 1, first + 2, last)
            )
            r1 = pltpu.roll(b1, 96, 1)
            r2 = pltpu.roll(b2, 64, 1)
            r3 = pltpu.roll(b3, 32, 1)
            tiles.append(jnp.where(lane16 < 96, b0, r1))
            tiles.append(jnp.where(lane16 < 64, r1, r2))
            tiles.append(jnp.where(lane16 < 32, r2, r3))
        return tiles[0:8]

    sub2 = iota((2, 8, 128), 1)
    lane2 = iota((2, 8, 128), 2)
    diag2 = (sub2 < 4) == (lane2 < 64)
    zero = jnp.zeros((8, 128), F32)

    def spread_queries(tiles):
        parts = []
        for tile in tiles:
            v = tile.reshape(2, 8, 128)
            w = pltpu.roll(v, 4, 1)
            even = jnp.where(diag2, jnp.where(sub2 < 4, v, w), 0.0)
            odd = jnp.where(diag2, jnp.where(sub2 < 4, w, v), 0.0)
            parts.append((even, odd))
        spread = []
        for pair in range(2):
            for parity in range(2):
                row = []
                for u in range(4):
                    upper = jnp.concatenate([parts[2 * u][parity][pair], zero], axis=1)
                    lower = jnp.concatenate([zero, parts[2 * u + 1][parity][pair]], axis=1)
                    row.append(jnp.concatenate([upper, lower], axis=0).astype(BF16))
                spread.append(row)
        return spread

    sub8 = iota((8, 8, 128), 1)
    lane8 = iota((8, 8, 128), 2)
    lane_in = lane8 % 64
    step_id = iota((8, 128), 0) % STEPS
    slot_id = s * 128 + iota((8, 128), 1)

    def merge(a, b):
        ar = pltpu.roll(a, 4, 1)
        br = pltpu.roll(b, 4, 1)
        return jnp.where(
            sub8 < 4, jnp.where(lane8 < 64, a, ar), jnp.where(lane8 < 64, br, b)
        )

    def attend_rows(group, _):
        cache_part(group).wait()
        wait_query(group)
        queries = spread_queries(query_tiles(pl.ds(pl.multiple_of(16 * group, 16), 16)))
        scores = []
        for k in range(4):
            for u in range(4):
                scores.append(
                    lax.dot_general(
                        queries[k][u],
                        kv[0, 4 * group + k, :, 256 * u : 256 * u + 256],
                        LAST,
                        preferred_element_type=F32,
                    )
                )
        score = jnp.concatenate(scores, axis=0).reshape(4, 8, 8, 128) * (HD ** (-0.5))
        lives = []
        for k in range(4):
            held = lengths_ref[4 * group + k] - SINKS
            age = (slot_id - held) & (WIN - 1)
            lives.append(((slot_id < jnp.minimum(WIN, held)) & (age > step_id)).astype(F32))
        live = jnp.concatenate(lives, axis=0).reshape(4, 1, 8, 128) > 0.0
        peak = jnp.max(jnp.where(live, score, MASKED), axis=-1, keepdims=True)
        weight = jnp.where(live, jnp.exp(score - peak), 0.0)
        total = jnp.sum(weight, axis=-1, keepdims=True)
        rounded = weight.reshape(256, 128).astype(BF16)
        values = []
        for k in range(4):
            found = []
            for u in range(4):
                at = 64 * k + 16 * u
                mixed = jnp.dot(
                    rounded[at : at + 16],
                    kv[1, 4 * group + k, :, 256 * u : 256 * u + 256],
                    preferred_element_type=F32,
                )
                found.append(mixed[0:8, 0:128])
                found.append(mixed[8:16, 128:256])
            values.append(jnp.concatenate(found, axis=0).reshape(8, 8, 128))
        peak = jnp.broadcast_to(peak, (4, 8, 8, 128))
        total = jnp.broadcast_to(total, (4, 8, 8, 128))
        p_hi = peak.astype(BF16).astype(F32)
        p_mid = (peak - p_hi).astype(BF16).astype(F32)
        p_low = peak - p_hi - p_mid
        t_hi = total.astype(BF16).astype(F32)
        t_low = total - t_hi
        lane_at = lane_in[None]
        stat = jnp.where(
            lane_at == 0,
            p_hi,
            jnp.where(
                lane_at == 1,
                p_mid,
                jnp.where(
                    lane_at == 2,
                    p_low,
                    jnp.where(lane_at == 3, t_hi, jnp.where(lane_at == 4, t_low, 0.0)),
                ),
            ),
        )
        part_out[group, :, 0:16, :] = jnp.concatenate(
            [merge(values[0], values[1]), merge(values[2], values[3])], axis=1
        ).astype(BF16)
        part_out[group, :, 16:32, :] = jnp.concatenate(
            [merge(stat[0], stat[1]), merge(stat[2], stat[3])], axis=1
        ).astype(BF16)

        def send(k, _):
            tile = 2 * ring4(k // 2, col) + lax.rem(core + k, 2)
            dest = holder(tile, group)

            @pl.when(dest != s)
            def _():
                rcopy(part_out.at[group, tile], part_in.at[s], 2, dest, z)

            return 0

        lax.fori_loop(0, 8, send, 0)
        return 0

    lax.fori_loop(0, 3, attend_rows, 0)

    @pl.when(owner)
    def _():
        part_in[s] = part_out[rg, t]
        rows = pl.ds(pl.multiple_of(16 * rg, 16), 16)
        lanes = pl.ds(pl.multiple_of(128 * t, 128), 128)

        def own_tile(tile):
            block = (128 * tile) // 96
            offset = 128 * tile - 96 * block
            for k in range(2):

                @pl.when((block + k >= QUERY_BLOCKS) & (block + k != s))
                def _():
                    wait_bytes(mix.at[pl.ds(0, 16)], mix_recv.at[2 * (tile // 16) + k])

            low = pltpu.roll(qkv_in[block, rows, :].astype(F32), 128 - offset, 1)
            high = pltpu.roll(qkv_in[block + 1, rows, :].astype(F32), 96 - offset, 1)
            return jnp.where(lane16 < 96 - offset, low, high)

        q_own = own_tile(t)
        k_own = own_tile(8 + t).astype(BF16)
        v_own = own_tile(16 + t).astype(BF16)
        k_sink = sinks[0, rows, lanes].astype(BF16)
        v_sink = sinks[1, rows, lanes].astype(BF16)
        rep_row = iota((64, 16), 0)
        rep_col = iota((64, 16), 1)
        repeat = (
            ((rep_row % 16) // 4 == rep_col // 4) & (rep_row // 16 == rep_col % 4)
        ).astype(F32).astype(BF16)
        keys = jnp.concatenate(
            [
                jnp.dot(repeat, k_sink, preferred_element_type=F32),
                jnp.dot(repeat, k_own, preferred_element_type=F32),
            ],
            axis=0,
        ).reshape(8, 16, 128)
        vals = jnp.concatenate(
            [
                jnp.dot(repeat, v_sink, preferred_element_type=F32),
                jnp.dot(repeat, v_own, preferred_element_type=F32),
            ],
            axis=0,
        ).reshape(8, 16, 128)
        prod = (q_own[None] * keys).reshape(128, 128)
        prod_hi = prod.astype(BF16)
        prod_low = (prod - prod_hi.astype(F32)).astype(BF16)
        same_half = (
            (iota((128, 128), 0) < 64) == (iota((128, 128), 1) < 64)
        ).astype(F32).astype(BF16)
        score = (
            jnp.dot(prod_hi, same_half, preferred_element_type=F32)
            + jnp.dot(prod_low, same_half, preferred_element_type=F32)
        ).reshape(8, 16, 128) * (HD ** (-0.5))
        key_id = iota((8, 16, 128), 0)
        row_step = iota((8, 16, 128), 1) % STEPS
        live = (key_id < SINKS) | (key_id - SINKS <= row_step)
        near_peak = jnp.max(jnp.where(live, score, MASKED), axis=0)
        weight = jnp.where(live, jnp.exp(score - near_peak[None]), 0.0)
        near_total = jnp.sum(weight, axis=0)
        near_value = jnp.sum(weight.astype(BF16).astype(F32) * vals, axis=0)

        near[0] = near_peak
        near[1] = near_total
        near[2] = near_value
        wait_bytes(part_in.at[pl.ds(0, seq_count - 1)], recv_sem.at[2])


    @pl.when(owner)
    def _():
        near_peak, near_total, near_value = near[0], near[1], near[2]
        spread_row = iota((128, 256), 0)
        spread_col = iota((128, 256), 1)
        kk = spread_row % 64
        wanted = jnp.where(spread_col < 128, (kk < 3).astype(F32), ((kk == 3) | (kk == 4)).astype(F32))
        spread = jnp.where(
            (spread_row < 64) == (spread_col % 128 < 64), wanted, 0.0
        ).astype(BF16)
        stats = jnp.dot(
            part_in[:, 16:32, :].reshape(seq_count * 16, 128), spread, preferred_element_type=F32
        ).reshape(seq_count, 16, 256)
        peaks = stats[:, :, 0:128]
        totals = stats[:, :, 128:256]
        overall = jnp.maximum(jnp.max(peaks, axis=0), near_peak)
        factor = jnp.exp(peaks - overall[None])
        near_factor = jnp.exp(near_peak - overall)
        total = jnp.sum(factor * totals, axis=0) + near_factor * near_total
        value = (
            jnp.sum(factor * part_in[:, 0:16, :].astype(F32), axis=0) + near_factor * near_value
        )
        att_in[8 * rg + t] = (value / total).astype(BF16)
        to_plane(att_in.at[8 * rg + t], att_in.at[8 * rg + t], 3)
        wait_bytes(att_in.at[pl.ds(0, 23)], recv_sem.at[3])

    @pl.when(jnp.logical_not(owner))
    def _():
        wait_bytes(att_in, recv_sem.at[3])

    @pl.when(own_rows)
    def _():
        wait_bytes(w_rows.at[pl.ds(0, 3)], recv_sem.at[1])

    @pl.when(jnp.logical_not(own_rows))
    def _():
        wait_bytes(w_rows, recv_sem.at[1])

    attended = jnp.concatenate(
        [jnp.concatenate([att_in[8 * g + k] for k in range(8)], axis=1) for g in range(3)], axis=0
    )
    proj_in[t] = lax.dot_general(
        attended, w_rows[...].reshape(128, 1024), LAST, preferred_element_type=F32
    ).astype(BF16)
    own_lanes = pl.ds(pl.multiple_of(128 * t, 128), 128)
    own_tile_rows = (x_tok[:, own_lanes] + proj_in[t].astype(F32)).astype(BF16)
    buffer = jnp.dot(dispatch, own_tile_rows, preferred_element_type=F32)
    disp_out[...] = buffer.reshape(16, 8, 128).astype(BF16)

    def send_rows(k, _):
        dest_z = ring8((k // 2) & 7, z)
        dest_col = ring4(k // 16, col)
        dest_s = 8 * dest_col + 2 * rg + lax.rem(core + 1 + k, 2)
        rcopy(
            disp_out.at[8 * (dest_col // 2) + dest_z], disp_in.at[8 * t + z], 5, dest_s, dest_z
        )
        return 0

    lax.fori_loop(0, 8 * group_count - 1, send_rows, 0)
    disp_in[8 * t + z] = disp_out[8 * half + z]

    def send_proj(k, _):
        tile = 2 * ring4(k // 2, col) + lax.rem(core + 1 + k, 2)
        rcopy(proj_in.at[t], proj_in.at[t], 4, holder(tile, rg), z)
        return 0

    lax.fori_loop(0, 7, send_proj, 0)
    wait_bytes(proj_in.at[pl.ds(0, 7)], recv_sem.at[4])
    projected = jnp.concatenate([proj_in[k] for k in range(8)], axis=1)
    residual = x_tok[...] + projected.astype(F32)
    x_tok[...] = residual
    inverse = lax.rsqrt(jnp.mean(residual * residual, axis=-1, keepdims=True) + EPSILON)
    normed = (residual * inverse * moe_gain_ref[...]).astype(BF16)

    logits = lax.dot_general(normed, router_ref[...], LAST, preferred_element_type=F32)
    gates = jnp.zeros((48, 64), F32)
    for c in range(2):
        logit = jnp.sum(onehots[c] * logits, axis=1, keepdims=True)
        gates = gates + picks[c] * jax.nn.sigmoid(logit)
    gates_hi = gates.astype(BF16)
    gates_low = (gates - gates_hi.astype(F32)).astype(BF16)

    pltpu.make_async_copy(in_hbm.at[:, 0], win, wt_sem.at[0]).wait()
    pltpu.make_async_copy(down_hbm.at[0], down, wt_sem.at[1]).wait()
    wait_bytes(disp_in.at[pl.ds(0, 8 * group_count - 1)], recv_sem.at[5])
    raw = jnp.concatenate(
        [disp_in[8 * k : 8 * k + 8].astype(F32).reshape(64, 128) for k in range(8)], axis=1
    )
    inverse = lax.rsqrt(jnp.mean(raw * raw, axis=-1, keepdims=True) + EPSILON)
    rows_in = (raw * inverse * moe_gain_ref[...]).astype(BF16)
    gate_part = lax.dot_general(rows_in, win[0], LAST, preferred_element_type=F32)
    up_part = lax.dot_general(rows_in, win[1], LAST, preferred_element_type=F32)
    hidden = (jax.nn.gelu(gate_part, approximate=True) * up_part).astype(BF16)
    partial = jnp.dot(hidden, down[...], preferred_element_type=F32)
    left32 = iota((32, 128), 1) < 64
    for k in range(8):
        upper = partial[0:32, 128 * k : 128 * k + 128]
        lower = partial[32:64, 128 * k : 128 * k + 128]
        exp_out[2 * k] = jnp.where(left32, upper, pltpu.roll(lower, 64, 1)).astype(BF16)
        exp_out[2 * k + 1] = jnp.where(left32, pltpu.roll(upper, 64, 1), lower).astype(BF16)

    def send_exp(k, _):
        dest = 8 * lax.rem(col + 1 + k // 8, 2) + 2 * ring4((k // 2) & 3, rg) + lax.rem(core + 1 + k, 2)
        rcopy(exp_out.at[dest], exp_in.at[owner16], 6, 16 * half + dest, z)
        return 0

    lax.fori_loop(0, 15, send_exp, 0)
    exp_in[owner16] = exp_out[owner16]
    wait_bytes(exp_in.at[pl.ds(0, 15)], recv_sem.at[6])
    summed = jnp.sum(exp_in[...].astype(F32), axis=0)
    back_out[...] = summed.reshape(4, 8, 128).astype(BF16)

    def send_back(k, _):
        dest = ring8(k, z)
        rcopy(back_out.at[lax.rem(dest, 4)], back_in.at[z], 7, s, dest)
        return 0

    lax.fori_loop(0, group_count - 1, send_back, 0)
    back_in[z] = back_out[lax.rem(z, 4)]
    wait_bytes(back_in.at[pl.ds(0, group_count - 1)], recv_sem.at[7])
    returned = back_in[...].astype(F32).reshape(64, 128).astype(BF16)
    shared = jnp.dot(gates_hi, returned, preferred_element_type=F32) + jnp.dot(
        gates_low, returned, preferred_element_type=F32
    )
    swapped = pltpu.roll(shared, 64, 1)
    left24 = iota((24, 128), 1) < 64
    fin_in[s] = jnp.where(
        z < 4,
        jnp.where(left24, shared[0:24], swapped[24:48]),
        jnp.where(left24, swapped[0:24], shared[24:48]),
    ).astype(BF16)
    to_plane(fin_in.at[s], fin_in.at[s], 8)
    wait_bytes(fin_in.at[pl.ds(0, seq_count - 1)], recv_sem.at[8])

    for k in range(8):
        lanes = slice(128 * k, 128 * k + 128)
        even = fin_in[2 * k].astype(F32) + fin_in[16 + 2 * k].astype(F32)
        odd = fin_in[2 * k + 1].astype(F32) + fin_in[17 + 2 * k].astype(F32)
        upper = jnp.where(left24, even, pltpu.roll(odd, 64, 1))
        lower = jnp.where(left24, pltpu.roll(even, 64, 1), odd)
        out_ref[0:24, lanes] = (x_tok[0:24, lanes] + upper).astype(BF16)
        out_ref[24:48, lanes] = (x_tok[24:48, lanes] + lower).astype(BF16)

    @pl.when(has_query)
    def _():
        wait_bytes(qkv_in.at[pl.ds(0, seq_count - 1)], query_send.at[0])

    each_owner(lambda copy: copy.wait_send())

    @pl.when(own_rows)
    def _():
        wait_bytes(w_rows.at[pl.ds(0, 3)], send_sem.at[1])

    @pl.when(jnp.logical_not(own_rows))
    def _():
        wait_bytes(w_rows, send_sem.at[1])

    @pl.when(owner)
    def _():
        wait_bytes(part_in.at[pl.ds(0, 23)], send_sem.at[2])
        wait_bytes(part_in.at[pl.ds(0, 31), pl.ds(0, 16)], send_sem.at[3])

    @pl.when(jnp.logical_not(owner))
    def _():
        wait_bytes(part_in.at[pl.ds(0, 24)], send_sem.at[2])

    wait_bytes(proj_in.at[pl.ds(0, 7)], send_sem.at[4])
    wait_bytes(disp_in.at[pl.ds(0, 8 * group_count - 1)], send_sem.at[5])
    wait_bytes(exp_in.at[pl.ds(0, 15)], send_sem.at[6])
    wait_bytes(back_in.at[pl.ds(0, group_count - 1)], send_sem.at[7])
    wait_bytes(fin_in.at[pl.ds(0, seq_count - 1)], send_sem.at[8])


def solution(mesh):
    seq_count = mesh.shape["seq"]
    group_count = mesh.shape["exp"]
    vmem = pl.BlockSpec(memory_space=pltpu.VMEM)
    hbm = pl.BlockSpec(memory_space=pltpu.HBM)

    def body(
        tokens,
        attn_gain,
        w_qkv,
        window_cache,
        sink_cache,
        lengths,
        w_out,
        moe_gain,
        router,
        expert_ids,
        slot_order,
        expert_in,
        expert_down,
    ):
        def pin(value):
            return pltpu.with_memory_space_constraint(value, pltpu.HBM)

        out = pl.pallas_call(
            functools.partial(layer_kernel, seq_count, group_count),
            out_shape=jax.ShapeDtypeStruct((48, 1024), BF16),
            in_specs=[hbm] * 13,
            out_specs=vmem,
            scratch_shapes=[
                pltpu.VMEM((12, 4, 1024), BF16),
                pltpu.VMEM((1, 1024), F32),
                pltpu.VMEM((96, 1024), BF16),
                pltpu.VMEM((2, 12, 4, 1024), BF16),
                pltpu.SMEM((12,), jnp.int32),
                pltpu.VMEM((32, 1024), BF16),
                pltpu.VMEM((1, 1024), F32),
                pltpu.VMEM((16, 1024), BF16),
                pltpu.VMEM((4, 2, 12), jnp.int32),
                pltpu.VMEM((1, 48), jnp.int32),
                pltpu.VMEM((2, 12, 128, 1024), BF16),
                pltpu.VMEM((2, 176, 1024), BF16),
                pltpu.VMEM((176, 1024), BF16),
                pltpu.VMEM((48, 1024), F32),
                pltpu.VMEM((48, 128), BF16),
                pltpu.VMEM((32, 48, 128), BF16),
                pltpu.VMEM((3, 16, 128), F32),
                pltpu.VMEM((3, 8, 32, 128), BF16),
                pltpu.VMEM((32, 32, 128), BF16),
                pltpu.VMEM((2, 48, 1024), F32),
                pltpu.VMEM((24, 16, 128), BF16),
                pltpu.VMEM((4, 32, 1024), BF16),
                pltpu.VMEM((8, 48, 128), BF16),
                pltpu.VMEM((16, 8, 128), BF16),
                pltpu.VMEM((64, 8, 128), BF16),
                pltpu.VMEM((16, 32, 128), BF16),
                pltpu.VMEM((16, 32, 128), BF16),
                pltpu.VMEM((4, 8, 128), BF16),
                pltpu.VMEM((8, 8, 128), BF16),
                pltpu.VMEM((32, 24, 128), BF16),
                pltpu.SemaphoreType.DMA((1,)),
                pltpu.SemaphoreType.DMA((3,)),
                pltpu.SemaphoreType.DMA((6,)),
                pltpu.SemaphoreType.DMA((4,)),
                pltpu.SemaphoreType.DMA((3,)),
                pltpu.SemaphoreType.DMA((2,)),
                pltpu.SemaphoreType.DMA((10,)),
                pltpu.SemaphoreType.DMA((9,)),
                pltpu.SemaphoreType.DMA((9,)),
            ],
            compiler_params=pltpu.CompilerParams(
                collective_id=0, has_side_effects=True, vmem_limit_bytes=48 * 1024 * 1024
            ),
            name="layer",
        )(
            pin(tokens),
            pin(attn_gain.reshape(1, -1)),
            pin(w_qkv),
            pin(window_cache),
            pin(sink_cache),
            pin(lengths),
            pin(w_out),
            pin(moe_gain.reshape(1, -1)),
            pin(router.T),
            pin(expert_ids.transpose(1, 2, 0)),
            pin(slot_order),
            pin(expert_in),
            pin(expert_down),
        )
        return out.reshape(tokens.shape)

    in_specs = (
        P("exp", None, None),
        P(),
        P("seq", None),
        P(None, "exp", "seq", None),
        P(None, "exp", None, None),
        P("exp"),
        P("seq", None),
        P(),
        P(),
        P("exp", None, None),
        P("exp", None),
        P(None, "exp", "seq", None),
        P("exp", "seq", None),
    )
    out_specs = P("exp", None, None)
    return jax.shard_map(body, mesh=mesh, in_specs=in_specs, out_specs=out_specs, check_vma=False)
```
